512 devices in a mesh: tm: 16 (over y, x_lo, core), expert: 32 (over x_hi, z).
Axes of the slice: x: 4 (x_hi: 2, x_lo: 2; x = x_hi * 2 + x_lo), y: 4, z: 16, core: 2. Of those that a mesh axis runs over, the one named last changes fastest.
Arguments:
- latents: bfloat16 [32, 2048, 1024], P('expert', 'tm'), may hold values from -16 to 16
- queries: bfloat16 [32, 2048, 1024], P('expert', 'tm'), may hold values from -6 to 6
- keys: bfloat16 [32, 2048, 1024], P('expert', 'tm'), may hold values from -6 to 6
- values: bfloat16 [32, 2048, 1024], P('expert', 'tm'), may hold values from -8 to 8
- inpaint_mask: int32 [32, 2048], P('expert', 'tm'), may hold values 0 or 1
- key_bias: bfloat16 [16], replicated, may hold values from -3 to 3
- out_weight: bfloat16 [1024, 1024], replicated, may hold values from -0.1875 to 0.1875
- modulation: float32 [32, 2, 1024], P('expert'), may hold values from -3 to 3
- branch_gates: float32 [32, 2, 1024], P('expert'), may hold values from 0.5 to 1.5
- expert_ids: int32 [32, 2048, 2], P('expert', 'tm'), may hold values from 0 to 31, as said below
- gate_values: float32 [32, 2048, 2], P('expert', 'tm'), may hold values from 0.2 to 1
- up_weight: bfloat16 [32, 1024, 1024], P('expert', None, 'tm'), may hold values from -0.1875 to 0.1875
- down_weight: bfloat16 [32, 1024, 1024], P('expert', 'tm'), may hold values from -0.1875 to 0.1875
Outputs:
- layer_out: bfloat16 [32, 2048, 1024], P('expert', 'tm')
The draws below stay inside these ranges and needn't reach their ends.
Inputs may be any that keep to these rules, and one draw needn't show every extreme that they name: `expert_ids`: A token's two ids differ. Within each device's block of 128 positions of one clip, no id is named more than 16 times, and one id is named exactly 16 times; that id is the same for all clips at the same block position.
All inputs are finite; a program needn't handle non-finite values. No bound on the sum of `inpaint_mask` on one device may be relied on, other than what follows from the above.
Results may differ from the reference program's by a relative error of at most 0.01.
Values may be sent and summed in bfloat16 or wider, within the bound.
A program may use at most 128 MiB of HBM per device.

```python
import jax
import jax.numpy as jnp
from jax import lax

D = 1024
HEADS = 16
HEAD_DIM = 64
FF = 1024
TOK_DEV = 128
EXPERTS = 32
CAP = 16
CLIPS = 32
LENGTH = 2048


def attention_pair(key):
    shape = (CLIPS, LENGTH, D)
    query_all = jnp.clip(1.4 * jax.random.normal(jax.random.fold_in(key, 1), shape, jnp.float32), -6.0, 6.0)
    key_all = jnp.clip(1.4 * jax.random.normal(jax.random.fold_in(key, 2), shape, jnp.float32), -6.0, 6.0)
    return (query_all.astype(jnp.bfloat16), key_all.astype(jnp.bfloat16))


def draw_queries(key, part):
    return attention_pair(key)[0]


def draw_keys(key, part):
    return attention_pair(key)[1]


def draw_latents(key, part):
    shape = (CLIPS, LENGTH, D)
    return jnp.clip(jax.random.normal(jax.random.fold_in(key, 24), shape, jnp.float32), -4.0, 4.0).astype(jnp.bfloat16)


def draw_expert_ids(key, part):
    per_clip = LENGTH // TOK_DEV
    total_blocks = CLIPS * per_clip
    label_count = EXPERTS * CAP
    designated = jax.random.randint(jax.random.fold_in(key, 31), (per_clip,), 0, EXPERTS)
    popularity = jax.random.randint(jax.random.fold_in(key, 32), (EXPERTS,), 0, 4)
    labels = jnp.arange(label_count, dtype=jnp.int32) // CAP
    label_order = jnp.arange(label_count, dtype=jnp.int32)

    def one_block(which):
        block_key = jax.random.fold_in(key, 1000 + which)
        chosen_expert = designated[which % per_clip]
        noise = jax.random.randint(jax.random.fold_in(block_key, 1), (label_count,), 0, 4096)
        priority = popularity[labels] * 4096 + noise + jnp.where(labels == chosen_expert, 32768, 0)
        ranking = priority * label_count + label_order
        _, picked = lax.top_k(ranking, 2 * TOK_DEV)
        chosen = labels[picked]
        grouped = chosen[jnp.argsort(chosen, stable=True)]
        pairs = jnp.stack([grouped[:TOK_DEV], grouped[TOK_DEV:]], axis=-1)
        shuffle = jax.random.permutation(jax.random.fold_in(block_key, 2), TOK_DEV)
        pairs = pairs[shuffle]
        flips = jax.random.randint(jax.random.fold_in(block_key, 3), (TOK_DEV,), 0, 2)
        return jnp.where(flips[:, None] == 1, pairs[:, ::-1], pairs)
    blocks = jax.vmap(one_block)(jnp.arange(total_blocks, dtype=jnp.int32))
    return blocks.reshape(CLIPS, LENGTH, 2).astype(jnp.int32)


def set_ends(array, key, least, high):
    longest = array.shape.index(max(array.shape))
    spots = []
    for shift in (0, 1):
        where = [jax.random.randint(jax.random.fold_in(key, axis), (), 0, length) for axis, length in enumerate(array.shape)]
        where[longest] = (where[longest] + shift) % array.shape[longest]
        spots.append(tuple(where))
    return array.at[spots[0]].set(least).at[spots[1]].set(high)


def levels(rng, dims, split, smallest, high):
    gain, own = 1.0, jax.random.fold_in(rng, 6)
    for dim, shards_of in split:
        draws = jnp.exp(jax.random.uniform(jax.random.fold_in(own, dim), (shards_of,), jnp.float32, smallest / len(split), high / len(split)))
        gain = gain * jnp.repeat(draws, dims[dim] // shards_of).reshape([-1 if axis == dim else 1 for axis in range(len(dims))])
    return gain


def centred(own_key, dims, width, reach, split=(), held_as=jnp.bfloat16):
    array = width * jax.random.normal(own_key, dims, jnp.float32)
    if split:
        array = array * levels(own_key, dims, split, -0.22, 0.18)
    return jnp.clip(array, -reach, reach).astype(held_as)


def setup_inputs(seed: int = 0) -> dict:
    streams_of = jax.random.split(jax.random.key(seed), 14)
    return {
        "latents": draw_latents(jax.random.fold_in(streams_of[13], 71), 0),
        "queries": draw_queries(jax.random.fold_in(streams_of[13], 71), 0),
        "keys": draw_keys(jax.random.fold_in(streams_of[13], 71), 0),
        "values": centred(streams_of[3], (CLIPS, LENGTH, D), 2.0, 8.0, ((0, 32), (1, 16))),
        "inpaint_mask": set_ends((jax.random.randint(streams_of[4], (CLIPS, LENGTH), 0, 2) < 1).astype(jnp.int32), jax.random.fold_in(streams_of[4], 1), 0, 1),
        "key_bias": jnp.clip(jax.random.uniform(streams_of[5], (HEADS,), jnp.float32, -3.0, 3.0), -3.0, 3.0).astype(jnp.bfloat16),
        "out_weight": centred(streams_of[6], (D, D), D ** -0.5, 0.1875),
        "modulation": centred(streams_of[7], (CLIPS, 2, D), 0.5, 3.0, ((0, 32),), jnp.float32),
        "branch_gates": jnp.clip(0.5 + 1.0 * jax.random.uniform(streams_of[8], (CLIPS, 2, D), jnp.float32) ** levels(streams_of[8], (CLIPS, 2, D), ((0, 32),), -0.2, 0.2), 0.5, 1.5),
        "expert_ids": draw_expert_ids(jax.random.fold_in(streams_of[13], 71), 0),
        "gate_values": jnp.clip(0.2 + 0.8 * jax.random.uniform(streams_of[10], (CLIPS, LENGTH, 2), jnp.float32) ** levels(streams_of[10], (CLIPS, LENGTH, 2), ((0, 32), (1, 16)), -0.2, 0.2), 0.2, 1.0),
        "up_weight": centred(streams_of[11], (EXPERTS, D, FF), D ** -0.5, 0.1875, ((0, 32), (2, 16))),
        "down_weight": centred(streams_of[12], (EXPERTS, FF, D), FF ** -0.5, 0.1875, ((0, 32), (1, 16))),
    }


eps = 1e-06

def attend_clip(operands):
    query, key_rows, value_rows, offsets = operands
    seq_length = query.shape[0]
    query = query.reshape(seq_length, HEADS, HEAD_DIM).astype(jnp.float32)
    key_rows = key_rows.reshape(seq_length, HEADS, HEAD_DIM).astype(jnp.float32)
    value_rows = value_rows.reshape(seq_length, HEADS, HEAD_DIM).astype(jnp.float32)
    scores = jnp.einsum('qhd,khd->hqk', query, key_rows) * HEAD_DIM ** (-0.5)
    scores = scores + jnp.transpose(offsets.astype(jnp.float32))[:, None, :]
    highest = lax.optimization_barrier(jnp.max(scores, axis=2, keepdims=True))
    unscaled = jnp.exp(scores - highest)
    total = lax.optimization_barrier(jnp.sum(unscaled, axis=2))
    weights = lax.optimization_barrier(unscaled.astype(jnp.bfloat16)).astype(jnp.float32)
    attended = jnp.einsum('hqk,khd->qhd', weights, value_rows) / jnp.transpose(total)[:, :, None]
    return attended.reshape(seq_length, HEADS * HEAD_DIM).astype(jnp.bfloat16)

def layer_norm(mixed, shift_row, scale_row):
    center = lax.optimization_barrier(jnp.mean(mixed, axis=-1, keepdims=True))
    deviation = mixed - center
    variance = lax.optimization_barrier(jnp.mean(deviation * deviation, axis=-1, keepdims=True))
    return deviation * lax.rsqrt(variance + eps) * (1.0 + scale_row) + shift_row

def reference(latents, queries, keys, values, inpaint_mask, key_bias, out_weight, modulation, branch_gates, expert_ids, gate_values, up_weight, down_weight):
    offsets = jnp.where(inpaint_mask[:, :, None] == 1, key_bias[None, None, :], jnp.zeros((), jnp.bfloat16)).astype(jnp.bfloat16)
    attended = lax.map(attend_clip, (queries, keys, values, offsets))
    projected = jnp.dot(attended.reshape(CLIPS * LENGTH, D), out_weight, preferred_element_type=jnp.float32).reshape(CLIPS, LENGTH, D)
    mixed = latents.astype(jnp.float32) + branch_gates[:, 0][:, None, :] * projected
    normed = layer_norm(mixed, modulation[:, 0][:, None, :], modulation[:, 1][:, None, :]).astype(jnp.bfloat16)
    blocks = CLIPS * (LENGTH // TOK_DEV)
    normed_blocks = normed.reshape(blocks, TOK_DEV, D)
    flat_ids = expert_ids.reshape(blocks, 2 * TOK_DEV)
    flat_gates = gate_values.reshape(blocks, 2 * TOK_DEV)
    source_token = jnp.arange(2 * TOK_DEV, dtype=jnp.int32) // 2
    slot_range = jnp.arange(CAP, dtype=jnp.int32)
    block_index = jnp.broadcast_to(jnp.arange(blocks, dtype=jnp.int32)[:, None], (blocks, CAP))

    def one_expert(carried, expert):
        chosen = (flat_ids == expert).astype(jnp.int32)
        ranks = jnp.cumsum(chosen, axis=1) - 1
        slot_hit = chosen[:, :, None] * (ranks[:, :, None] == slot_range[None, None, :]).astype(jnp.int32)
        token_index = lax.optimization_barrier(jnp.sum(slot_hit * source_token[None, :, None], axis=1)).astype(jnp.int32)
        live = lax.optimization_barrier(jnp.sum(slot_hit, axis=1)).astype(jnp.float32)
        slot_gate = lax.optimization_barrier(jnp.sum(slot_hit.astype(jnp.float32) * flat_gates[:, :, None], axis=1))
        rows = jnp.take_along_axis(normed_blocks, token_index[:, :, None], axis=1)
        hidden = jax.nn.gelu(jnp.dot(rows.reshape(blocks * CAP, D), up_weight[expert], preferred_element_type=jnp.float32), approximate=True).astype(jnp.bfloat16)
        produced = jnp.dot(hidden, down_weight[expert], preferred_element_type=jnp.float32).astype(jnp.bfloat16)
        produced = lax.optimization_barrier(produced).astype(jnp.float32).reshape(blocks, CAP, D)
        produced = produced * (slot_gate * live)[:, :, None]
        carried = carried.at[block_index, token_index].add(produced)
        return (carried, None)
    combined, _ = lax.scan(one_expert, jnp.zeros((blocks, TOK_DEV, D), jnp.float32), jnp.arange(EXPERTS, dtype=jnp.int32))
    combined = combined.reshape(CLIPS, LENGTH, D)
    return (mixed + branch_gates[:, 1][:, None, :] * combined).astype(jnp.bfloat16)
```

```python
import jax
import jax.numpy as jnp
from jax import lax
from jax.sharding import PartitionSpec as P

eps = 1e-06
query_block = 512


def head_attention(query_rows, key_rows, value_rows, offset_row):
    outputs = []
    for first in range(0, query_rows.shape[0], query_block):
        block = query_rows[first:first + query_block]
        scores = jnp.dot(block, key_rows.T, preferred_element_type=jnp.float32) + offset_row[None, :]
        highest = jnp.max(scores, axis=1, keepdims=True)
        unscaled = jnp.exp(scores - highest)
        total = jnp.sum(unscaled, axis=1, keepdims=True)
        weighted = jnp.dot(
            unscaled.astype(jnp.bfloat16), value_rows, preferred_element_type=jnp.float32
        )
        outputs.append((weighted / total).astype(jnp.bfloat16))
    return jnp.concatenate(outputs, axis=0)


def layer_norm(mixed, shift_row, scale_row):
    center = jnp.mean(mixed, axis=-1, keepdims=True)
    deviation = mixed - center
    variance = jnp.mean(deviation * deviation, axis=-1, keepdims=True)
    return deviation * lax.rsqrt(variance + eps) * (1.0 + scale_row) + shift_row


def on_device(
    latents,
    queries,
    keys,
    values,
    inpaint_mask,
    key_bias,
    out_weight,
    modulation,
    branch_gates,
    expert_ids,
    gate_values,
    up_weight,
    down_weight,
):
    tok_rows = latents.shape[1]
    model_width = latents.shape[2]
    head_count = key_bias.shape[0]
    head_width = model_width // head_count
    score_scale = head_width ** (-0.5)
    full_up, full_down = (
        lax.all_gather(up_weight, "tm", axis=2, tiled=True),
        lax.all_gather(down_weight, "tm", axis=1, tiled=True),
    )
    scaled_queries = queries[0] * jnp.asarray(score_scale, jnp.bfloat16)
    offsets = jnp.where(
        inpaint_mask[0][:, None] == 1, key_bias[None, :], jnp.zeros((), jnp.bfloat16)
    )
    offset_cols = jnp.zeros((tok_rows, head_count, head_width), jnp.bfloat16).at[:, :, 0].set(offsets)
    packed = jnp.concatenate(
        [
            scaled_queries.reshape(tok_rows, head_count, head_width),
            keys[0].reshape(tok_rows, head_count, head_width),
            values[0].reshape(tok_rows, head_count, head_width),
            offset_cols,
        ],
        axis=2,
    )
    packed = jnp.transpose(packed, (1, 0, 2))
    gathered = lax.all_to_all(packed, "tm", split_axis=0, concat_axis=0, tiled=True)
    clip_rows = gathered.reshape(-1, 4 * head_width)
    head_out = head_attention(
        clip_rows[:, :head_width],
        clip_rows[:, head_width:2 * head_width],
        clip_rows[:, 2 * head_width:3 * head_width],
        clip_rows[:, 3 * head_width].astype(jnp.float32),
    )
    head_out = head_out.reshape(head_count, tok_rows, head_width)
    attended_heads = lax.all_to_all(head_out, "tm", split_axis=0, concat_axis=0, tiled=True)
    projected = jnp.einsum(
        "hid,hdo->io",
        attended_heads,
        out_weight.reshape(head_count, head_width, model_width),
        preferred_element_type=jnp.float32,
    )
    mixed = latents[0].astype(jnp.float32) + branch_gates[0, 0][None, :] * projected
    normed = layer_norm(mixed, modulation[0, 0][None, :], modulation[0, 1][None, :]).astype(
        jnp.bfloat16
    )
    local_experts = up_weight.shape[0]
    source_count = lax.axis_size("expert")
    expert_count = local_experts * source_count
    capacity = 4 * tok_rows // expert_count
    choice_list = expert_ids[0].reshape(2 * tok_rows)
    hits = (choice_list[:, None] == jnp.arange(expert_count, dtype=jnp.int32)[None, :]).astype(
        jnp.int32
    )
    ranks = jnp.sum((jnp.cumsum(hits, axis=0) - 1) * hits, axis=1)
    target = ranks * expert_count + choice_list
    placing = (
        jnp.arange(capacity * expert_count, dtype=jnp.int32)[:, None] == target[None, :]
    ).astype(jnp.bfloat16)
    doubled = jnp.repeat(normed, 2, axis=0)
    slots = jnp.dot(placing, doubled, preferred_element_type=jnp.float32).astype(jnp.bfloat16)
    slots = slots.reshape(capacity, expert_count, model_width)
    arrived = lax.all_to_all(slots, "expert", split_axis=1, concat_axis=1, tiled=True)
    slot_count = arrived.shape[0]
    grouped = arrived.reshape(slot_count, source_count, local_experts, model_width)
    hidden = jax.nn.gelu(
        jnp.einsum("csed,edf->csef", grouped, full_up, preferred_element_type=jnp.float32),
        approximate=True,
    ).astype(jnp.bfloat16)
    produced = jnp.einsum(
        "csef,efd->csed", hidden, full_down, preferred_element_type=jnp.float32
    ).astype(jnp.bfloat16)
    produced = produced.reshape(slot_count, source_count * local_experts, model_width)
    returned = lax.all_to_all(produced, "expert", split_axis=1, concat_axis=1, tiled=True)
    picked = jnp.einsum(
        "sa,sd->ad",
        placing,
        returned.reshape(capacity * expert_count, model_width),
        preferred_element_type=jnp.float32,
    )
    picked = picked.reshape(tok_rows, 2, model_width)
    combined = jnp.sum(gate_values[0][:, :, None] * picked, axis=1)
    layer_out = (mixed + branch_gates[0, 1][None, :] * combined).astype(jnp.bfloat16)
    return layer_out[None]


def solution(mesh):
    placed = (
        P("expert", "tm", None),
        P("expert", "tm", None),
        P("expert", "tm", None),
        P("expert", "tm", None),
        P("expert", "tm"),
        P(),
        P(),
        P("expert", None, None),
        P("expert", None, None),
        P("expert", "tm", None),
        P("expert", "tm", None),
        P("expert", None, "tm"),
        P("expert", "tm", None),
    )
    return jax.shard_map(
        on_device, mesh=mesh, in_specs=placed, out_specs=P("expert", "tm", None), check_vma=False
    )
```

```python
import functools

import jax
import jax.numpy as jnp
from jax import lax
from jax.experimental import pallas as pl
from jax.experimental.pallas import tpu as pltpu
from jax.sharding import PartitionSpec as P

eps = 1e-06
query_block = 512


def head_attention(query_rows, key_rows, value_rows, offset_row):
    outputs = []
    for first in range(0, query_rows.shape[0], query_block):
        block = query_rows[first:first + query_block]
        scores = jnp.dot(block, key_rows.T, preferred_element_type=jnp.float32) + offset_row[None, :]
        highest = jnp.max(scores, axis=1, keepdims=True)
        unscaled = jnp.exp(scores - highest)
        total = jnp.sum(unscaled, axis=1, keepdims=True)
        weighted = jnp.dot(
            unscaled.astype(jnp.bfloat16), value_rows, preferred_element_type=jnp.float32
        )
        outputs.append((weighted / total).astype(jnp.bfloat16))
    return jnp.concatenate(outputs, axis=0)


def exchange_kernel(axis, n, x_ref, y_ref, send_sems, recv_sems, local_sem):
    me = lax.axis_index(axis)
    barrier = pltpu.get_barrier_semaphore()
    for k in range(1, n):
        pl.semaphore_signal(
            barrier, inc=1, device_id={axis: lax.rem(me + k, n)}, device_id_type=pl.DeviceIdType.MESH
        )
    pl.semaphore_wait(barrier, n - 1)
    local = pltpu.make_async_copy(x_ref.at[me], y_ref.at[me], local_sem)
    local.start()
    copies = []
    for k in range(1, n):
        peer = lax.rem(me + k, n)
        copy = pltpu.make_async_remote_copy(
            src_ref=x_ref.at[peer],
            dst_ref=y_ref.at[me],
            send_sem=send_sems.at[k],
            recv_sem=recv_sems.at[k],
            device_id={axis: peer},
            device_id_type=pl.DeviceIdType.MESH,
        )
        copy.start()
        copies.append(copy)
    local.wait()
    for copy in copies:
        copy.wait_send()
    for k in range(1, n):
        source = lax.rem(me + n - k, n)
        pltpu.make_async_remote_copy(
            src_ref=x_ref.at[source],
            dst_ref=y_ref.at[source],
            send_sem=send_sems.at[k],
            recv_sem=recv_sems.at[k],
            device_id={axis: source},
            device_id_type=pl.DeviceIdType.MESH,
        ).wait_recv()


def exchange(x, axis, collective_id):
    n = x.shape[0]
    return pl.pallas_call(
        functools.partial(exchange_kernel, axis, n),
        out_shape=jax.ShapeDtypeStruct(x.shape, x.dtype),
        in_specs=[pl.BlockSpec(memory_space=pl.ANY)],
        out_specs=pl.BlockSpec(memory_space=pl.ANY),
        scratch_shapes=[
            pltpu.SemaphoreType.DMA((n,)),
            pltpu.SemaphoreType.DMA((n,)),
            pltpu.SemaphoreType.DMA,
        ],
        compiler_params=pltpu.CompilerParams(collective_id=collective_id, has_side_effects=True),
    )(x)


def layer_norm(mixed, shift_row, scale_row):
    center = jnp.mean(mixed, axis=-1, keepdims=True)
    deviation = mixed - center
    variance = jnp.mean(deviation * deviation, axis=-1, keepdims=True)
    return deviation * lax.rsqrt(variance + eps) * (1.0 + scale_row) + shift_row


def on_device(
    latents,
    queries,
    keys,
    values,
    inpaint_mask,
    key_bias,
    out_weight,
    modulation,
    branch_gates,
    expert_ids,
    gate_values,
    up_weight,
    down_weight,
):
    tok_rows = latents.shape[1]
    model_width = latents.shape[2]
    head_count = key_bias.shape[0]
    head_width = model_width // head_count
    score_scale = head_width ** (-0.5)
    full_up, full_down = (
        lax.all_gather(up_weight, "tm", axis=2, tiled=True),
        lax.all_gather(down_weight, "tm", axis=1, tiled=True),
    )
    scaled_queries = queries[0] * jnp.asarray(score_scale, jnp.bfloat16)
    offsets = jnp.where(
        inpaint_mask[0][:, None] == 1, key_bias[None, :], jnp.zeros((), jnp.bfloat16)
    )
    offset_cols = jnp.zeros((tok_rows, head_count, head_width), jnp.bfloat16).at[:, :, 0].set(offsets)
    packed = jnp.concatenate(
        [
            scaled_queries.reshape(tok_rows, head_count, head_width),
            keys[0].reshape(tok_rows, head_count, head_width),
            values[0].reshape(tok_rows, head_count, head_width),
            offset_cols,
        ],
        axis=2,
    )
    packed = jnp.transpose(packed, (1, 0, 2))
    gathered = exchange(packed, "tm", 0)
    clip_rows = gathered.reshape(-1, 4 * head_width)
    head_out = head_attention(
        clip_rows[:, :head_width],
        clip_rows[:, head_width:2 * head_width],
        clip_rows[:, 2 * head_width:3 * head_width],
        clip_rows[:, 3 * head_width].astype(jnp.float32),
    )
    head_out = head_out.reshape(head_count, tok_rows, head_width)
    attended_heads = exchange(head_out, "tm", 1)
    projected = jnp.einsum(
        "hid,hdo->io",
        attended_heads,
        out_weight.reshape(head_count, head_width, model_width),
        preferred_element_type=jnp.float32,
    )
    mixed = latents[0].astype(jnp.float32) + branch_gates[0, 0][None, :] * projected
    normed = layer_norm(mixed, modulation[0, 0][None, :], modulation[0, 1][None, :]).astype(
        jnp.bfloat16
    )
    local_experts = up_weight.shape[0]
    source_count = lax.axis_size("expert")
    expert_count = local_experts * source_count
    capacity = 4 * tok_rows // expert_count
    choice_list = expert_ids[0].reshape(2 * tok_rows)
    hits = (choice_list[:, None] == jnp.arange(expert_count, dtype=jnp.int32)[None, :]).astype(
        jnp.int32
    )
    ranks = jnp.sum((jnp.cumsum(hits, axis=0) - 1) * hits, axis=1)
    target = ranks * expert_count + choice_list
    placing = (
        jnp.arange(capacity * expert_count, dtype=jnp.int32)[:, None] == target[None, :]
    ).astype(jnp.bfloat16)
    doubled = jnp.repeat(normed, 2, axis=0)
    slots = jnp.dot(placing, doubled, preferred_element_type=jnp.float32).astype(jnp.bfloat16)
    slots = slots.reshape(capacity, expert_count, model_width)
    arrived = lax.all_to_all(slots, "expert", split_axis=1, concat_axis=1, tiled=True)
    slot_count = arrived.shape[0]
    grouped = arrived.reshape(slot_count, source_count, local_experts, model_width)
    hidden = jax.nn.gelu(
        jnp.einsum("csed,edf->csef", grouped, full_up, preferred_element_type=jnp.float32),
        approximate=True,
    ).astype(jnp.bfloat16)
    produced = jnp.einsum(
        "csef,efd->csed", hidden, full_down, preferred_element_type=jnp.float32
    ).astype(jnp.bfloat16)
    produced = produced.reshape(slot_count, source_count * local_experts, model_width)
    returned = lax.all_to_all(produced, "expert", split_axis=1, concat_axis=1, tiled=True)
    picked = jnp.einsum(
        "sa,sd->ad",
        placing,
        returned.reshape(capacity * expert_count, model_width),
        preferred_element_type=jnp.float32,
    )
    picked = picked.reshape(tok_rows, 2, model_width)
    combined = jnp.sum(gate_values[0][:, :, None] * picked, axis=1)
    layer_out = (mixed + branch_gates[0, 1][None, :] * combined).astype(jnp.bfloat16)
    return layer_out[None]


def solution(mesh):
    placed = (
        P("expert", "tm", None),
        P("expert", "tm", None),
        P("expert", "tm", None),
        P("expert", "tm", None),
        P("expert", "tm"),
        P(),
        P(),
        P("expert", None, None),
        P("expert", None, None),
        P("expert", "tm", None),
        P("expert", "tm", None),
        P("expert", None, "tm"),
        P("expert", "tm", None),
    )
    return jax.shard_map(
        on_device, mesh=mesh, in_specs=placed, out_specs=P("expert", "tm", None), check_vma=False
    )
```

```python
import jax
import jax.numpy as jnp
from jax import lax
from jax.sharding import PartitionSpec as P

eps = 1e-06
query_block = 512


def head_attention(query_rows, key_rows, value_rows, offset_row):
    outputs = []
    for first in range(0, query_rows.shape[0], query_block):
        block = query_rows[first:first + query_block]
        scores = jnp.dot(block, key_rows.T, preferred_element_type=jnp.float32) + offset_row[None, :]
        highest = jnp.max(scores, axis=1, keepdims=True)
        unscaled = jnp.exp(scores - highest)
        total = jnp.sum(unscaled, axis=1, keepdims=True)
        weighted = jnp.dot(
            unscaled.astype(jnp.bfloat16), value_rows, preferred_element_type=jnp.float32
        )
        outputs.append((weighted / total).astype(jnp.bfloat16))
    return jnp.concatenate(outputs, axis=0)


def layer_norm(mixed, shift_row, scale_row):
    center = jnp.mean(mixed, axis=-1, keepdims=True)
    deviation = mixed - center
    variance = jnp.mean(deviation * deviation, axis=-1, keepdims=True)
    return deviation * lax.rsqrt(variance + eps) * (1.0 + scale_row) + shift_row


def on_device(
    latents,
    queries,
    keys,
    values,
    inpaint_mask,
    key_bias,
    out_weight,
    modulation,
    branch_gates,
    expert_ids,
    gate_values,
    up_weight,
    down_weight,
):
    tok_rows = latents.shape[1]
    model_width = latents.shape[2]
    head_count = key_bias.shape[0]
    head_width = model_width // head_count
    score_scale = head_width ** (-0.5)
    tm_count = lax.axis_size("tm")
    parity_groups = [list(range(p, tm_count, 2)) for p in range(2)]
    own_slices = jnp.stack([jnp.transpose(up_weight[0]), down_weight[0]])
    parity_slices = lax.all_gather(
        own_slices, "tm", axis=1, tiled=True, axis_index_groups=parity_groups
    )
    sibling_slices = lax.ppermute(
        parity_slices, "tm", [(t, t ^ 1) for t in range(tm_count)]
    )
    both = jnp.concatenate([parity_slices, sibling_slices], axis=1)
    full_up = jnp.transpose(both[0])[None]
    full_down = both[1][None]
    scaled_queries = queries[0] * jnp.asarray(score_scale, jnp.bfloat16)
    offsets = jnp.where(
        inpaint_mask[0][:, None] == 1, key_bias[None, :], jnp.zeros((), jnp.bfloat16)
    )
    offset_cols = jnp.zeros((tok_rows, head_count, head_width), jnp.bfloat16).at[:, :, 0].set(offsets)
    packed = jnp.concatenate(
        [
            scaled_queries.reshape(tok_rows, head_count, head_width),
            keys[0].reshape(tok_rows, head_count, head_width),
            values[0].reshape(tok_rows, head_count, head_width),
            offset_cols,
        ],
        axis=2,
    )
    packed = jnp.transpose(packed, (1, 0, 2))
    gathered = lax.all_to_all(packed, "tm", split_axis=0, concat_axis=0, tiled=True)
    clip_rows = gathered.reshape(-1, 4 * head_width)
    head_out = head_attention(
        clip_rows[:, :head_width],
        clip_rows[:, head_width:2 * head_width],
        clip_rows[:, 2 * head_width:3 * head_width],
        clip_rows[:, 3 * head_width].astype(jnp.float32),
    )
    head_out = head_out.reshape(head_count, tok_rows, head_width)
    attended_heads = lax.all_to_all(head_out, "tm", split_axis=0, concat_axis=0, tiled=True)
    projected = jnp.einsum(
        "hid,hdo->io",
        attended_heads,
        out_weight.reshape(head_count, head_width, model_width),
        preferred_element_type=jnp.float32,
    )
    mixed = latents[0].astype(jnp.float32) + branch_gates[0, 0][None, :] * projected
    normed = layer_norm(mixed, modulation[0, 0][None, :], modulation[0, 1][None, :]).astype(
        jnp.bfloat16
    )
    local_experts = up_weight.shape[0]
    source_count = lax.axis_size("expert")
    expert_count = local_experts * source_count
    capacity = 4 * tok_rows // expert_count
    choice_list = expert_ids[0].reshape(2 * tok_rows)
    hits = (choice_list[:, None] == jnp.arange(expert_count, dtype=jnp.int32)[None, :]).astype(
        jnp.int32
    )
    ranks = jnp.sum((jnp.cumsum(hits, axis=0) - 1) * hits, axis=1)
    target = ranks * expert_count + choice_list
    placing = (
        jnp.arange(capacity * expert_count, dtype=jnp.int32)[:, None] == target[None, :]
    ).astype(jnp.bfloat16)
    doubled = jnp.repeat(normed, 2, axis=0)
    slots = jnp.dot(placing, doubled, preferred_element_type=jnp.float32).astype(jnp.bfloat16)
    slots = slots.reshape(capacity, expert_count, model_width)
    arrived = lax.all_to_all(slots, "expert", split_axis=1, concat_axis=1, tiled=True)
    slot_count = arrived.shape[0]
    grouped = arrived.reshape(slot_count, source_count, local_experts, model_width)
    hidden = jax.nn.gelu(
        jnp.einsum("csed,edf->csef", grouped, full_up, preferred_element_type=jnp.float32),
        approximate=True,
    ).astype(jnp.bfloat16)
    produced = jnp.einsum(
        "csef,efd->csed", hidden, full_down, preferred_element_type=jnp.float32
    ).astype(jnp.bfloat16)
    produced = produced.reshape(slot_count, source_count * local_experts, model_width)
    returned = lax.all_to_all(produced, "expert", split_axis=1, concat_axis=1, tiled=True)
    picked = jnp.einsum(
        "sa,sd->ad",
        placing,
        returned.reshape(capacity * expert_count, model_width),
        preferred_element_type=jnp.float32,
    )
    picked = picked.reshape(tok_rows, 2, model_width)
    combined = jnp.sum(gate_values[0][:, :, None] * picked, axis=1)
    layer_out = (mixed + branch_gates[0, 1][None, :] * combined).astype(jnp.bfloat16)
    return layer_out[None]


def solution(mesh):
    placed = (
        P("expert", "tm", None),
        P("expert", "tm", None),
        P("expert", "tm", None),
        P("expert", "tm", None),
        P("expert", "tm"),
        P(),
        P(),
        P("expert", None, None),
        P("expert", None, None),
        P("expert", "tm", None),
        P("expert", "tm", None),
        P("expert", None, "tm"),
        P("expert", "tm", None),
    )
    return jax.shard_map(
        on_device, mesh=mesh, in_specs=placed, out_specs=P("expert", "tm", None), check_vma=False
    )
```

```python
import functools

import jax
import jax.numpy as jnp
from jax import lax
from jax.experimental import pallas as pl
from jax.experimental.pallas import tpu as pltpu
from jax.sharding import PartitionSpec as P

eps = 1e-06
query_block = 512


def head_attention(query_rows, key_rows, value_rows, offset_row):
    outputs = []
    for first in range(0, query_rows.shape[0], query_block):
        block = query_rows[first:first + query_block]
        scores = jnp.dot(block, key_rows.T, preferred_element_type=jnp.float32) + offset_row[None, :]
        highest = jnp.max(scores, axis=1, keepdims=True)
        unscaled = jnp.exp(scores - highest)
        total = jnp.sum(unscaled, axis=1, keepdims=True)
        weighted = jnp.dot(
            unscaled.astype(jnp.bfloat16), value_rows, preferred_element_type=jnp.float32
        )
        outputs.append((weighted / total).astype(jnp.bfloat16))
    return jnp.concatenate(outputs, axis=0)


def exchange_kernel(axis, n, x_ref, y_ref, send_sems, recv_sems, local_sem):
    me = lax.axis_index(axis)
    barrier = pltpu.get_barrier_semaphore()
    for k in range(1, n):
        pl.semaphore_signal(
            barrier, inc=1, device_id={axis: lax.rem(me + k, n)}, device_id_type=pl.DeviceIdType.MESH
        )
    pl.semaphore_wait(barrier, n - 1)
    local = pltpu.make_async_copy(x_ref.at[me], y_ref.at[me], local_sem)
    local.start()
    copies = []
    for k in range(1, n):
        peer = lax.rem(me + k, n)
        copy = pltpu.make_async_remote_copy(
            src_ref=x_ref.at[peer],
            dst_ref=y_ref.at[me],
            send_sem=send_sems.at[k],
            recv_sem=recv_sems.at[k],
            device_id={axis: peer},
            device_id_type=pl.DeviceIdType.MESH,
        )
        copy.start()
        copies.append(copy)
    local.wait()
    for copy in copies:
        copy.wait_send()
    for k in range(1, n):
        source = lax.rem(me + n - k, n)
        pltpu.make_async_remote_copy(
            src_ref=x_ref.at[source],
            dst_ref=y_ref.at[source],
            send_sem=send_sems.at[k],
            recv_sem=recv_sems.at[k],
            device_id={axis: source},
            device_id_type=pl.DeviceIdType.MESH,
        ).wait_recv()


def exchange(x, axis, collective_id):
    n = x.shape[0]
    return pl.pallas_call(
        functools.partial(exchange_kernel, axis, n),
        out_shape=jax.ShapeDtypeStruct(x.shape, x.dtype),
        in_specs=[pl.BlockSpec(memory_space=pl.ANY)],
        out_specs=pl.BlockSpec(memory_space=pl.ANY),
        scratch_shapes=[
            pltpu.SemaphoreType.DMA((n,)),
            pltpu.SemaphoreType.DMA((n,)),
            pltpu.SemaphoreType.DMA,
        ],
        compiler_params=pltpu.CompilerParams(collective_id=collective_id, has_side_effects=True),
    )(x)


def layer_norm(mixed, shift_row, scale_row):
    center = jnp.mean(mixed, axis=-1, keepdims=True)
    deviation = mixed - center
    variance = jnp.mean(deviation * deviation, axis=-1, keepdims=True)
    return deviation * lax.rsqrt(variance + eps) * (1.0 + scale_row) + shift_row


def on_device(
    latents,
    queries,
    keys,
    values,
    inpaint_mask,
    key_bias,
    out_weight,
    modulation,
    branch_gates,
    expert_ids,
    gate_values,
    up_weight,
    down_weight,
):
    tok_rows = latents.shape[1]
    model_width = latents.shape[2]
    head_count = key_bias.shape[0]
    head_width = model_width // head_count
    score_scale = head_width ** (-0.5)
    tm_count = lax.axis_size("tm")
    parity_groups = [list(range(p, tm_count, 2)) for p in range(2)]
    own_slices = jnp.stack([jnp.transpose(up_weight[0]), down_weight[0]])
    parity_slices = lax.all_gather(
        own_slices, "tm", axis=1, tiled=True, axis_index_groups=parity_groups
    )
    sibling_slices = lax.ppermute(
        parity_slices, "tm", [(t, t ^ 1) for t in range(tm_count)]
    )
    both = jnp.concatenate([parity_slices, sibling_slices], axis=1)
    full_up = jnp.transpose(both[0])[None]
    full_down = both[1][None]
    scaled_queries = queries[0] * jnp.asarray(score_scale, jnp.bfloat16)
    offsets = jnp.where(
        inpaint_mask[0][:, None] == 1, key_bias[None, :], jnp.zeros((), jnp.bfloat16)
    )
    offset_cols = jnp.zeros((tok_rows, head_count, head_width), jnp.bfloat16).at[:, :, 0].set(offsets)
    packed = jnp.concatenate(
        [
            scaled_queries.reshape(tok_rows, head_count, head_width),
            keys[0].reshape(tok_rows, head_count, head_width),
            values[0].reshape(tok_rows, head_count, head_width),
            offset_cols,
        ],
        axis=2,
    )
    packed = jnp.transpose(packed, (1, 0, 2))
    gathered = lax.all_to_all(packed, "tm", split_axis=0, concat_axis=0, tiled=True)
    clip_rows = gathered.reshape(-1, 4 * head_width)
    head_out = head_attention(
        clip_rows[:, :head_width],
        clip_rows[:, head_width:2 * head_width],
        clip_rows[:, 2 * head_width:3 * head_width],
        clip_rows[:, 3 * head_width].astype(jnp.float32),
    )
    head_out = head_out.reshape(head_count, tok_rows, head_width)
    attended_heads = lax.all_to_all(head_out, "tm", split_axis=0, concat_axis=0, tiled=True)
    projected = jnp.einsum(
        "hid,hdo->io",
        attended_heads,
        out_weight.reshape(head_count, head_width, model_width),
        preferred_element_type=jnp.float32,
    )
    mixed = latents[0].astype(jnp.float32) + branch_gates[0, 0][None, :] * projected
    normed = layer_norm(mixed, modulation[0, 0][None, :], modulation[0, 1][None, :]).astype(
        jnp.bfloat16
    )
    local_experts = up_weight.shape[0]
    source_count = lax.axis_size("expert")
    expert_count = local_experts * source_count
    capacity = 4 * tok_rows // expert_count
    choice_list = expert_ids[0].reshape(2 * tok_rows)
    hits = (choice_list[:, None] == jnp.arange(expert_count, dtype=jnp.int32)[None, :]).astype(
        jnp.int32
    )
    ranks = jnp.sum((jnp.cumsum(hits, axis=0) - 1) * hits, axis=1)
    target = choice_list * capacity + ranks
    placing = (
        jnp.arange(capacity * expert_count, dtype=jnp.int32)[:, None] == target[None, :]
    ).astype(jnp.bfloat16)
    doubled = jnp.repeat(normed, 2, axis=0)
    slots = jnp.dot(placing, doubled, preferred_element_type=jnp.float32).astype(jnp.bfloat16)
    slots = slots.reshape(expert_count, capacity, model_width)
    arrived = exchange(slots, "expert", 2)
    grouped = arrived.reshape(source_count, local_experts, capacity, model_width)
    hidden = jax.nn.gelu(
        jnp.einsum("secd,edf->secf", grouped, full_up, preferred_element_type=jnp.float32),
        approximate=True,
    ).astype(jnp.bfloat16)
    produced = jnp.einsum(
        "secf,efd->secd", hidden, full_down, preferred_element_type=jnp.float32
    ).astype(jnp.bfloat16)
    produced = produced.reshape(source_count * local_experts, capacity, model_width)
    returned = exchange(produced, "expert", 3)
    picked = jnp.einsum(
        "sa,sd->ad",
        placing,
        returned.reshape(expert_count * capacity, model_width),
        preferred_element_type=jnp.float32,
    )
    picked = picked.reshape(tok_rows, 2, model_width)
    combined = jnp.sum(gate_values[0][:, :, None] * picked, axis=1)
    layer_out = (mixed + branch_gates[0, 1][None, :] * combined).astype(jnp.bfloat16)
    return layer_out[None]


def solution(mesh):
    placed = (
        P("expert", "tm", None),
        P("expert", "tm", None),
        P("expert", "tm", None),
        P("expert", "tm", None),
        P("expert", "tm"),
        P(),
        P(),
        P("expert", None, None),
        P("expert", None, None),
        P("expert", "tm", None),
        P("expert", "tm", None),
        P("expert", None, "tm"),
        P("expert", "tm", None),
    )
    return jax.shard_map(
        on_device, mesh=mesh, in_specs=placed, out_specs=P("expert", "tm", None), check_vma=False
    )
```

```python
import functools

import jax
import jax.numpy as jnp
from jax import lax
from jax.experimental import pallas as pl
from jax.experimental.pallas import tpu as pltpu
from jax.sharding import PartitionSpec as P

eps = 1e-06
query_block = 512


def head_attention(query_rows, key_rows, value_rows, offset_row):
    outputs = []
    for first in range(0, query_rows.shape[0], query_block):
        block = query_rows[first:first + query_block]
        scores = jnp.dot(block, key_rows.T, preferred_element_type=jnp.float32) + offset_row[None, :]
        highest = jnp.max(scores, axis=1, keepdims=True)
        unscaled = jnp.exp(scores - highest)
        total = jnp.sum(unscaled, axis=1, keepdims=True)
        weighted = jnp.dot(
            unscaled.astype(jnp.bfloat16), value_rows, preferred_element_type=jnp.float32
        )
        outputs.append((weighted / total).astype(jnp.bfloat16))
    return jnp.concatenate(outputs, axis=0)


def exchange_kernel(axis, n, x_ref, y_ref, send_sems, recv_sems, local_sem):
    me = lax.axis_index(axis)
    barrier = pltpu.get_barrier_semaphore()
    for k in range(1, n):
        pl.semaphore_signal(
            barrier, inc=1, device_id={axis: lax.rem(me + k, n)}, device_id_type=pl.DeviceIdType.MESH
        )
    pl.semaphore_wait(barrier, n - 1)
    local = pltpu.make_async_copy(x_ref.at[me], y_ref.at[me], local_sem)
    local.start()
    copies = []
    for k in range(1, n):
        peer = lax.rem(me + k, n)
        copy = pltpu.make_async_remote_copy(
            src_ref=x_ref.at[peer],
            dst_ref=y_ref.at[me],
            send_sem=send_sems.at[k],
            recv_sem=recv_sems.at[k],
            device_id={axis: peer},
            device_id_type=pl.DeviceIdType.MESH,
        )
        copy.start()
        copies.append(copy)
    local.wait()
    for copy in copies:
        copy.wait_send()
    for k in range(1, n):
        source = lax.rem(me + n - k, n)
        pltpu.make_async_remote_copy(
            src_ref=x_ref.at[source],
            dst_ref=y_ref.at[source],
            send_sem=send_sems.at[k],
            recv_sem=recv_sems.at[k],
            device_id={axis: source},
            device_id_type=pl.DeviceIdType.MESH,
        ).wait_recv()


def exchange(x, axis, collective_id):
    n = x.shape[0]
    return pl.pallas_call(
        functools.partial(exchange_kernel, axis, n),
        out_shape=jax.ShapeDtypeStruct(x.shape, x.dtype),
        in_specs=[pl.BlockSpec(memory_space=pl.ANY)],
        out_specs=pl.BlockSpec(memory_space=pl.ANY),
        scratch_shapes=[
            pltpu.SemaphoreType.DMA((n,)),
            pltpu.SemaphoreType.DMA((n,)),
            pltpu.SemaphoreType.DMA,
        ],
        compiler_params=pltpu.CompilerParams(collective_id=collective_id, has_side_effects=True),
    )(x)


def dispatch_kernel(
    expert_n, tm_n, slots_ref, own_ref, arrived_ref, gathered_ref,
    send_sems, recv_sems, weight_send_sems, weight_recv_sems, local_sems,
):
    mesh_ids = pl.DeviceIdType.MESH
    me_e = lax.axis_index("expert")
    me_t = lax.axis_index("tm")
    barrier = pltpu.get_barrier_semaphore()
    for k in range(1, expert_n):
        pl.semaphore_signal(barrier, inc=1, device_id={"expert": lax.rem(me_e + k, expert_n)}, device_id_type=mesh_ids)
    for k in range(1, tm_n):
        pl.semaphore_signal(barrier, inc=1, device_id={"tm": lax.rem(me_t + k, tm_n)}, device_id_type=mesh_ids)
    pl.semaphore_wait(barrier, expert_n - 1 + tm_n - 1)
    local_slots = pltpu.make_async_copy(slots_ref.at[me_e], arrived_ref.at[me_e], local_sems.at[0])
    local_weights = pltpu.make_async_copy(own_ref, gathered_ref.at[me_t], local_sems.at[1])
    local_slots.start()
    local_weights.start()
    copies = []
    for k in range(1, max(expert_n, tm_n)):
        if k < tm_n:
            peer = lax.rem(me_t + k, tm_n)
            copy = pltpu.make_async_remote_copy(
                src_ref=own_ref,
                dst_ref=gathered_ref.at[me_t],
                send_sem=weight_send_sems.at[k],
                recv_sem=weight_recv_sems.at[k],
                device_id={"tm": peer},
                device_id_type=mesh_ids,
            )
            copy.start()
            copies.append(copy)
        if k < expert_n:
            peer = lax.rem(me_e + k, expert_n)
            copy = pltpu.make_async_remote_copy(
                src_ref=slots_ref.at[peer],
                dst_ref=arrived_ref.at[me_e],
                send_sem=send_sems.at[k],
                recv_sem=recv_sems.at[k],
                device_id={"expert": peer},
                device_id_type=mesh_ids,
            )
            copy.start()
            copies.append(copy)
    local_slots.wait()
    local_weights.wait()
    for copy in copies:
        copy.wait_send()
    for k in range(1, expert_n):
        source = lax.rem(me_e + expert_n - k, expert_n)
        pltpu.make_async_remote_copy(
            src_ref=slots_ref.at[source],
            dst_ref=arrived_ref.at[source],
            send_sem=send_sems.at[k],
            recv_sem=recv_sems.at[k],
            device_id={"expert": source},
            device_id_type=mesh_ids,
        ).wait_recv()
    for k in range(1, tm_n):
        source = lax.rem(me_t + tm_n - k, tm_n)
        pltpu.make_async_remote_copy(
            src_ref=own_ref,
            dst_ref=gathered_ref.at[source],
            send_sem=weight_send_sems.at[k],
            recv_sem=weight_recv_sems.at[k],
            device_id={"tm": source},
            device_id_type=mesh_ids,
        ).wait_recv()


def dispatch(slots, own_slices, tm_n, collective_id):
    expert_n = slots.shape[0]
    return pl.pallas_call(
        functools.partial(dispatch_kernel, expert_n, tm_n),
        out_shape=(
            jax.ShapeDtypeStruct(slots.shape, slots.dtype),
            jax.ShapeDtypeStruct((tm_n,) + own_slices.shape, own_slices.dtype),
        ),
        in_specs=[pl.BlockSpec(memory_space=pl.ANY)] * 2,
        out_specs=(pl.BlockSpec(memory_space=pl.ANY), pl.BlockSpec(memory_space=pl.ANY)),
        scratch_shapes=[
            pltpu.SemaphoreType.DMA((expert_n,)),
            pltpu.SemaphoreType.DMA((expert_n,)),
            pltpu.SemaphoreType.DMA((tm_n,)),
            pltpu.SemaphoreType.DMA((tm_n,)),
            pltpu.SemaphoreType.DMA((2,)),
        ],
        compiler_params=pltpu.CompilerParams(collective_id=collective_id, has_side_effects=True),
    )(slots, own_slices)


def layer_norm(mixed, shift_row, scale_row):
    center = jnp.mean(mixed, axis=-1, keepdims=True)
    deviation = mixed - center
    variance = jnp.mean(deviation * deviation, axis=-1, keepdims=True)
    return deviation * lax.rsqrt(variance + eps) * (1.0 + scale_row) + shift_row


def on_device(
    latents,
    queries,
    keys,
    values,
    inpaint_mask,
    key_bias,
    out_weight,
    modulation,
    branch_gates,
    expert_ids,
    gate_values,
    up_weight,
    down_weight,
):
    tok_rows = latents.shape[1]
    model_width = latents.shape[2]
    head_count = key_bias.shape[0]
    head_width = model_width // head_count
    score_scale = head_width ** (-0.5)
    scaled_queries = queries[0] * jnp.asarray(score_scale, jnp.bfloat16)
    offsets = jnp.where(
        inpaint_mask[0][:, None] == 1, key_bias[None, :], jnp.zeros((), jnp.bfloat16)
    )
    offset_cols = jnp.zeros((tok_rows, head_count, head_width), jnp.bfloat16).at[:, :, 0].set(offsets)
    packed = jnp.concatenate(
        [
            scaled_queries.reshape(tok_rows, head_count, head_width),
            keys[0].reshape(tok_rows, head_count, head_width),
            values[0].reshape(tok_rows, head_count, head_width),
            offset_cols,
        ],
        axis=2,
    )
    packed = jnp.transpose(packed, (1, 0, 2))
    gathered = lax.all_to_all(packed, "tm", split_axis=0, concat_axis=0, tiled=True)
    clip_rows = gathered.reshape(-1, 4 * head_width)
    head_out = head_attention(
        clip_rows[:, :head_width],
        clip_rows[:, head_width:2 * head_width],
        clip_rows[:, 2 * head_width:3 * head_width],
        clip_rows[:, 3 * head_width].astype(jnp.float32),
    )
    head_out = head_out.reshape(head_count, tok_rows, head_width)
    attended_heads = lax.all_to_all(head_out, "tm", split_axis=0, concat_axis=0, tiled=True)
    projected = jnp.einsum(
        "hid,hdo->io",
        attended_heads,
        out_weight.reshape(head_count, head_width, model_width),
        preferred_element_type=jnp.float32,
    )
    mixed = latents[0].astype(jnp.float32) + branch_gates[0, 0][None, :] * projected
    normed = layer_norm(mixed, modulation[0, 0][None, :], modulation[0, 1][None, :]).astype(
        jnp.bfloat16
    )
    local_experts = up_weight.shape[0]
    source_count = lax.axis_size("expert")
    expert_count = local_experts * source_count
    capacity = 4 * tok_rows // expert_count
    choice_list = expert_ids[0].reshape(2 * tok_rows)
    hits = (choice_list[:, None] == jnp.arange(expert_count, dtype=jnp.int32)[None, :]).astype(
        jnp.int32
    )
    ranks = jnp.sum((jnp.cumsum(hits, axis=0) - 1) * hits, axis=1)
    target = choice_list * capacity + ranks
    placing = (
        jnp.arange(capacity * expert_count, dtype=jnp.int32)[:, None] == target[None, :]
    ).astype(jnp.bfloat16)
    doubled = jnp.repeat(normed, 2, axis=0)
    slots = jnp.dot(placing, doubled, preferred_element_type=jnp.float32).astype(jnp.bfloat16)
    slots = slots.reshape(expert_count, capacity, model_width)
    own_slices = jnp.stack([jnp.transpose(up_weight[0]), down_weight[0]])
    arrived, gathered_slices = dispatch(slots, own_slices, lax.axis_size("tm"), 2)
    up_rows = gathered_slices[:, 0].reshape(-1, model_width)
    down_rows = gathered_slices[:, 1].reshape(-1, model_width)
    grouped = arrived.reshape(source_count * local_experts * capacity, model_width)
    hidden = jax.nn.gelu(
        jnp.einsum("rd,fd->rf", grouped, up_rows, preferred_element_type=jnp.float32),
        approximate=True,
    ).astype(jnp.bfloat16)
    produced = jnp.dot(hidden, down_rows, preferred_element_type=jnp.float32).astype(jnp.bfloat16)
    produced = produced.reshape(source_count * local_experts, capacity, model_width)
    returned = exchange(produced, "expert", 3)
    picked = jnp.einsum(
        "sa,sd->ad",
        placing,
        returned.reshape(expert_count * capacity, model_width),
        preferred_element_type=jnp.float32,
    )
    picked = picked.reshape(tok_rows, 2, model_width)
    combined = jnp.sum(gate_values[0][:, :, None] * picked, axis=1)
    layer_out = (mixed + branch_gates[0, 1][None, :] * combined).astype(jnp.bfloat16)
    return layer_out[None]


def solution(mesh):
    placed = (
        P("expert", "tm", None),
        P("expert", "tm", None),
        P("expert", "tm", None),
        P("expert", "tm", None),
        P("expert", "tm"),
        P(),
        P(),
        P("expert", None, None),
        P("expert", None, None),
        P("expert", "tm", None),
        P("expert", "tm", None),
        P("expert", None, "tm"),
        P("expert", "tm", None),
    )
    return jax.shard_map(
        on_device, mesh=mesh, in_specs=placed, out_specs=P("expert", "tm", None), check_vma=False
    )
```

```python
import functools

import jax
import jax.numpy as jnp
from jax import lax
from jax.experimental import pallas as pl
from jax.experimental.pallas import tpu as pltpu
from jax.sharding import PartitionSpec as P

eps = 1e-06
query_block = 512


def head_attention(query_rows, key_rows, value_rows, offset_row):
    outputs = []
    for first in range(0, query_rows.shape[0], query_block):
        block = query_rows[first:first + query_block]
        scores = jnp.dot(block, key_rows.T, preferred_element_type=jnp.float32) + offset_row[None, :]
        highest = jnp.max(scores, axis=1, keepdims=True)
        unscaled = jnp.exp(scores - highest)
        total = jnp.sum(unscaled, axis=1, keepdims=True)
        weighted = jnp.dot(
            unscaled.astype(jnp.bfloat16), value_rows, preferred_element_type=jnp.float32
        )
        outputs.append((weighted / total).astype(jnp.bfloat16))
    return jnp.concatenate(outputs, axis=0)


def exchange_kernel(axis, n, x_ref, y_ref, send_sems, recv_sems, local_sem):
    me = lax.axis_index(axis)
    barrier = pltpu.get_barrier_semaphore()
    for k in range(1, n):
        pl.semaphore_signal(
            barrier, inc=1, device_id={axis: lax.rem(me + k, n)}, device_id_type=pl.DeviceIdType.MESH
        )
    pl.semaphore_wait(barrier, n - 1)
    local = pltpu.make_async_copy(x_ref.at[me], y_ref.at[me], local_sem)
    local.start()
    copies = []
    for k in range(1, n):
        peer = lax.rem(me + k, n)
        copy = pltpu.make_async_remote_copy(
            src_ref=x_ref.at[peer],
            dst_ref=y_ref.at[me],
            send_sem=send_sems.at[k],
            recv_sem=recv_sems.at[k],
            device_id={axis: peer},
            device_id_type=pl.DeviceIdType.MESH,
        )
        copy.start()
        copies.append(copy)
    local.wait()
    for copy in copies:
        copy.wait_send()
    for k in range(1, n):
        source = lax.rem(me + n - k, n)
        pltpu.make_async_remote_copy(
            src_ref=x_ref.at[source],
            dst_ref=y_ref.at[source],
            send_sem=send_sems.at[k],
            recv_sem=recv_sems.at[k],
            device_id={axis: source},
            device_id_type=pl.DeviceIdType.MESH,
        ).wait_recv()


def exchange(x, axis, collective_id):
    n = x.shape[0]
    return pl.pallas_call(
        functools.partial(exchange_kernel, axis, n),
        out_shape=jax.ShapeDtypeStruct(x.shape, x.dtype),
        in_specs=[pl.BlockSpec(memory_space=pl.ANY)],
        out_specs=pl.BlockSpec(memory_space=pl.ANY),
        scratch_shapes=[
            pltpu.SemaphoreType.DMA((n,)),
            pltpu.SemaphoreType.DMA((n,)),
            pltpu.SemaphoreType.DMA,
        ],
        compiler_params=pltpu.CompilerParams(collective_id=collective_id, has_side_effects=True),
    )(x)


def dispatch_kernel(
    expert_n, tm_n, slots_ref, own_ref, arrived_ref, gathered_ref,
    send_sems, recv_sems, weight_send_sems, weight_recv_sems, local_sems,
):
    mesh_ids = pl.DeviceIdType.MESH
    me_e = lax.axis_index("expert")
    me_t = lax.axis_index("tm")
    barrier = pltpu.get_barrier_semaphore()
    for k in range(1, expert_n):
        pl.semaphore_signal(barrier, inc=1, device_id={"expert": lax.rem(me_e + k, expert_n)}, device_id_type=mesh_ids)
    for k in range(1, tm_n):
        pl.semaphore_signal(barrier, inc=1, device_id={"tm": lax.rem(me_t + k, tm_n)}, device_id_type=mesh_ids)
    pl.semaphore_wait(barrier, expert_n - 1 + tm_n - 1)
    local_slots = pltpu.make_async_copy(slots_ref.at[me_e], arrived_ref.at[me_e], local_sems.at[0])
    local_weights = pltpu.make_async_copy(own_ref, gathered_ref.at[me_t], local_sems.at[1])
    local_slots.start()
    local_weights.start()
    copies = []
    for k in range(1, max(expert_n, tm_n)):
        if k < tm_n:
            peer = lax.rem(me_t + k, tm_n)
            copy = pltpu.make_async_remote_copy(
                src_ref=own_ref,
                dst_ref=gathered_ref.at[me_t],
                send_sem=weight_send_sems.at[k],
                recv_sem=weight_recv_sems.at[k],
                device_id={"tm": peer},
                device_id_type=mesh_ids,
            )
            copy.start()
            copies.append(copy)
        if k < expert_n:
            peer = lax.rem(me_e + k, expert_n)
            copy = pltpu.make_async_remote_copy(
                src_ref=slots_ref.at[peer],
                dst_ref=arrived_ref.at[me_e],
                send_sem=send_sems.at[k],
                recv_sem=recv_sems.at[k],
                device_id={"expert": peer},
                device_id_type=mesh_ids,
            )
            copy.start()
            copies.append(copy)
    local_slots.wait()
    local_weights.wait()
    for copy in copies:
        copy.wait_send()
    for k in range(1, expert_n):
        source = lax.rem(me_e + expert_n - k, expert_n)
        pltpu.make_async_remote_copy(
            src_ref=slots_ref.at[source],
            dst_ref=arrived_ref.at[source],
            send_sem=send_sems.at[k],
            recv_sem=recv_sems.at[k],
            device_id={"expert": source},
            device_id_type=mesh_ids,
        ).wait_recv()
    for k in range(1, tm_n):
        source = lax.rem(me_t + tm_n - k, tm_n)
        pltpu.make_async_remote_copy(
            src_ref=own_ref,
            dst_ref=gathered_ref.at[source],
            send_sem=weight_send_sems.at[k],
            recv_sem=weight_recv_sems.at[k],
            device_id={"tm": source},
            device_id_type=mesh_ids,
        ).wait_recv()


def dispatch(slots, own_slices, tm_n, collective_id):
    expert_n = slots.shape[0]
    return pl.pallas_call(
        functools.partial(dispatch_kernel, expert_n, tm_n),
        out_shape=(
            jax.ShapeDtypeStruct(slots.shape, slots.dtype),
            jax.ShapeDtypeStruct((tm_n,) + own_slices.shape, own_slices.dtype),
        ),
        in_specs=[pl.BlockSpec(memory_space=pl.ANY)] * 2,
        out_specs=(pl.BlockSpec(memory_space=pl.ANY), pl.BlockSpec(memory_space=pl.ANY)),
        scratch_shapes=[
            pltpu.SemaphoreType.DMA((expert_n,)),
            pltpu.SemaphoreType.DMA((expert_n,)),
            pltpu.SemaphoreType.DMA((tm_n,)),
            pltpu.SemaphoreType.DMA((tm_n,)),
            pltpu.SemaphoreType.DMA((2,)),
        ],
        compiler_params=pltpu.CompilerParams(collective_id=collective_id, has_side_effects=True),
    )(slots, own_slices)


def layer_norm(mixed, shift_row, scale_row):
    center = jnp.mean(mixed, axis=-1, keepdims=True)
    deviation = mixed - center
    variance = jnp.mean(deviation * deviation, axis=-1, keepdims=True)
    return deviation * lax.rsqrt(variance + eps) * (1.0 + scale_row) + shift_row


def on_device(
    latents,
    queries,
    keys,
    values,
    inpaint_mask,
    key_bias,
    out_weight,
    modulation,
    branch_gates,
    expert_ids,
    gate_values,
    up_weight,
    down_weight,
):
    tok_rows = latents.shape[1]
    model_width = latents.shape[2]
    head_count = key_bias.shape[0]
    head_width = model_width // head_count
    score_scale = head_width ** (-0.5)
    scaled_queries = queries[0] * jnp.asarray(score_scale, jnp.bfloat16)
    offsets = jnp.where(
        inpaint_mask[0][:, None] == 1, key_bias[None, :], jnp.zeros((), jnp.bfloat16)
    )
    offset_cols = jnp.zeros((tok_rows, head_count, head_width), jnp.bfloat16).at[:, :, 0].set(offsets)
    packed = jnp.concatenate(
        [
            scaled_queries.reshape(tok_rows, head_count, head_width),
            keys[0].reshape(tok_rows, head_count, head_width),
            values[0].reshape(tok_rows, head_count, head_width),
            offset_cols,
        ],
        axis=2,
    )
    packed = jnp.transpose(packed, (1, 0, 2))
    gathered = exchange(packed, "tm", 0)
    clip_rows = gathered.reshape(-1, 4 * head_width)
    head_out = head_attention(
        clip_rows[:, :head_width],
        clip_rows[:, head_width:2 * head_width],
        clip_rows[:, 2 * head_width:3 * head_width],
        clip_rows[:, 3 * head_width].astype(jnp.float32),
    )
    head_out = head_out.reshape(head_count, tok_rows, head_width)
    attended_heads = exchange(head_out, "tm", 1)
    projected = jnp.einsum(
        "hid,hdo->io",
        attended_heads,
        out_weight.reshape(head_count, head_width, model_width),
        preferred_element_type=jnp.float32,
    )
    mixed = latents[0].astype(jnp.float32) + branch_gates[0, 0][None, :] * projected
    normed = layer_norm(mixed, modulation[0, 0][None, :], modulation[0, 1][None, :]).astype(
        jnp.bfloat16
    )
    local_experts = up_weight.shape[0]
    source_count = lax.axis_size("expert")
    expert_count = local_experts * source_count
    capacity = 4 * tok_rows // expert_count
    choice_list = expert_ids[0].reshape(2 * tok_rows)
    hits = (choice_list[:, None] == jnp.arange(expert_count, dtype=jnp.int32)[None, :]).astype(
        jnp.int32
    )
    ranks = jnp.sum((jnp.cumsum(hits, axis=0) - 1) * hits, axis=1)
    target = choice_list * capacity + ranks
    placing = (
        jnp.arange(capacity * expert_count, dtype=jnp.int32)[:, None] == target[None, :]
    ).astype(jnp.bfloat16)
    doubled = jnp.repeat(normed, 2, axis=0)
    slots = jnp.dot(placing, doubled, preferred_element_type=jnp.float32).astype(jnp.bfloat16)
    slots = slots.reshape(expert_count, capacity, model_width)
    own_slices = jnp.stack([jnp.transpose(up_weight[0]), down_weight[0]])
    arrived, gathered_slices = dispatch(slots, own_slices, lax.axis_size("tm"), 2)
    up_rows = gathered_slices[:, 0].reshape(-1, model_width)
    down_rows = gathered_slices[:, 1].reshape(-1, model_width)
    grouped = arrived.reshape(source_count * local_experts * capacity, model_width)
    hidden = jax.nn.gelu(
        jnp.einsum("rd,fd->rf", grouped, up_rows, preferred_element_type=jnp.float32),
        approximate=True,
    ).astype(jnp.bfloat16)
    produced = jnp.dot(hidden, down_rows, preferred_element_type=jnp.float32).astype(jnp.bfloat16)
    produced = produced.reshape(source_count * local_experts, capacity, model_width)
    returned = exchange(produced, "expert", 3)
    picked = jnp.einsum(
        "sa,sd->ad",
        placing,
        returned.reshape(expert_count * capacity, model_width),
        preferred_element_type=jnp.float32,
    )
    picked = picked.reshape(tok_rows, 2, model_width)
    combined = jnp.sum(gate_values[0][:, :, None] * picked, axis=1)
    layer_out = (mixed + branch_gates[0, 1][None, :] * combined).astype(jnp.bfloat16)
    return layer_out[None]


def solution(mesh):
    placed = (
        P("expert", "tm", None),
        P("expert", "tm", None),
        P("expert", "tm", None),
        P("expert", "tm", None),
        P("expert", "tm"),
        P(),
        P(),
        P("expert", None, None),
        P("expert", None, None),
        P("expert", "tm", None),
        P("expert", "tm", None),
        P("expert", None, "tm"),
        P("expert", "tm", None),
    )
    return jax.shard_map(
        on_device, mesh=mesh, in_specs=placed, out_specs=P("expert", "tm", None), check_vma=False
    )
```

```python
import functools

import jax
import jax.numpy as jnp
from jax import lax
from jax.experimental import pallas as pl
from jax.experimental.pallas import tpu as pltpu
from jax.sharding import PartitionSpec as P

eps = 1e-06
query_block = 512


def head_attention(query_rows, key_rows, value_rows, offset_row):
    outputs = []
    for first in range(0, query_rows.shape[0], query_block):
        block = query_rows[first:first + query_block]
        scores = jnp.dot(block, key_rows.T, preferred_element_type=jnp.float32) + offset_row[None, :]
        highest = jnp.max(scores, axis=1, keepdims=True)
        unscaled = jnp.exp(scores - highest)
        total = jnp.sum(unscaled, axis=1, keepdims=True)
        weighted = jnp.dot(
            unscaled.astype(jnp.bfloat16), value_rows, preferred_element_type=jnp.float32
        )
        outputs.append((weighted / total).astype(jnp.bfloat16))
    return jnp.concatenate(outputs, axis=0)


def exchange_kernel(axis, n, x_ref, y_ref, send_sems, recv_sems, local_sem):
    me = lax.axis_index(axis)
    barrier = pltpu.get_barrier_semaphore()
    for k in range(1, n):
        pl.semaphore_signal(
            barrier, inc=1, device_id={axis: lax.rem(me + k, n)}, device_id_type=pl.DeviceIdType.MESH
        )
    pl.semaphore_wait(barrier, n - 1)
    local = pltpu.make_async_copy(x_ref.at[me], y_ref.at[me], local_sem)
    local.start()
    copies = []
    for k in range(1, n):
        peer = lax.rem(me + k, n)
        copy = pltpu.make_async_remote_copy(
            src_ref=x_ref.at[peer],
            dst_ref=y_ref.at[me],
            send_sem=send_sems.at[k],
            recv_sem=recv_sems.at[k],
            device_id={axis: peer},
            device_id_type=pl.DeviceIdType.MESH,
        )
        copy.start()
        copies.append(copy)
    local.wait()
    for copy in copies:
        copy.wait_send()
    for k in range(1, n):
        source = lax.rem(me + n - k, n)
        pltpu.make_async_remote_copy(
            src_ref=x_ref.at[source],
            dst_ref=y_ref.at[source],
            send_sem=send_sems.at[k],
            recv_sem=recv_sems.at[k],
            device_id={axis: source},
            device_id_type=pl.DeviceIdType.MESH,
        ).wait_recv()


def exchange(x, axis, collective_id):
    n = x.shape[0]
    return pl.pallas_call(
        functools.partial(exchange_kernel, axis, n),
        out_shape=jax.ShapeDtypeStruct(x.shape, x.dtype),
        in_specs=[pl.BlockSpec(memory_space=pl.ANY)],
        out_specs=pl.BlockSpec(memory_space=pl.ANY),
        scratch_shapes=[
            pltpu.SemaphoreType.DMA((n,)),
            pltpu.SemaphoreType.DMA((n,)),
            pltpu.SemaphoreType.DMA,
        ],
        compiler_params=pltpu.CompilerParams(collective_id=collective_id, has_side_effects=True),
    )(x)


def dispatch_kernel(
    expert_n, tm_n, slots_ref, own_ref, arrived_ref, gathered_ref,
    send_sems, recv_sems, weight_send_sems, weight_recv_sems, sibling_sems, local_sems,
):
    mesh_ids = pl.DeviceIdType.MESH
    half = tm_n // 2
    me_e = lax.axis_index("expert")
    me_t = lax.axis_index("tm")
    parity = me_t % 2
    rank = me_t // 2
    sibling = me_t + 1 - 2 * parity
    barrier = pltpu.get_barrier_semaphore()
    for k in range(1, expert_n):
        pl.semaphore_signal(barrier, inc=1, device_id={"expert": lax.rem(me_e + k, expert_n)}, device_id_type=mesh_ids)
    for k in range(1, half):
        pl.semaphore_signal(barrier, inc=1, device_id={"tm": 2 * lax.rem(rank + k, half) + parity}, device_id_type=mesh_ids)
    pl.semaphore_signal(barrier, inc=1, device_id={"tm": sibling}, device_id_type=mesh_ids)
    pl.semaphore_wait(barrier, expert_n - 1 + half)
    local_slots = pltpu.make_async_copy(slots_ref.at[me_e], arrived_ref.at[me_e], local_sems.at[0])
    local_weights = pltpu.make_async_copy(own_ref, gathered_ref.at[parity, rank], local_sems.at[1])
    local_weights.start()
    local_slots.start()
    copies = []
    for k in range(1, half):
        copy = pltpu.make_async_remote_copy(
            src_ref=own_ref,
            dst_ref=gathered_ref.at[parity, rank],
            send_sem=weight_send_sems.at[k],
            recv_sem=weight_recv_sems.at[k],
            device_id={"tm": 2 * lax.rem(rank + k, half) + parity},
            device_id_type=mesh_ids,
        )
        copy.start()
        copies.append(copy)
    for k in range(1, expert_n):
        peer = lax.rem(me_e + k, expert_n)
        copy = pltpu.make_async_remote_copy(
            src_ref=slots_ref.at[peer],
            dst_ref=arrived_ref.at[me_e],
            send_sem=send_sems.at[k],
            recv_sem=recv_sems.at[k],
            device_id={"expert": peer},
            device_id_type=mesh_ids,
        )
        copy.start()
        copies.append(copy)
    local_weights.wait()
    for k in range(1, half):
        source = lax.rem(rank + half - k, half)
        pltpu.make_async_remote_copy(
            src_ref=own_ref,
            dst_ref=gathered_ref.at[parity, source],
            send_sem=weight_send_sems.at[k],
            recv_sem=weight_recv_sems.at[k],
            device_id={"tm": 2 * source + parity},
            device_id_type=mesh_ids,
        ).wait_recv()
    forward = pltpu.make_async_remote_copy(
        src_ref=gathered_ref.at[parity],
        dst_ref=gathered_ref.at[parity],
        send_sem=sibling_sems.at[0],
        recv_sem=sibling_sems.at[1],
        device_id={"tm": sibling},
        device_id_type=mesh_ids,
    )
    forward.start()
    local_slots.wait()
    for copy in copies:
        copy.wait_send()
    for k in range(1, expert_n):
        source = lax.rem(me_e + expert_n - k, expert_n)
        pltpu.make_async_remote_copy(
            src_ref=slots_ref.at[source],
            dst_ref=arrived_ref.at[source],
            send_sem=send_sems.at[k],
            recv_sem=recv_sems.at[k],
            device_id={"expert": source},
            device_id_type=mesh_ids,
        ).wait_recv()
    forward.wait_send()
    pltpu.make_async_remote_copy(
        src_ref=gathered_ref.at[1 - parity],
        dst_ref=gathered_ref.at[1 - parity],
        send_sem=sibling_sems.at[0],
        recv_sem=sibling_sems.at[1],
        device_id={"tm": sibling},
        device_id_type=mesh_ids,
    ).wait_recv()


def dispatch(slots, own_slices, tm_n, collective_id):
    expert_n = slots.shape[0]
    return pl.pallas_call(
        functools.partial(dispatch_kernel, expert_n, tm_n),
        out_shape=(
            jax.ShapeDtypeStruct(slots.shape, slots.dtype),
            jax.ShapeDtypeStruct((2, tm_n // 2) + own_slices.shape, own_slices.dtype),
        ),
        in_specs=[pl.BlockSpec(memory_space=pl.ANY)] * 2,
        out_specs=(pl.BlockSpec(memory_space=pl.ANY), pl.BlockSpec(memory_space=pl.ANY)),
        scratch_shapes=[
            pltpu.SemaphoreType.DMA((expert_n,)),
            pltpu.SemaphoreType.DMA((expert_n,)),
            pltpu.SemaphoreType.DMA((tm_n // 2,)),
            pltpu.SemaphoreType.DMA((tm_n // 2,)),
            pltpu.SemaphoreType.DMA((2,)),
            pltpu.SemaphoreType.DMA((2,)),
        ],
        compiler_params=pltpu.CompilerParams(collective_id=collective_id, has_side_effects=True),
    )(slots, own_slices)

def layer_norm(mixed, shift_row, scale_row):
    center = jnp.mean(mixed, axis=-1, keepdims=True)
    deviation = mixed - center
    variance = jnp.mean(deviation * deviation, axis=-1, keepdims=True)
    return deviation * lax.rsqrt(variance + eps) * (1.0 + scale_row) + shift_row


def on_device(
    latents,
    queries,
    keys,
    values,
    inpaint_mask,
    key_bias,
    out_weight,
    modulation,
    branch_gates,
    expert_ids,
    gate_values,
    up_weight,
    down_weight,
):
    tok_rows = latents.shape[1]
    model_width = latents.shape[2]
    head_count = key_bias.shape[0]
    head_width = model_width // head_count
    score_scale = head_width ** (-0.5)
    scaled_queries = queries[0] * jnp.asarray(score_scale, jnp.bfloat16)
    offsets = jnp.where(
        inpaint_mask[0][:, None] == 1, key_bias[None, :], jnp.zeros((), jnp.bfloat16)
    )
    offset_cols = jnp.zeros((tok_rows, head_count, head_width), jnp.bfloat16).at[:, :, 0].set(offsets)
    packed = jnp.concatenate(
        [
            scaled_queries.reshape(tok_rows, head_count, head_width),
            keys[0].reshape(tok_rows, head_count, head_width),
            values[0].reshape(tok_rows, head_count, head_width),
            offset_cols,
        ],
        axis=2,
    )
    packed = jnp.transpose(packed, (1, 0, 2))
    gathered = lax.all_to_all(packed, "tm", split_axis=0, concat_axis=0, tiled=True)
    clip_rows = gathered.reshape(-1, 4 * head_width)
    head_out = head_attention(
        clip_rows[:, :head_width],
        clip_rows[:, head_width:2 * head_width],
        clip_rows[:, 2 * head_width:3 * head_width],
        clip_rows[:, 3 * head_width].astype(jnp.float32),
    )
    head_out = head_out.reshape(head_count, tok_rows, head_width)
    attended_heads = lax.all_to_all(head_out, "tm", split_axis=0, concat_axis=0, tiled=True)
    projected = jnp.einsum(
        "hid,hdo->io",
        attended_heads,
        out_weight.reshape(head_count, head_width, model_width),
        preferred_element_type=jnp.float32,
    )
    mixed = latents[0].astype(jnp.float32) + branch_gates[0, 0][None, :] * projected
    normed = layer_norm(mixed, modulation[0, 0][None, :], modulation[0, 1][None, :]).astype(
        jnp.bfloat16
    )
    local_experts = up_weight.shape[0]
    source_count = lax.axis_size("expert")
    expert_count = local_experts * source_count
    capacity = 4 * tok_rows // expert_count
    choice_list = expert_ids[0].reshape(2 * tok_rows)
    hits = (choice_list[:, None] == jnp.arange(expert_count, dtype=jnp.int32)[None, :]).astype(
        jnp.int32
    )
    ranks = jnp.sum((jnp.cumsum(hits, axis=0) - 1) * hits, axis=1)
    target = choice_list * capacity + ranks
    placing = (
        jnp.arange(capacity * expert_count, dtype=jnp.int32)[:, None] == target[None, :]
    ).astype(jnp.bfloat16)
    doubled = jnp.repeat(normed, 2, axis=0)
    slots = jnp.dot(placing, doubled, preferred_element_type=jnp.float32).astype(jnp.bfloat16)
    slots = slots.reshape(expert_count, capacity, model_width)
    own_slices = jnp.stack([jnp.transpose(up_weight[0]), down_weight[0]])
    arrived, gathered_slices = dispatch(slots, own_slices, lax.axis_size("tm"), 2)
    up_rows = gathered_slices[:, :, 0].reshape(-1, model_width)
    down_rows = gathered_slices[:, :, 1].reshape(-1, model_width)
    grouped = arrived.reshape(source_count * local_experts * capacity, model_width)
    hidden = jax.nn.gelu(
        jnp.einsum("rd,fd->rf", grouped, up_rows, preferred_element_type=jnp.float32),
        approximate=True,
    ).astype(jnp.bfloat16)
    produced = jnp.dot(hidden, down_rows, preferred_element_type=jnp.float32).astype(jnp.bfloat16)
    produced = produced.reshape(source_count * local_experts, capacity, model_width)
    returned = exchange(produced, "expert", 3)
    picked = jnp.einsum(
        "sa,sd->ad",
        placing,
        returned.reshape(expert_count * capacity, model_width),
        preferred_element_type=jnp.float32,
    )
    picked = picked.reshape(tok_rows, 2, model_width)
    combined = jnp.sum(gate_values[0][:, :, None] * picked, axis=1)
    layer_out = (mixed + branch_gates[0, 1][None, :] * combined).astype(jnp.bfloat16)
    return layer_out[None]


def solution(mesh):
    placed = (
        P("expert", "tm", None),
        P("expert", "tm", None),
        P("expert", "tm", None),
        P("expert", "tm", None),
        P("expert", "tm"),
        P(),
        P(),
        P("expert", None, None),
        P("expert", None, None),
        P("expert", "tm", None),
        P("expert", "tm", None),
        P("expert", None, "tm"),
        P("expert", "tm", None),
    )
    return jax.shard_map(
        on_device, mesh=mesh, in_specs=placed, out_specs=P("expert", "tm", None), check_vma=False
    )
```

```python
import functools

import jax
import jax.numpy as jnp
from jax import lax
from jax.experimental import pallas as pl
from jax.experimental.pallas import tpu as pltpu
from jax.sharding import PartitionSpec as P

eps = 1e-06
query_block = 512


def head_attention(query_rows, key_rows, value_rows, offset_row):
    outputs = []
    for first in range(0, query_rows.shape[0], query_block):
        block = query_rows[first:first + query_block]
        scores = jnp.dot(block, key_rows.T, preferred_element_type=jnp.float32) + offset_row[None, :]
        highest = jnp.max(scores, axis=1, keepdims=True)
        unscaled = jnp.exp(scores - highest)
        total = jnp.sum(unscaled, axis=1, keepdims=True)
        weighted = jnp.dot(
            unscaled.astype(jnp.bfloat16), value_rows, preferred_element_type=jnp.float32
        )
        outputs.append((weighted / total).astype(jnp.bfloat16))
    return jnp.concatenate(outputs, axis=0)


def exchange_kernel(axis, n, x_ref, y_ref, send_sems, recv_sems, local_sem):
    me = lax.axis_index(axis)
    barrier = pltpu.get_barrier_semaphore()
    for k in range(1, n):
        pl.semaphore_signal(
            barrier, inc=1, device_id={axis: lax.rem(me + k, n)}, device_id_type=pl.DeviceIdType.MESH
        )
    pl.semaphore_wait(barrier, n - 1)
    local = pltpu.make_async_copy(x_ref.at[me], y_ref.at[me], local_sem)
    local.start()
    copies = []
    for k in range(1, n):
        peer = lax.rem(me + k, n)
        copy = pltpu.make_async_remote_copy(
            src_ref=x_ref.at[peer],
            dst_ref=y_ref.at[me],
            send_sem=send_sems.at[k],
            recv_sem=recv_sems.at[k],
            device_id={axis: peer},
            device_id_type=pl.DeviceIdType.MESH,
        )
        copy.start()
        copies.append(copy)
    local.wait()
    for copy in copies:
        copy.wait_send()
    for k in range(1, n):
        source = lax.rem(me + n - k, n)
        pltpu.make_async_remote_copy(
            src_ref=x_ref.at[source],
            dst_ref=y_ref.at[source],
            send_sem=send_sems.at[k],
            recv_sem=recv_sems.at[k],
            device_id={axis: source},
            device_id_type=pl.DeviceIdType.MESH,
        ).wait_recv()


def exchange(x, axis, collective_id):
    n = x.shape[0]
    return pl.pallas_call(
        functools.partial(exchange_kernel, axis, n),
        out_shape=jax.ShapeDtypeStruct(x.shape, x.dtype),
        in_specs=[pl.BlockSpec(memory_space=pl.ANY)],
        out_specs=pl.BlockSpec(memory_space=pl.ANY),
        scratch_shapes=[
            pltpu.SemaphoreType.DMA((n,)),
            pltpu.SemaphoreType.DMA((n,)),
            pltpu.SemaphoreType.DMA,
        ],
        compiler_params=pltpu.CompilerParams(collective_id=collective_id, has_side_effects=True),
    )(x)


def dispatch_kernel(
    expert_n, tm_n, slots_ref, own_up_ref, own_down_ref, arrived_ref, up_ref, down_ref,
    send_sems, recv_sems, weight_send_sems, weight_recv_sems, sibling_sems, local_sems,
):
    mesh_ids = pl.DeviceIdType.MESH
    half = tm_n // 2
    me_e = lax.axis_index("expert")
    me_t = lax.axis_index("tm")
    parity = me_t % 2
    rank = me_t // 2
    sibling = me_t + 1 - 2 * parity
    owned = (own_up_ref, own_down_ref)
    gathered = (up_ref, down_ref)
    barrier = pltpu.get_barrier_semaphore()
    for k in range(1, expert_n):
        pl.semaphore_signal(barrier, inc=1, device_id={"expert": lax.rem(me_e + k, expert_n)}, device_id_type=mesh_ids)
    for k in range(1, half):
        pl.semaphore_signal(barrier, inc=1, device_id={"tm": 2 * lax.rem(rank + k, half) + parity}, device_id_type=mesh_ids)
    pl.semaphore_signal(barrier, inc=1, device_id={"tm": sibling}, device_id_type=mesh_ids)
    pl.semaphore_wait(barrier, expert_n - 1 + half)
    local_copies = [pltpu.make_async_copy(slots_ref.at[me_e], arrived_ref.at[me_e], local_sems.at[0])]
    for w in range(2):
        local_copies.append(
            pltpu.make_async_copy(owned[w], gathered[w].at[parity, rank], local_sems.at[1 + w])
        )
    for copy in local_copies:
        copy.start()
    copies = []
    for k in range(1, half):
        for w in range(2):
            copy = pltpu.make_async_remote_copy(
                src_ref=owned[w],
                dst_ref=gathered[w].at[parity, rank],
                send_sem=weight_send_sems.at[w, k],
                recv_sem=weight_recv_sems.at[w, k],
                device_id={"tm": 2 * lax.rem(rank + k, half) + parity},
                device_id_type=mesh_ids,
            )
            copy.start()
            copies.append(copy)
    for k in range(1, expert_n):
        peer = lax.rem(me_e + k, expert_n)
        copy = pltpu.make_async_remote_copy(
            src_ref=slots_ref.at[peer],
            dst_ref=arrived_ref.at[me_e],
            send_sem=send_sems.at[k],
            recv_sem=recv_sems.at[k],
            device_id={"expert": peer},
            device_id_type=mesh_ids,
        )
        copy.start()
        copies.append(copy)
    for copy in local_copies:
        copy.wait()
    forwards = []
    for w in range(2):
        for k in range(1, half):
            source = lax.rem(rank + half - k, half)
            pltpu.make_async_remote_copy(
                src_ref=owned[w],
                dst_ref=gathered[w].at[parity, source],
                send_sem=weight_send_sems.at[w, k],
                recv_sem=weight_recv_sems.at[w, k],
                device_id={"tm": 2 * source + parity},
                device_id_type=mesh_ids,
            ).wait_recv()
        forward = pltpu.make_async_remote_copy(
            src_ref=gathered[w].at[parity],
            dst_ref=gathered[w].at[parity],
            send_sem=sibling_sems.at[0, w],
            recv_sem=sibling_sems.at[1, w],
            device_id={"tm": sibling},
            device_id_type=mesh_ids,
        )
        forward.start()
        forwards.append(forward)
    for copy in copies:
        copy.wait_send()
    for k in range(1, expert_n):
        source = lax.rem(me_e + expert_n - k, expert_n)
        pltpu.make_async_remote_copy(
            src_ref=slots_ref.at[source],
            dst_ref=arrived_ref.at[source],
            send_sem=send_sems.at[k],
            recv_sem=recv_sems.at[k],
            device_id={"expert": source},
            device_id_type=mesh_ids,
        ).wait_recv()
    for w in range(2):
        forwards[w].wait_send()
        pltpu.make_async_remote_copy(
            src_ref=gathered[w].at[1 - parity],
            dst_ref=gathered[w].at[1 - parity],
            send_sem=sibling_sems.at[0, w],
            recv_sem=sibling_sems.at[1, w],
            device_id={"tm": sibling},
            device_id_type=mesh_ids,
        ).wait_recv()


def dispatch(slots, own_up, own_down, tm_n, collective_id):
    expert_n = slots.shape[0]
    gathered_shape = jax.ShapeDtypeStruct((2, tm_n // 2) + own_up.shape, own_up.dtype)
    return pl.pallas_call(
        functools.partial(dispatch_kernel, expert_n, tm_n),
        out_shape=(jax.ShapeDtypeStruct(slots.shape, slots.dtype), gathered_shape, gathered_shape),
        in_specs=[pl.BlockSpec(memory_space=pl.ANY)] * 3,
        out_specs=tuple(pl.BlockSpec(memory_space=pl.ANY) for _ in range(3)),
        scratch_shapes=[
            pltpu.SemaphoreType.DMA((expert_n,)),
            pltpu.SemaphoreType.DMA((expert_n,)),
            pltpu.SemaphoreType.DMA((2, tm_n // 2)),
            pltpu.SemaphoreType.DMA((2, tm_n // 2)),
            pltpu.SemaphoreType.DMA((2, 2)),
            pltpu.SemaphoreType.DMA((3,)),
        ],
        compiler_params=pltpu.CompilerParams(collective_id=collective_id, has_side_effects=True),
    )(slots, own_up, own_down)

def layer_norm(mixed, shift_row, scale_row):
    center = jnp.mean(mixed, axis=-1, keepdims=True)
    deviation = mixed - center
    variance = jnp.mean(deviation * deviation, axis=-1, keepdims=True)
    return deviation * lax.rsqrt(variance + eps) * (1.0 + scale_row) + shift_row


def on_device(
    latents,
    queries,
    keys,
    values,
    inpaint_mask,
    key_bias,
    out_weight,
    modulation,
    branch_gates,
    expert_ids,
    gate_values,
    up_weight,
    down_weight,
):
    tok_rows = latents.shape[1]
    model_width = latents.shape[2]
    head_count = key_bias.shape[0]
    head_width = model_width // head_count
    score_scale = head_width ** (-0.5)
    scaled_queries = queries[0] * jnp.asarray(score_scale, jnp.bfloat16)
    offsets = jnp.where(
        inpaint_mask[0][:, None] == 1, key_bias[None, :], jnp.zeros((), jnp.bfloat16)
    )
    offset_cols = jnp.zeros((tok_rows, head_count, head_width), jnp.bfloat16).at[:, :, 0].set(offsets)
    packed = jnp.concatenate(
        [
            scaled_queries.reshape(tok_rows, head_count, head_width),
            keys[0].reshape(tok_rows, head_count, head_width),
            values[0].reshape(tok_rows, head_count, head_width),
            offset_cols,
        ],
        axis=2,
    )
    packed = jnp.transpose(packed, (1, 0, 2))
    gathered = lax.all_to_all(packed, "tm", split_axis=0, concat_axis=0, tiled=True)
    clip_rows = gathered.reshape(-1, 4 * head_width)
    head_out = head_attention(
        clip_rows[:, :head_width],
        clip_rows[:, head_width:2 * head_width],
        clip_rows[:, 2 * head_width:3 * head_width],
        clip_rows[:, 3 * head_width].astype(jnp.float32),
    )
    head_out = head_out.reshape(head_count, tok_rows, head_width)
    attended_heads = lax.all_to_all(head_out, "tm", split_axis=0, concat_axis=0, tiled=True)
    projected = jnp.einsum(
        "hid,hdo->io",
        attended_heads,
        out_weight.reshape(head_count, head_width, model_width),
        preferred_element_type=jnp.float32,
    )
    mixed = latents[0].astype(jnp.float32) + branch_gates[0, 0][None, :] * projected
    normed = layer_norm(mixed, modulation[0, 0][None, :], modulation[0, 1][None, :]).astype(
        jnp.bfloat16
    )
    local_experts = up_weight.shape[0]
    source_count = lax.axis_size("expert")
    expert_count = local_experts * source_count
    capacity = 4 * tok_rows // expert_count
    choice_list = expert_ids[0].reshape(2 * tok_rows)
    hits = (choice_list[:, None] == jnp.arange(expert_count, dtype=jnp.int32)[None, :]).astype(
        jnp.int32
    )
    ranks = jnp.sum((jnp.cumsum(hits, axis=0) - 1) * hits, axis=1)
    target = choice_list * capacity + ranks
    placing = (
        jnp.arange(capacity * expert_count, dtype=jnp.int32)[:, None] == target[None, :]
    ).astype(jnp.bfloat16)
    doubled = jnp.repeat(normed, 2, axis=0)
    slots = jnp.dot(placing, doubled, preferred_element_type=jnp.float32).astype(jnp.bfloat16)
    slots = slots.reshape(expert_count, capacity, model_width)
    arrived, gathered_up, gathered_down = dispatch(
        slots, jnp.transpose(up_weight[0]), down_weight[0], lax.axis_size("tm"), 2
    )
    up_rows = gathered_up.reshape(-1, model_width)
    down_rows = gathered_down.reshape(-1, model_width)
    grouped = arrived.reshape(source_count * local_experts * capacity, model_width)
    hidden = jax.nn.gelu(
        jnp.einsum("rd,fd->rf", grouped, up_rows, preferred_element_type=jnp.float32),
        approximate=True,
    ).astype(jnp.bfloat16)
    produced = jnp.dot(hidden, down_rows, preferred_element_type=jnp.float32).astype(jnp.bfloat16)
    produced = produced.reshape(source_count * local_experts, capacity, model_width)
    returned = exchange(produced, "expert", 3)
    picked = jnp.einsum(
        "sa,sd->ad",
        placing,
        returned.reshape(expert_count * capacity, model_width),
        preferred_element_type=jnp.float32,
    )
    picked = picked.reshape(tok_rows, 2, model_width)
    combined = jnp.sum(gate_values[0][:, :, None] * picked, axis=1)
    layer_out = (mixed + branch_gates[0, 1][None, :] * combined).astype(jnp.bfloat16)
    return layer_out[None]


def solution(mesh):
    placed = (
        P("expert", "tm", None),
        P("expert", "tm", None),
        P("expert", "tm", None),
        P("expert", "tm", None),
        P("expert", "tm"),
        P(),
        P(),
        P("expert", None, None),
        P("expert", None, None),
        P("expert", "tm", None),
        P("expert", "tm", None),
        P("expert", None, "tm"),
        P("expert", "tm", None),
    )
    return jax.shard_map(
        on_device, mesh=mesh, in_specs=placed, out_specs=P("expert", "tm", None), check_vma=False
    )
```

```python
import functools

import jax
import jax.numpy as jnp
from jax import lax
from jax.experimental import pallas as pl
from jax.experimental.pallas import tpu as pltpu
from jax.sharding import PartitionSpec as P

eps = 1e-06
query_block = 512


def head_attention(query_rows, key_rows, value_rows, offset_row):
    outputs = []
    for first in range(0, query_rows.shape[0], query_block):
        block = query_rows[first:first + query_block]
        scores = jnp.dot(block, key_rows.T, preferred_element_type=jnp.float32) + offset_row[None, :]
        highest = jnp.max(scores, axis=1, keepdims=True)
        unscaled = jnp.exp(scores - highest)
        total = jnp.sum(unscaled, axis=1, keepdims=True)
        weighted = jnp.dot(
            unscaled.astype(jnp.bfloat16), value_rows, preferred_element_type=jnp.float32
        )
        outputs.append((weighted / total).astype(jnp.bfloat16))
    return jnp.concatenate(outputs, axis=0)


def exchange_kernel(axis, n, x_ref, y_ref, send_sems, recv_sems, local_sem):
    me = lax.axis_index(axis)
    barrier = pltpu.get_barrier_semaphore()
    for k in range(1, n):
        pl.semaphore_signal(
            barrier, inc=1, device_id={axis: lax.rem(me + k, n)}, device_id_type=pl.DeviceIdType.MESH
        )
    pl.semaphore_wait(barrier, n - 1)
    local = pltpu.make_async_copy(x_ref.at[me], y_ref.at[me], local_sem)
    local.start()
    copies = []
    for k in range(1, n):
        peer = lax.rem(me + k, n)
        copy = pltpu.make_async_remote_copy(
            src_ref=x_ref.at[peer],
            dst_ref=y_ref.at[me],
            send_sem=send_sems.at[k],
            recv_sem=recv_sems.at[k],
            device_id={axis: peer},
            device_id_type=pl.DeviceIdType.MESH,
        )
        copy.start()
        copies.append(copy)
    local.wait()
    for copy in copies:
        copy.wait_send()
    for k in range(1, n):
        source = lax.rem(me + n - k, n)
        pltpu.make_async_remote_copy(
            src_ref=x_ref.at[source],
            dst_ref=y_ref.at[source],
            send_sem=send_sems.at[k],
            recv_sem=recv_sems.at[k],
            device_id={axis: source},
            device_id_type=pl.DeviceIdType.MESH,
        ).wait_recv()


def exchange(x, axis, collective_id):
    n = x.shape[0]
    return pl.pallas_call(
        functools.partial(exchange_kernel, axis, n),
        out_shape=jax.ShapeDtypeStruct(x.shape, x.dtype),
        in_specs=[pl.BlockSpec(memory_space=pl.ANY)],
        out_specs=pl.BlockSpec(memory_space=pl.ANY),
        scratch_shapes=[
            pltpu.SemaphoreType.DMA((n,)),
            pltpu.SemaphoreType.DMA((n,)),
            pltpu.SemaphoreType.DMA,
        ],
        compiler_params=pltpu.CompilerParams(collective_id=collective_id, has_side_effects=True),
    )(x)


def dispatch_kernel(
    expert_n, tm_n, slots_ref, own_up_ref, own_down_ref, arrived_ref, up_ref, down_ref,
    send_sems, recv_sems, weight_send_sems, weight_recv_sems, sibling_sems, local_sems,
):
    mesh_ids = pl.DeviceIdType.MESH
    half = tm_n // 2
    me_e = lax.axis_index("expert")
    me_t = lax.axis_index("tm")
    parity = me_t % 2
    rank = me_t // 2
    sibling = me_t + 1 - 2 * parity
    owned = (own_up_ref, own_down_ref)
    gathered = (up_ref, down_ref)
    barrier = pltpu.get_barrier_semaphore()
    for k in range(1, expert_n):
        pl.semaphore_signal(barrier, inc=1, device_id={"expert": lax.rem(me_e + k, expert_n)}, device_id_type=mesh_ids)
    for k in range(1, half):
        pl.semaphore_signal(barrier, inc=1, device_id={"tm": 2 * lax.rem(rank + k, half) + parity}, device_id_type=mesh_ids)
    pl.semaphore_signal(barrier, inc=1, device_id={"tm": sibling}, device_id_type=mesh_ids)
    pl.semaphore_wait(barrier, expert_n - 1 + half)
    local_copies = [pltpu.make_async_copy(slots_ref.at[me_e], arrived_ref.at[me_e], local_sems.at[0])]
    for w in range(2):
        local_copies.append(
            pltpu.make_async_copy(owned[w], gathered[w].at[parity, rank], local_sems.at[1 + w])
        )
    for copy in local_copies:
        copy.start()
    copies = []
    for k in range(1, half):
        for w in range(2):
            copy = pltpu.make_async_remote_copy(
                src_ref=owned[w],
                dst_ref=gathered[w].at[parity, rank],
                send_sem=weight_send_sems.at[w, k],
                recv_sem=weight_recv_sems.at[w, k],
                device_id={"tm": 2 * lax.rem(rank + k, half) + parity},
                device_id_type=mesh_ids,
            )
            copy.start()
            copies.append(copy)
    for k in range(1, expert_n):
        peer = lax.rem(me_e + k, expert_n)
        copy = pltpu.make_async_remote_copy(
            src_ref=slots_ref.at[peer],
            dst_ref=arrived_ref.at[me_e],
            send_sem=send_sems.at[k],
            recv_sem=recv_sems.at[k],
            device_id={"expert": peer},
            device_id_type=mesh_ids,
        )
        copy.start()
        copies.append(copy)
    for copy in local_copies:
        copy.wait()
    forwards = []
    for w in range(2):
        for k in range(1, half):
            source = lax.rem(rank + half - k, half)
            pltpu.make_async_remote_copy(
                src_ref=owned[w],
                dst_ref=gathered[w].at[parity, source],
                send_sem=weight_send_sems.at[w, k],
                recv_sem=weight_recv_sems.at[w, k],
                device_id={"tm": 2 * source + parity},
                device_id_type=mesh_ids,
            ).wait_recv()
        forward = pltpu.make_async_remote_copy(
            src_ref=gathered[w].at[parity],
            dst_ref=gathered[w].at[parity],
            send_sem=sibling_sems.at[0, w],
            recv_sem=sibling_sems.at[1, w],
            device_id={"tm": sibling},
            device_id_type=mesh_ids,
        )
        forward.start()
        forwards.append(forward)
    for copy in copies:
        copy.wait_send()
    for k in range(1, expert_n):
        source = lax.rem(me_e + expert_n - k, expert_n)
        pltpu.make_async_remote_copy(
            src_ref=slots_ref.at[source],
            dst_ref=arrived_ref.at[source],
            send_sem=send_sems.at[k],
            recv_sem=recv_sems.at[k],
            device_id={"expert": source},
            device_id_type=mesh_ids,
        ).wait_recv()
    for w in range(2):
        forwards[w].wait_send()
        pltpu.make_async_remote_copy(
            src_ref=gathered[w].at[1 - parity],
            dst_ref=gathered[w].at[1 - parity],
            send_sem=sibling_sems.at[0, w],
            recv_sem=sibling_sems.at[1, w],
            device_id={"tm": sibling},
            device_id_type=mesh_ids,
        ).wait_recv()


def dispatch(slots, own_up, own_down, tm_n, collective_id):
    expert_n = slots.shape[0]
    gathered_shape = jax.ShapeDtypeStruct((2, tm_n // 2) + own_up.shape, own_up.dtype)
    return pl.pallas_call(
        functools.partial(dispatch_kernel, expert_n, tm_n),
        out_shape=(jax.ShapeDtypeStruct(slots.shape, slots.dtype), gathered_shape, gathered_shape),
        in_specs=[pl.BlockSpec(memory_space=pl.ANY)] * 3,
        out_specs=tuple(pl.BlockSpec(memory_space=pl.ANY) for _ in range(3)),
        scratch_shapes=[
            pltpu.SemaphoreType.DMA((expert_n,)),
            pltpu.SemaphoreType.DMA((expert_n,)),
            pltpu.SemaphoreType.DMA((2, tm_n // 2)),
            pltpu.SemaphoreType.DMA((2, tm_n // 2)),
            pltpu.SemaphoreType.DMA((2, 2)),
            pltpu.SemaphoreType.DMA((3,)),
        ],
        compiler_params=pltpu.CompilerParams(collective_id=collective_id, has_side_effects=True),
    )(slots, own_up, own_down)

def layer_norm(mixed, shift_row, scale_row):
    center = jnp.mean(mixed, axis=-1, keepdims=True)
    deviation = mixed - center
    variance = jnp.mean(deviation * deviation, axis=-1, keepdims=True)
    return deviation * lax.rsqrt(variance + eps) * (1.0 + scale_row) + shift_row


def on_device(
    latents,
    queries,
    keys,
    values,
    inpaint_mask,
    key_bias,
    out_weight,
    modulation,
    branch_gates,
    expert_ids,
    gate_values,
    up_weight,
    down_weight,
):
    tok_rows = latents.shape[1]
    model_width = latents.shape[2]
    head_count = key_bias.shape[0]
    head_width = model_width // head_count
    score_scale = head_width ** (-0.5)
    scaled_queries = queries[0] * jnp.asarray(score_scale, jnp.bfloat16)
    offsets = jnp.where(
        inpaint_mask[0][:, None] == 1, key_bias[None, :], jnp.zeros((), jnp.bfloat16)
    )
    offset_cols = jnp.zeros((tok_rows, head_count, 16), jnp.bfloat16).at[:, :, 0].set(offsets)
    packed = jnp.concatenate(
        [
            scaled_queries.reshape(tok_rows, head_count, head_width),
            keys[0].reshape(tok_rows, head_count, head_width),
            values[0].reshape(tok_rows, head_count, head_width),
            offset_cols,
        ],
        axis=2,
    )
    packed = jnp.transpose(packed, (1, 0, 2))
    gathered = lax.all_to_all(packed, "tm", split_axis=0, concat_axis=0, tiled=True)
    clip_rows = gathered.reshape(-1, 3 * head_width + 16)
    head_out = head_attention(
        clip_rows[:, :head_width],
        clip_rows[:, head_width:2 * head_width],
        clip_rows[:, 2 * head_width:3 * head_width],
        clip_rows[:, 3 * head_width].astype(jnp.float32),
    )
    head_out = head_out.reshape(head_count, tok_rows, head_width)
    attended_heads = lax.all_to_all(head_out, "tm", split_axis=0, concat_axis=0, tiled=True)
    projected = jnp.einsum(
        "hid,hdo->io",
        attended_heads,
        out_weight.reshape(head_count, head_width, model_width),
        preferred_element_type=jnp.float32,
    )
    mixed = latents[0].astype(jnp.float32) + branch_gates[0, 0][None, :] * projected
    normed = layer_norm(mixed, modulation[0, 0][None, :], modulation[0, 1][None, :]).astype(
        jnp.bfloat16
    )
    local_experts = up_weight.shape[0]
    source_count = lax.axis_size("expert")
    expert_count = local_experts * source_count
    capacity = 4 * tok_rows // expert_count
    choice_list = expert_ids[0].reshape(2 * tok_rows)
    hits = (choice_list[:, None] == jnp.arange(expert_count, dtype=jnp.int32)[None, :]).astype(
        jnp.int32
    )
    ranks = jnp.sum((jnp.cumsum(hits, axis=0) - 1) * hits, axis=1)
    target = choice_list * capacity + ranks
    placing = (
        jnp.arange(capacity * expert_count, dtype=jnp.int32)[:, None] == target[None, :]
    ).astype(jnp.bfloat16)
    token_placing = placing.reshape(capacity * expert_count, tok_rows, 2).sum(axis=2)
    slots = jnp.dot(token_placing, normed, preferred_element_type=jnp.float32).astype(jnp.bfloat16)
    slots = slots.reshape(expert_count, capacity, model_width)
    arrived, gathered_up, gathered_down = dispatch(
        slots, jnp.transpose(up_weight[0]), down_weight[0], lax.axis_size("tm"), 2
    )
    up_rows = gathered_up.reshape(-1, model_width)
    down_rows = gathered_down.reshape(-1, model_width)
    grouped = arrived.reshape(source_count * local_experts * capacity, model_width)
    hidden = jax.nn.gelu(
        jnp.einsum("rd,fd->rf", grouped, up_rows, preferred_element_type=jnp.float32),
        approximate=True,
    ).astype(jnp.bfloat16)
    produced = jnp.dot(hidden, down_rows, preferred_element_type=jnp.float32).astype(jnp.bfloat16)
    produced = produced.reshape(source_count * local_experts, capacity, model_width)
    returned = exchange(produced, "expert", 3)
    picked = jnp.einsum(
        "sa,sd->ad",
        placing,
        returned.reshape(expert_count * capacity, model_width),
        preferred_element_type=jnp.float32,
    )
    picked = picked.reshape(tok_rows, 2, model_width)
    combined = jnp.sum(gate_values[0][:, :, None] * picked, axis=1)
    layer_out = (mixed + branch_gates[0, 1][None, :] * combined).astype(jnp.bfloat16)
    return layer_out[None]


def solution(mesh):
    placed = (
        P("expert", "tm", None),
        P("expert", "tm", None),
        P("expert", "tm", None),
        P("expert", "tm", None),
        P("expert", "tm"),
        P(),
        P(),
        P("expert", None, None),
        P("expert", None, None),
        P("expert", "tm", None),
        P("expert", "tm", None),
        P("expert", None, "tm"),
        P("expert", "tm", None),
    )
    return jax.shard_map(
        on_device, mesh=mesh, in_specs=placed, out_specs=P("expert", "tm", None), check_vma=False
    )
```

```python
import functools

import jax
import jax.numpy as jnp
from jax import lax
from jax.experimental import pallas as pl
from jax.experimental.pallas import tpu as pltpu
from jax.sharding import PartitionSpec as P

eps = 1e-06
query_block = 512


def head_attention(query_rows, key_rows, value_rows, offset_row):
    outputs = []
    for first in range(0, query_rows.shape[0], query_block):
        block = query_rows[first:first + query_block]
        scores = jnp.dot(block, key_rows.T, preferred_element_type=jnp.float32) + offset_row[None, :]
        highest = jnp.max(scores, axis=1, keepdims=True)
        unscaled = jnp.exp(scores - highest)
        total = jnp.sum(unscaled, axis=1, keepdims=True)
        weighted = jnp.dot(
            unscaled.astype(jnp.bfloat16), value_rows, preferred_element_type=jnp.float32
        )
        outputs.append((weighted / total).astype(jnp.bfloat16))
    return jnp.concatenate(outputs, axis=0)


def both_ways(n):
    order = []
    for k in range(1, n // 2 + 1):
        order += [k] if 2 * k == n else [k, n - k]
    return order


def exchange_kernel(axis, n, x_ref, y_ref, send_sems, recv_sems, local_sem):
    me = lax.axis_index(axis)
    barrier = pltpu.get_barrier_semaphore()
    for k in range(1, n):
        pl.semaphore_signal(
            barrier, inc=1, device_id={axis: lax.rem(me + k, n)}, device_id_type=pl.DeviceIdType.MESH
        )
    pl.semaphore_wait(barrier, n - 1)
    local = pltpu.make_async_copy(x_ref.at[me], y_ref.at[me], local_sem)
    local.start()
    copies = []
    for k in both_ways(n):
        peer = lax.rem(me + k, n)
        copy = pltpu.make_async_remote_copy(
            src_ref=x_ref.at[peer],
            dst_ref=y_ref.at[me],
            send_sem=send_sems.at[k],
            recv_sem=recv_sems.at[k],
            device_id={axis: peer},
            device_id_type=pl.DeviceIdType.MESH,
        )
        copy.start()
        copies.append(copy)
    local.wait()
    for copy in copies:
        copy.wait_send()
    for k in range(1, n):
        source = lax.rem(me + n - k, n)
        pltpu.make_async_remote_copy(
            src_ref=x_ref.at[source],
            dst_ref=y_ref.at[source],
            send_sem=send_sems.at[k],
            recv_sem=recv_sems.at[k],
            device_id={axis: source},
            device_id_type=pl.DeviceIdType.MESH,
        ).wait_recv()


def exchange(x, axis, collective_id):
    n = x.shape[0]
    return pl.pallas_call(
        functools.partial(exchange_kernel, axis, n),
        out_shape=jax.ShapeDtypeStruct(x.shape, x.dtype),
        in_specs=[pl.BlockSpec(memory_space=pl.ANY)],
        out_specs=pl.BlockSpec(memory_space=pl.ANY),
        scratch_shapes=[
            pltpu.SemaphoreType.DMA((n,)),
            pltpu.SemaphoreType.DMA((n,)),
            pltpu.SemaphoreType.DMA,
        ],
        compiler_params=pltpu.CompilerParams(collective_id=collective_id, has_side_effects=True),
    )(x)


def dispatch_kernel(
    expert_n, tm_n, slots_ref, own_up_ref, own_down_ref, arrived_ref, up_ref, down_ref,
    send_sems, recv_sems, weight_send_sems, weight_recv_sems, sibling_sems, local_sems,
):
    mesh_ids = pl.DeviceIdType.MESH
    half = tm_n // 2
    me_e = lax.axis_index("expert")
    me_t = lax.axis_index("tm")
    parity = me_t % 2
    rank = me_t // 2
    sibling = me_t + 1 - 2 * parity
    owned = (own_up_ref, own_down_ref)
    gathered = (up_ref, down_ref)
    barrier = pltpu.get_barrier_semaphore()
    for k in range(1, expert_n):
        pl.semaphore_signal(barrier, inc=1, device_id={"expert": lax.rem(me_e + k, expert_n)}, device_id_type=mesh_ids)
    for k in range(1, half):
        pl.semaphore_signal(barrier, inc=1, device_id={"tm": 2 * lax.rem(rank + k, half) + parity}, device_id_type=mesh_ids)
    pl.semaphore_signal(barrier, inc=1, device_id={"tm": sibling}, device_id_type=mesh_ids)
    pl.semaphore_wait(barrier, expert_n - 1 + half)
    local_copies = [pltpu.make_async_copy(slots_ref.at[me_e], arrived_ref.at[me_e], local_sems.at[0])]
    for w in range(2):
        local_copies.append(
            pltpu.make_async_copy(owned[w], gathered[w].at[parity, rank], local_sems.at[1 + w])
        )
    for copy in local_copies:
        copy.start()
    copies = []
    for k in range(1, half):
        for w in range(2):
            copy = pltpu.make_async_remote_copy(
                src_ref=owned[w],
                dst_ref=gathered[w].at[parity, rank],
                send_sem=weight_send_sems.at[w, k],
                recv_sem=weight_recv_sems.at[w, k],
                device_id={"tm": 2 * lax.rem(rank + k, half) + parity},
                device_id_type=mesh_ids,
            )
            copy.start()
            copies.append(copy)
    for k in both_ways(expert_n):
        peer = lax.rem(me_e + k, expert_n)
        copy = pltpu.make_async_remote_copy(
            src_ref=slots_ref.at[peer],
            dst_ref=arrived_ref.at[me_e],
            send_sem=send_sems.at[k],
            recv_sem=recv_sems.at[k],
            device_id={"expert": peer},
            device_id_type=mesh_ids,
        )
        copy.start()
        copies.append(copy)
    for copy in local_copies:
        copy.wait()
    forwards = []
    for w in range(2):
        for k in range(1, half):
            source = lax.rem(rank + half - k, half)
            pltpu.make_async_remote_copy(
                src_ref=owned[w],
                dst_ref=gathered[w].at[parity, source],
                send_sem=weight_send_sems.at[w, k],
                recv_sem=weight_recv_sems.at[w, k],
                device_id={"tm": 2 * source + parity},
                device_id_type=mesh_ids,
            ).wait_recv()
        forward = pltpu.make_async_remote_copy(
            src_ref=gathered[w].at[parity],
            dst_ref=gathered[w].at[parity],
            send_sem=sibling_sems.at[0, w],
            recv_sem=sibling_sems.at[1, w],
            device_id={"tm": sibling},
            device_id_type=mesh_ids,
        )
        forward.start()
        forwards.append(forward)
    for copy in copies:
        copy.wait_send()
    for k in range(1, expert_n):
        source = lax.rem(me_e + expert_n - k, expert_n)
        pltpu.make_async_remote_copy(
            src_ref=slots_ref.at[source],
            dst_ref=arrived_ref.at[source],
            send_sem=send_sems.at[k],
            recv_sem=recv_sems.at[k],
            device_id={"expert": source},
            device_id_type=mesh_ids,
        ).wait_recv()
    for w in range(2):
        forwards[w].wait_send()
        pltpu.make_async_remote_copy(
            src_ref=gathered[w].at[1 - parity],
            dst_ref=gathered[w].at[1 - parity],
            send_sem=sibling_sems.at[0, w],
            recv_sem=sibling_sems.at[1, w],
            device_id={"tm": sibling},
            device_id_type=mesh_ids,
        ).wait_recv()


def dispatch(slots, own_up, own_down, tm_n, collective_id):
    expert_n = slots.shape[0]
    gathered_shape = jax.ShapeDtypeStruct((2, tm_n // 2) + own_up.shape, own_up.dtype)
    return pl.pallas_call(
        functools.partial(dispatch_kernel, expert_n, tm_n),
        out_shape=(jax.ShapeDtypeStruct(slots.shape, slots.dtype), gathered_shape, gathered_shape),
        in_specs=[pl.BlockSpec(memory_space=pl.ANY)] * 3,
        out_specs=tuple(pl.BlockSpec(memory_space=pl.ANY) for _ in range(3)),
        scratch_shapes=[
            pltpu.SemaphoreType.DMA((expert_n,)),
            pltpu.SemaphoreType.DMA((expert_n,)),
            pltpu.SemaphoreType.DMA((2, tm_n // 2)),
            pltpu.SemaphoreType.DMA((2, tm_n // 2)),
            pltpu.SemaphoreType.DMA((2, 2)),
            pltpu.SemaphoreType.DMA((3,)),
        ],
        compiler_params=pltpu.CompilerParams(collective_id=collective_id, has_side_effects=True),
    )(slots, own_up, own_down)

def layer_norm(mixed, shift_row, scale_row):
    center = jnp.mean(mixed, axis=-1, keepdims=True)
    deviation = mixed - center
    variance = jnp.mean(deviation * deviation, axis=-1, keepdims=True)
    return deviation * lax.rsqrt(variance + eps) * (1.0 + scale_row) + shift_row


def on_device(
    latents,
    queries,
    keys,
    values,
    inpaint_mask,
    key_bias,
    out_weight,
    modulation,
    branch_gates,
    expert_ids,
    gate_values,
    up_weight,
    down_weight,
):
    tok_rows = latents.shape[1]
    model_width = latents.shape[2]
    head_count = key_bias.shape[0]
    head_width = model_width // head_count
    score_scale = head_width ** (-0.5)
    scaled_queries = queries[0] * jnp.asarray(score_scale, jnp.bfloat16)
    offsets = jnp.where(
        inpaint_mask[0][:, None] == 1, key_bias[None, :], jnp.zeros((), jnp.bfloat16)
    )
    offset_cols = jnp.zeros((tok_rows, head_count, 16), jnp.bfloat16).at[:, :, 0].set(offsets)
    packed = jnp.concatenate(
        [
            scaled_queries.reshape(tok_rows, head_count, head_width),
            keys[0].reshape(tok_rows, head_count, head_width),
            values[0].reshape(tok_rows, head_count, head_width),
            offset_cols,
        ],
        axis=2,
    )
    packed = jnp.transpose(packed, (1, 0, 2))
    gathered = lax.all_to_all(packed, "tm", split_axis=0, concat_axis=0, tiled=True)
    clip_rows = gathered.reshape(-1, 3 * head_width + 16)
    head_out = head_attention(
        clip_rows[:, :head_width],
        clip_rows[:, head_width:2 * head_width],
        clip_rows[:, 2 * head_width:3 * head_width],
        clip_rows[:, 3 * head_width].astype(jnp.float32),
    )
    head_out = head_out.reshape(head_count, tok_rows, head_width)
    attended_heads = lax.all_to_all(head_out, "tm", split_axis=0, concat_axis=0, tiled=True)
    projected = jnp.einsum(
        "hid,hdo->io",
        attended_heads,
        out_weight.reshape(head_count, head_width, model_width),
        preferred_element_type=jnp.float32,
    )
    mixed = latents[0].astype(jnp.float32) + branch_gates[0, 0][None, :] * projected
    normed = layer_norm(mixed, modulation[0, 0][None, :], modulation[0, 1][None, :]).astype(
        jnp.bfloat16
    )
    local_experts = up_weight.shape[0]
    source_count = lax.axis_size("expert")
    expert_count = local_experts * source_count
    capacity = 4 * tok_rows // expert_count
    choice_list = expert_ids[0].reshape(2 * tok_rows)
    hits = (choice_list[:, None] == jnp.arange(expert_count, dtype=jnp.int32)[None, :]).astype(
        jnp.int32
    )
    ranks = jnp.sum((jnp.cumsum(hits, axis=0) - 1) * hits, axis=1)
    target = choice_list * capacity + ranks
    placing = (
        jnp.arange(capacity * expert_count, dtype=jnp.int32)[:, None] == target[None, :]
    ).astype(jnp.bfloat16)
    token_placing = placing.reshape(capacity * expert_count, tok_rows, 2).sum(axis=2)
    slots = jnp.dot(token_placing, normed, preferred_element_type=jnp.float32).astype(jnp.bfloat16)
    slots = slots.reshape(expert_count, capacity, model_width)
    arrived, gathered_up, gathered_down = dispatch(
        slots, jnp.transpose(up_weight[0]), down_weight[0], lax.axis_size("tm"), 2
    )
    up_rows = gathered_up.reshape(-1, model_width)
    down_rows = gathered_down.reshape(-1, model_width)
    grouped = arrived.reshape(source_count * local_experts * capacity, model_width)
    hidden = jax.nn.gelu(
        jnp.einsum("rd,fd->rf", grouped, up_rows, preferred_element_type=jnp.float32),
        approximate=True,
    ).astype(jnp.bfloat16)
    produced = jnp.dot(hidden, down_rows, preferred_element_type=jnp.float32).astype(jnp.bfloat16)
    produced = produced.reshape(source_count * local_experts, capacity, model_width)
    returned = exchange(produced, "expert", 3)
    picked = jnp.einsum(
        "sa,sd->ad",
        placing,
        returned.reshape(expert_count * capacity, model_width),
        preferred_element_type=jnp.float32,
    )
    picked = picked.reshape(tok_rows, 2, model_width)
    combined = jnp.sum(gate_values[0][:, :, None] * picked, axis=1)
    layer_out = (mixed + branch_gates[0, 1][None, :] * combined).astype(jnp.bfloat16)
    return layer_out[None]


def solution(mesh):
    placed = (
        P("expert", "tm", None),
        P("expert", "tm", None),
        P("expert", "tm", None),
        P("expert", "tm", None),
        P("expert", "tm"),
        P(),
        P(),
        P("expert", None, None),
        P("expert", None, None),
        P("expert", "tm", None),
        P("expert", "tm", None),
        P("expert", None, "tm"),
        P("expert", "tm", None),
    )
    return jax.shard_map(
        on_device, mesh=mesh, in_specs=placed, out_specs=P("expert", "tm", None), check_vma=False
    )
```

```python
import functools

import jax
import jax.numpy as jnp
from jax import lax
from jax.experimental import pallas as pl
from jax.experimental.pallas import tpu as pltpu
from jax.sharding import PartitionSpec as P

eps = 1e-06
query_block = 1024


def head_attention(query_rows, key_rows, value_rows, offset_row):
    outputs = []
    for first in range(0, query_rows.shape[0], query_block):
        block = query_rows[first:first + query_block]
        scores = jnp.dot(block, key_rows.T, preferred_element_type=jnp.float32) + offset_row[None, :]
        highest = jnp.max(scores, axis=1, keepdims=True)
        unscaled = jnp.exp(scores - highest)
        total = jnp.sum(unscaled, axis=1, keepdims=True)
        weighted = jnp.dot(
            unscaled.astype(jnp.bfloat16), value_rows, preferred_element_type=jnp.float32
        )
        outputs.append((weighted / total).astype(jnp.bfloat16))
    return jnp.concatenate(outputs, axis=0)


def both_ways(n):
    order = []
    for k in range(1, n // 2 + 1):
        order += [k] if 2 * k == n else [k, n - k]
    return order


def exchange_kernel(axis, n, x_ref, y_ref, send_sems, recv_sems, local_sem):
    me = lax.axis_index(axis)
    barrier = pltpu.get_barrier_semaphore()
    for k in range(1, n):
        pl.semaphore_signal(
            barrier, inc=1, device_id={axis: lax.rem(me + k, n)}, device_id_type=pl.DeviceIdType.MESH
        )
    pl.semaphore_wait(barrier, n - 1)
    local = pltpu.make_async_copy(x_ref.at[me], y_ref.at[me], local_sem)
    local.start()
    copies = []
    for k in both_ways(n):
        peer = lax.rem(me + k, n)
        copy = pltpu.make_async_remote_copy(
            src_ref=x_ref.at[peer],
            dst_ref=y_ref.at[me],
            send_sem=send_sems.at[k],
            recv_sem=recv_sems.at[k],
            device_id={axis: peer},
            device_id_type=pl.DeviceIdType.MESH,
        )
        copy.start()
        copies.append(copy)
    local.wait()
    for copy in copies:
        copy.wait_send()
    for k in range(1, n):
        source = lax.rem(me + n - k, n)
        pltpu.make_async_remote_copy(
            src_ref=x_ref.at[source],
            dst_ref=y_ref.at[source],
            send_sem=send_sems.at[k],
            recv_sem=recv_sems.at[k],
            device_id={axis: source},
            device_id_type=pl.DeviceIdType.MESH,
        ).wait_recv()


def exchange(x, axis, collective_id):
    n = x.shape[0]
    return pl.pallas_call(
        functools.partial(exchange_kernel, axis, n),
        out_shape=jax.ShapeDtypeStruct(x.shape, x.dtype),
        in_specs=[pl.BlockSpec(memory_space=pl.ANY)],
        out_specs=pl.BlockSpec(memory_space=pl.ANY),
        scratch_shapes=[
            pltpu.SemaphoreType.DMA((n,)),
            pltpu.SemaphoreType.DMA((n,)),
            pltpu.SemaphoreType.DMA,
        ],
        compiler_params=pltpu.CompilerParams(collective_id=collective_id, has_side_effects=True),
    )(x)


def dispatch_kernel(
    expert_n, tm_n, slots_ref, own_up_ref, own_down_ref, arrived_ref, up_ref, down_ref,
    send_sems, recv_sems, weight_send_sems, weight_recv_sems, sibling_sems, local_sems,
):
    mesh_ids = pl.DeviceIdType.MESH
    half = tm_n // 2
    me_e = lax.axis_index("expert")
    me_t = lax.axis_index("tm")
    parity = me_t % 2
    rank = me_t // 2
    sibling = me_t + 1 - 2 * parity
    owned = (own_up_ref, own_down_ref)
    gathered = (up_ref, down_ref)
    barrier = pltpu.get_barrier_semaphore()
    for k in range(1, expert_n):
        pl.semaphore_signal(barrier, inc=1, device_id={"expert": lax.rem(me_e + k, expert_n)}, device_id_type=mesh_ids)
    for k in range(1, half):
        pl.semaphore_signal(barrier, inc=1, device_id={"tm": 2 * lax.rem(rank + k, half) + parity}, device_id_type=mesh_ids)
    pl.semaphore_signal(barrier, inc=1, device_id={"tm": sibling}, device_id_type=mesh_ids)
    pl.semaphore_wait(barrier, expert_n - 1 + half)
    local_copies = [pltpu.make_async_copy(slots_ref.at[me_e], arrived_ref.at[me_e], local_sems.at[0])]
    for w in range(2):
        local_copies.append(
            pltpu.make_async_copy(owned[w], gathered[w].at[parity, rank], local_sems.at[1 + w])
        )
    for copy in local_copies:
        copy.start()
    copies = []
    for k in range(1, half):
        for w in range(2):
            copy = pltpu.make_async_remote_copy(
                src_ref=owned[w],
                dst_ref=gathered[w].at[parity, rank],
                send_sem=weight_send_sems.at[w, k],
                recv_sem=weight_recv_sems.at[w, k],
                device_id={"tm": 2 * lax.rem(rank + k, half) + parity},
                device_id_type=mesh_ids,
            )
            copy.start()
            copies.append(copy)
    for k in both_ways(expert_n):
        peer = lax.rem(me_e + k, expert_n)
        copy = pltpu.make_async_remote_copy(
            src_ref=slots_ref.at[peer],
            dst_ref=arrived_ref.at[me_e],
            send_sem=send_sems.at[k],
            recv_sem=recv_sems.at[k],
            device_id={"expert": peer},
            device_id_type=mesh_ids,
        )
        copy.start()
        copies.append(copy)
    for copy in local_copies:
        copy.wait()
    forwards = []
    for w in range(2):
        for k in range(1, half):
            source = lax.rem(rank + half - k, half)
            pltpu.make_async_remote_copy(
                src_ref=owned[w],
                dst_ref=gathered[w].at[parity, source],
                send_sem=weight_send_sems.at[w, k],
                recv_sem=weight_recv_sems.at[w, k],
                device_id={"tm": 2 * source + parity},
                device_id_type=mesh_ids,
            ).wait_recv()
        forward = pltpu.make_async_remote_copy(
            src_ref=gathered[w].at[parity],
            dst_ref=gathered[w].at[parity],
            send_sem=sibling_sems.at[0, w],
            recv_sem=sibling_sems.at[1, w],
            device_id={"tm": sibling},
            device_id_type=mesh_ids,
        )
        forward.start()
        forwards.append(forward)
    for copy in copies:
        copy.wait_send()
    for k in range(1, expert_n):
        source = lax.rem(me_e + expert_n - k, expert_n)
        pltpu.make_async_remote_copy(
            src_ref=slots_ref.at[source],
            dst_ref=arrived_ref.at[source],
            send_sem=send_sems.at[k],
            recv_sem=recv_sems.at[k],
            device_id={"expert": source},
            device_id_type=mesh_ids,
        ).wait_recv()
    for w in range(2):
        forwards[w].wait_send()
        pltpu.make_async_remote_copy(
            src_ref=gathered[w].at[1 - parity],
            dst_ref=gathered[w].at[1 - parity],
            send_sem=sibling_sems.at[0, w],
            recv_sem=sibling_sems.at[1, w],
            device_id={"tm": sibling},
            device_id_type=mesh_ids,
        ).wait_recv()


def dispatch(slots, own_up, own_down, tm_n, collective_id):
    expert_n = slots.shape[0]
    gathered_shape = jax.ShapeDtypeStruct((2, tm_n // 2) + own_up.shape, own_up.dtype)
    return pl.pallas_call(
        functools.partial(dispatch_kernel, expert_n, tm_n),
        out_shape=(jax.ShapeDtypeStruct(slots.shape, slots.dtype), gathered_shape, gathered_shape),
        in_specs=[pl.BlockSpec(memory_space=pl.ANY)] * 3,
        out_specs=tuple(pl.BlockSpec(memory_space=pl.ANY) for _ in range(3)),
        scratch_shapes=[
            pltpu.SemaphoreType.DMA((expert_n,)),
            pltpu.SemaphoreType.DMA((expert_n,)),
            pltpu.SemaphoreType.DMA((2, tm_n // 2)),
            pltpu.SemaphoreType.DMA((2, tm_n // 2)),
            pltpu.SemaphoreType.DMA((2, 2)),
            pltpu.SemaphoreType.DMA((3,)),
        ],
        compiler_params=pltpu.CompilerParams(collective_id=collective_id, has_side_effects=True),
    )(slots, own_up, own_down)

def layer_norm(mixed, shift_row, scale_row):
    center = jnp.mean(mixed, axis=-1, keepdims=True)
    deviation = mixed - center
    variance = jnp.mean(deviation * deviation, axis=-1, keepdims=True)
    return deviation * lax.rsqrt(variance + eps) * (1.0 + scale_row) + shift_row


def on_device(
    latents,
    queries,
    keys,
    values,
    inpaint_mask,
    key_bias,
    out_weight,
    modulation,
    branch_gates,
    expert_ids,
    gate_values,
    up_weight,
    down_weight,
):
    tok_rows = latents.shape[1]
    model_width = latents.shape[2]
    head_count = key_bias.shape[0]
    head_width = model_width // head_count
    score_scale = head_width ** (-0.5)
    scaled_queries = queries[0] * jnp.asarray(score_scale, jnp.bfloat16)
    offsets = jnp.where(
        inpaint_mask[0][:, None] == 1, key_bias[None, :], jnp.zeros((), jnp.bfloat16)
    )
    offset_cols = jnp.zeros((tok_rows, head_count, 16), jnp.bfloat16).at[:, :, 0].set(offsets)
    packed = jnp.concatenate(
        [
            scaled_queries.reshape(tok_rows, head_count, head_width),
            keys[0].reshape(tok_rows, head_count, head_width),
            values[0].reshape(tok_rows, head_count, head_width),
            offset_cols,
        ],
        axis=2,
    )
    packed = jnp.transpose(packed, (1, 0, 2))
    gathered = lax.all_to_all(packed, "tm", split_axis=0, concat_axis=0, tiled=True)
    clip_rows = gathered.reshape(-1, 3 * head_width + 16)
    head_out = head_attention(
        clip_rows[:, :head_width],
        clip_rows[:, head_width:2 * head_width],
        clip_rows[:, 2 * head_width:3 * head_width],
        clip_rows[:, 3 * head_width].astype(jnp.float32),
    )
    head_out = head_out.reshape(head_count, tok_rows, head_width)
    attended_heads = lax.all_to_all(head_out, "tm", split_axis=0, concat_axis=0, tiled=True)
    projected = jnp.einsum(
        "hid,hdo->io",
        attended_heads,
        out_weight.reshape(head_count, head_width, model_width),
        preferred_element_type=jnp.float32,
    )
    mixed = latents[0].astype(jnp.float32) + branch_gates[0, 0][None, :] * projected
    normed = layer_norm(mixed, modulation[0, 0][None, :], modulation[0, 1][None, :]).astype(
        jnp.bfloat16
    )
    local_experts = up_weight.shape[0]
    source_count = lax.axis_size("expert")
    expert_count = local_experts * source_count
    capacity = 4 * tok_rows // expert_count
    choice_list = expert_ids[0].reshape(2 * tok_rows)
    hits = (choice_list[:, None] == jnp.arange(expert_count, dtype=jnp.int32)[None, :]).astype(
        jnp.int32
    )
    ranks = jnp.sum((jnp.cumsum(hits, axis=0) - 1) * hits, axis=1)
    target = choice_list * capacity + ranks
    placing = (
        jnp.arange(capacity * expert_count, dtype=jnp.int32)[:, None] == target[None, :]
    ).astype(jnp.bfloat16)
    token_placing = placing.reshape(capacity * expert_count, tok_rows, 2).sum(axis=2)
    slots = jnp.dot(token_placing, normed, preferred_element_type=jnp.float32).astype(jnp.bfloat16)
    slots = slots.reshape(expert_count, capacity, model_width)
    arrived, gathered_up, gathered_down = dispatch(
        slots, jnp.transpose(up_weight[0]), down_weight[0], lax.axis_size("tm"), 2
    )
    up_rows = gathered_up.reshape(-1, model_width)
    down_rows = gathered_down.reshape(-1, model_width)
    grouped = arrived.reshape(source_count * local_experts * capacity, model_width)
    hidden = jax.nn.gelu(
        jnp.einsum("rd,fd->rf", grouped, up_rows, preferred_element_type=jnp.float32),
        approximate=True,
    ).astype(jnp.bfloat16)
    produced = jnp.dot(hidden, down_rows, preferred_element_type=jnp.float32).astype(jnp.bfloat16)
    produced = produced.reshape(source_count * local_experts, capacity, model_width)
    returned = exchange(produced, "expert", 3)
    picked = jnp.einsum(
        "sa,sd->ad",
        placing,
        returned.reshape(expert_count * capacity, model_width),
        preferred_element_type=jnp.float32,
    )
    picked = picked.reshape(tok_rows, 2, model_width)
    combined = jnp.sum(gate_values[0][:, :, None] * picked, axis=1)
    layer_out = (mixed + branch_gates[0, 1][None, :] * combined).astype(jnp.bfloat16)
    return layer_out[None]


def solution(mesh):
    placed = (
        P("expert", "tm", None),
        P("expert", "tm", None),
        P("expert", "tm", None),
        P("expert", "tm", None),
        P("expert", "tm"),
        P(),
        P(),
        P("expert", None, None),
        P("expert", None, None),
        P("expert", "tm", None),
        P("expert", "tm", None),
        P("expert", None, "tm"),
        P("expert", "tm", None),
    )
    return jax.shard_map(
        on_device, mesh=mesh, in_specs=placed, out_specs=P("expert", "tm", None), check_vma=False
    )
```

```python
import functools

import jax
import jax.numpy as jnp
from jax import lax
from jax.experimental import pallas as pl
from jax.experimental.pallas import tpu as pltpu
from jax.sharding import PartitionSpec as P

eps = 1e-06
query_block = 2048


def head_attention(query_rows, key_rows, value_rows, offset_row):
    outputs = []
    for first in range(0, query_rows.shape[0], query_block):
        block = query_rows[first:first + query_block]
        scores = jnp.dot(block, key_rows.T, preferred_element_type=jnp.float32) + offset_row[None, :]
        highest = jnp.max(scores, axis=1, keepdims=True)
        unscaled = jnp.exp(scores - highest)
        total = jnp.sum(unscaled, axis=1, keepdims=True)
        weighted = jnp.dot(
            unscaled.astype(jnp.bfloat16), value_rows, preferred_element_type=jnp.float32
        )
        outputs.append((weighted / total).astype(jnp.bfloat16))
    return jnp.concatenate(outputs, axis=0)


def both_ways(n):
    order = []
    for k in range(1, n // 2 + 1):
        order += [k] if 2 * k == n else [k, n - k]
    return order


def exchange_kernel(axis, n, x_ref, y_ref, send_sems, recv_sems, local_sem):
    me = lax.axis_index(axis)
    barrier = pltpu.get_barrier_semaphore()
    for k in range(1, n):
        pl.semaphore_signal(
            barrier, inc=1, device_id={axis: lax.rem(me + k, n)}, device_id_type=pl.DeviceIdType.MESH
        )
    pl.semaphore_wait(barrier, n - 1)
    local = pltpu.make_async_copy(x_ref.at[me], y_ref.at[me], local_sem)
    local.start()
    copies = []
    for k in both_ways(n):
        peer = lax.rem(me + k, n)
        copy = pltpu.make_async_remote_copy(
            src_ref=x_ref.at[peer],
            dst_ref=y_ref.at[me],
            send_sem=send_sems.at[k],
            recv_sem=recv_sems.at[k],
            device_id={axis: peer},
            device_id_type=pl.DeviceIdType.MESH,
        )
        copy.start()
        copies.append(copy)
    local.wait()
    for copy in copies:
        copy.wait_send()
    for k in range(1, n):
        source = lax.rem(me + n - k, n)
        pltpu.make_async_remote_copy(
            src_ref=x_ref.at[source],
            dst_ref=y_ref.at[source],
            send_sem=send_sems.at[k],
            recv_sem=recv_sems.at[k],
            device_id={axis: source},
            device_id_type=pl.DeviceIdType.MESH,
        ).wait_recv()


def exchange(x, axis, collective_id):
    n = x.shape[0]
    return pl.pallas_call(
        functools.partial(exchange_kernel, axis, n),
        out_shape=jax.ShapeDtypeStruct(x.shape, x.dtype),
        in_specs=[pl.BlockSpec(memory_space=pl.ANY)],
        out_specs=pl.BlockSpec(memory_space=pl.ANY),
        scratch_shapes=[
            pltpu.SemaphoreType.DMA((n,)),
            pltpu.SemaphoreType.DMA((n,)),
            pltpu.SemaphoreType.DMA,
        ],
        compiler_params=pltpu.CompilerParams(collective_id=collective_id, has_side_effects=True),
    )(x)


def dispatch_kernel(
    expert_n, tm_n, slots_ref, own_up_ref, own_down_ref, arrived_ref, up_ref, down_ref,
    send_sems, recv_sems, weight_send_sems, weight_recv_sems, sibling_sems, local_sems,
):
    mesh_ids = pl.DeviceIdType.MESH
    half = tm_n // 2
    me_e = lax.axis_index("expert")
    me_t = lax.axis_index("tm")
    parity = me_t % 2
    rank = me_t // 2
    sibling = me_t + 1 - 2 * parity
    owned = (own_up_ref, own_down_ref)
    gathered = (up_ref, down_ref)
    barrier = pltpu.get_barrier_semaphore()
    for k in range(1, expert_n):
        pl.semaphore_signal(barrier, inc=1, device_id={"expert": lax.rem(me_e + k, expert_n)}, device_id_type=mesh_ids)
    for k in range(1, half):
        pl.semaphore_signal(barrier, inc=1, device_id={"tm": 2 * lax.rem(rank + k, half) + parity}, device_id_type=mesh_ids)
    pl.semaphore_signal(barrier, inc=1, device_id={"tm": sibling}, device_id_type=mesh_ids)
    pl.semaphore_wait(barrier, expert_n - 1 + half)
    local_copies = [pltpu.make_async_copy(slots_ref.at[me_e], arrived_ref.at[me_e], local_sems.at[0])]
    for w in range(2):
        local_copies.append(
            pltpu.make_async_copy(owned[w], gathered[w].at[parity, rank], local_sems.at[1 + w])
        )
    for copy in local_copies:
        copy.start()
    copies = []
    for k in range(1, half):
        for w in range(2):
            copy = pltpu.make_async_remote_copy(
                src_ref=owned[w],
                dst_ref=gathered[w].at[parity, rank],
                send_sem=weight_send_sems.at[w, k],
                recv_sem=weight_recv_sems.at[w, k],
                device_id={"tm": 2 * lax.rem(rank + k, half) + parity},
                device_id_type=mesh_ids,
            )
            copy.start()
            copies.append(copy)
    for k in both_ways(expert_n):
        peer = lax.rem(me_e + k, expert_n)
        copy = pltpu.make_async_remote_copy(
            src_ref=slots_ref.at[peer],
            dst_ref=arrived_ref.at[me_e],
            send_sem=send_sems.at[k],
            recv_sem=recv_sems.at[k],
            device_id={"expert": peer},
            device_id_type=mesh_ids,
        )
        copy.start()
        copies.append(copy)
    for copy in local_copies:
        copy.wait()
    forwards = []
    for w in range(2):
        for k in range(1, half):
            source = lax.rem(rank + half - k, half)
            pltpu.make_async_remote_copy(
                src_ref=owned[w],
                dst_ref=gathered[w].at[parity, source],
                send_sem=weight_send_sems.at[w, k],
                recv_sem=weight_recv_sems.at[w, k],
                device_id={"tm": 2 * source + parity},
                device_id_type=mesh_ids,
            ).wait_recv()
        forward = pltpu.make_async_remote_copy(
            src_ref=gathered[w].at[parity],
            dst_ref=gathered[w].at[parity],
            send_sem=sibling_sems.at[0, w],
            recv_sem=sibling_sems.at[1, w],
            device_id={"tm": sibling},
            device_id_type=mesh_ids,
        )
        forward.start()
        forwards.append(forward)
    for copy in copies:
        copy.wait_send()
    for k in range(1, expert_n):
        source = lax.rem(me_e + expert_n - k, expert_n)
        pltpu.make_async_remote_copy(
            src_ref=slots_ref.at[source],
            dst_ref=arrived_ref.at[source],
            send_sem=send_sems.at[k],
            recv_sem=recv_sems.at[k],
            device_id={"expert": source},
            device_id_type=mesh_ids,
        ).wait_recv()
    for w in range(2):
        forwards[w].wait_send()
        pltpu.make_async_remote_copy(
            src_ref=gathered[w].at[1 - parity],
            dst_ref=gathered[w].at[1 - parity],
            send_sem=sibling_sems.at[0, w],
            recv_sem=sibling_sems.at[1, w],
            device_id={"tm": sibling},
            device_id_type=mesh_ids,
        ).wait_recv()


def dispatch(slots, own_up, own_down, tm_n, collective_id):
    expert_n = slots.shape[0]
    gathered_shape = jax.ShapeDtypeStruct((2, tm_n // 2) + own_up.shape, own_up.dtype)
    return pl.pallas_call(
        functools.partial(dispatch_kernel, expert_n, tm_n),
        out_shape=(jax.ShapeDtypeStruct(slots.shape, slots.dtype), gathered_shape, gathered_shape),
        in_specs=[pl.BlockSpec(memory_space=pl.ANY)] * 3,
        out_specs=tuple(pl.BlockSpec(memory_space=pl.ANY) for _ in range(3)),
        scratch_shapes=[
            pltpu.SemaphoreType.DMA((expert_n,)),
            pltpu.SemaphoreType.DMA((expert_n,)),
            pltpu.SemaphoreType.DMA((2, tm_n // 2)),
            pltpu.SemaphoreType.DMA((2, tm_n // 2)),
            pltpu.SemaphoreType.DMA((2, 2)),
            pltpu.SemaphoreType.DMA((3,)),
        ],
        compiler_params=pltpu.CompilerParams(collective_id=collective_id, has_side_effects=True),
    )(slots, own_up, own_down)

def layer_norm(mixed, shift_row, scale_row):
    center = jnp.mean(mixed, axis=-1, keepdims=True)
    deviation = mixed - center
    variance = jnp.mean(deviation * deviation, axis=-1, keepdims=True)
    return deviation * lax.rsqrt(variance + eps) * (1.0 + scale_row) + shift_row


def on_device(
    latents,
    queries,
    keys,
    values,
    inpaint_mask,
    key_bias,
    out_weight,
    modulation,
    branch_gates,
    expert_ids,
    gate_values,
    up_weight,
    down_weight,
):
    tok_rows = latents.shape[1]
    model_width = latents.shape[2]
    head_count = key_bias.shape[0]
    head_width = model_width // head_count
    score_scale = head_width ** (-0.5)
    scaled_queries = queries[0] * jnp.asarray(score_scale, jnp.bfloat16)
    offsets = jnp.where(
        inpaint_mask[0][:, None] == 1, key_bias[None, :], jnp.zeros((), jnp.bfloat16)
    )
    offset_cols = jnp.zeros((tok_rows, head_count, 16), jnp.bfloat16).at[:, :, 0].set(offsets)
    packed = jnp.concatenate(
        [
            scaled_queries.reshape(tok_rows, head_count, head_width),
            keys[0].reshape(tok_rows, head_count, head_width),
            values[0].reshape(tok_rows, head_count, head_width),
            offset_cols,
        ],
        axis=2,
    )
    packed = jnp.transpose(packed, (1, 0, 2))
    gathered = lax.all_to_all(packed, "tm", split_axis=0, concat_axis=0, tiled=True)
    clip_rows = gathered.reshape(-1, 3 * head_width + 16)
    head_out = head_attention(
        clip_rows[:, :head_width],
        clip_rows[:, head_width:2 * head_width],
        clip_rows[:, 2 * head_width:3 * head_width],
        clip_rows[:, 3 * head_width].astype(jnp.float32),
    )
    head_out = head_out.reshape(head_count, tok_rows, head_width)
    attended_heads = lax.all_to_all(head_out, "tm", split_axis=0, concat_axis=0, tiled=True)
    projected = jnp.einsum(
        "hid,hdo->io",
        attended_heads,
        out_weight.reshape(head_count, head_width, model_width),
        preferred_element_type=jnp.float32,
    )
    mixed = latents[0].astype(jnp.float32) + branch_gates[0, 0][None, :] * projected
    normed = layer_norm(mixed, modulation[0, 0][None, :], modulation[0, 1][None, :]).astype(
        jnp.bfloat16
    )
    local_experts = up_weight.shape[0]
    source_count = lax.axis_size("expert")
    expert_count = local_experts * source_count
    capacity = 4 * tok_rows // expert_count
    choice_list = expert_ids[0].reshape(2 * tok_rows)
    hits = (choice_list[:, None] == jnp.arange(expert_count, dtype=jnp.int32)[None, :]).astype(
        jnp.int32
    )
    ranks = jnp.sum((jnp.cumsum(hits, axis=0) - 1) * hits, axis=1)
    target = choice_list * capacity + ranks
    placing = (
        jnp.arange(capacity * expert_count, dtype=jnp.int32)[:, None] == target[None, :]
    ).astype(jnp.bfloat16)
    token_placing = placing.reshape(capacity * expert_count, tok_rows, 2).sum(axis=2)
    slots = jnp.dot(token_placing, normed, preferred_element_type=jnp.float32).astype(jnp.bfloat16)
    slots = slots.reshape(expert_count, capacity, model_width)
    arrived, gathered_up, gathered_down = dispatch(
        slots, jnp.transpose(up_weight[0]), down_weight[0], lax.axis_size("tm"), 2
    )
    up_rows = gathered_up.reshape(-1, model_width)
    down_rows = gathered_down.reshape(-1, model_width)
    grouped = arrived.reshape(source_count * local_experts * capacity, model_width)
    hidden = jax.nn.gelu(
        jnp.einsum("rd,fd->rf", grouped, up_rows, preferred_element_type=jnp.float32),
        approximate=True,
    ).astype(jnp.bfloat16)
    produced = jnp.dot(hidden, down_rows, preferred_element_type=jnp.float32).astype(jnp.bfloat16)
    produced = produced.reshape(source_count * local_experts, capacity, model_width)
    returned = exchange(produced, "expert", 3)
    picked = jnp.einsum(
        "sa,sd->ad",
        placing,
        returned.reshape(expert_count * capacity, model_width),
        preferred_element_type=jnp.float32,
    )
    picked = picked.reshape(tok_rows, 2, model_width)
    combined = jnp.sum(gate_values[0][:, :, None] * picked, axis=1)
    layer_out = (mixed + branch_gates[0, 1][None, :] * combined).astype(jnp.bfloat16)
    return layer_out[None]


def solution(mesh):
    placed = (
        P("expert", "tm", None),
        P("expert", "tm", None),
        P("expert", "tm", None),
        P("expert", "tm", None),
        P("expert", "tm"),
        P(),
        P(),
        P("expert", None, None),
        P("expert", None, None),
        P("expert", "tm", None),
        P("expert", "tm", None),
        P("expert", None, "tm"),
        P("expert", "tm", None),
    )
    return jax.shard_map(
        on_device, mesh=mesh, in_specs=placed, out_specs=P("expert", "tm", None), check_vma=False
    )
```

```python
import functools

import jax
import jax.numpy as jnp
from jax import lax
from jax.experimental import pallas as pl
from jax.experimental.pallas import tpu as pltpu
from jax.sharding import PartitionSpec as P

eps = 1e-06
query_block = 1024


def head_attention(query_rows, key_rows, value_rows, offset_row):
    outputs = []
    for first in range(0, query_rows.shape[0], query_block):
        block = query_rows[first:first + query_block]
        scores = jnp.dot(block, key_rows.T, preferred_element_type=jnp.float32) + offset_row[None, :]
        highest = jnp.max(scores, axis=1, keepdims=True)
        unscaled = jnp.exp(scores - highest)
        total = jnp.sum(unscaled, axis=1, keepdims=True)
        weighted = jnp.dot(
            unscaled.astype(jnp.bfloat16), value_rows, preferred_element_type=jnp.float32
        )
        outputs.append((weighted / total).astype(jnp.bfloat16))
    return jnp.concatenate(outputs, axis=0)


def both_ways(n):
    order = []
    for k in range(1, n // 2 + 1):
        order += [k] if 2 * k == n else [k, n - k]
    return order


def exchange_kernel(axis, n, x_ref, y_ref, send_sems, recv_sems, local_sem):
    me = lax.axis_index(axis)
    barrier = pltpu.get_barrier_semaphore()
    for k in range(1, n):
        pl.semaphore_signal(
            barrier, inc=1, device_id={axis: lax.rem(me + k, n)}, device_id_type=pl.DeviceIdType.MESH
        )
    pl.semaphore_wait(barrier, n - 1)
    local = pltpu.make_async_copy(x_ref.at[me], y_ref.at[me], local_sem)
    local.start()
    copies = []
    for k in both_ways(n):
        peer = lax.rem(me + k, n)
        copy = pltpu.make_async_remote_copy(
            src_ref=x_ref.at[peer],
            dst_ref=y_ref.at[me],
            send_sem=send_sems.at[k],
            recv_sem=recv_sems.at[k],
            device_id={axis: peer},
            device_id_type=pl.DeviceIdType.MESH,
        )
        copy.start()
        copies.append(copy)
    local.wait()
    for copy in copies:
        copy.wait_send()
    for k in range(1, n):
        source = lax.rem(me + n - k, n)
        pltpu.make_async_remote_copy(
            src_ref=x_ref.at[source],
            dst_ref=y_ref.at[source],
            send_sem=send_sems.at[k],
            recv_sem=recv_sems.at[k],
            device_id={axis: source},
            device_id_type=pl.DeviceIdType.MESH,
        ).wait_recv()


def exchange(x, axis, collective_id):
    n = x.shape[0]
    return pl.pallas_call(
        functools.partial(exchange_kernel, axis, n),
        out_shape=jax.ShapeDtypeStruct(x.shape, x.dtype),
        in_specs=[pl.BlockSpec(memory_space=pl.ANY)],
        out_specs=pl.BlockSpec(memory_space=pl.ANY),
        scratch_shapes=[
            pltpu.SemaphoreType.DMA((n,)),
            pltpu.SemaphoreType.DMA((n,)),
            pltpu.SemaphoreType.DMA,
        ],
        compiler_params=pltpu.CompilerParams(collective_id=collective_id, has_side_effects=True),
    )(x)


def dispatch_kernel(
    expert_n, tm_n, slots_ref, own_up_ref, own_down_ref, arrived_ref, up_ref, down_ref,
    send_sems, recv_sems, weight_send_sems, weight_recv_sems, sibling_sems, local_sems,
):
    mesh_ids = pl.DeviceIdType.MESH
    half = tm_n // 2
    me_e = lax.axis_index("expert")
    me_t = lax.axis_index("tm")
    parity = me_t % 2
    rank = me_t // 2
    sibling = me_t + 1 - 2 * parity
    owned = (own_up_ref, own_down_ref)
    gathered = (up_ref, down_ref)
    barrier = pltpu.get_barrier_semaphore()
    for k in range(1, expert_n):
        pl.semaphore_signal(barrier, inc=1, device_id={"expert": lax.rem(me_e + k, expert_n)}, device_id_type=mesh_ids)
    for k in range(1, half):
        pl.semaphore_signal(barrier, inc=1, device_id={"tm": 2 * lax.rem(rank + k, half) + parity}, device_id_type=mesh_ids)
    pl.semaphore_signal(barrier, inc=1, device_id={"tm": sibling}, device_id_type=mesh_ids)
    pl.semaphore_wait(barrier, expert_n - 1 + half)
    local_copies = [pltpu.make_async_copy(slots_ref.at[me_e], arrived_ref.at[me_e], local_sems.at[0])]
    for w in range(2):
        local_copies.append(
            pltpu.make_async_copy(owned[w], gathered[w].at[parity, rank], local_sems.at[1 + w])
        )
    for copy in local_copies:
        copy.start()
    copies = []
    for k in range(1, half):
        for w in range(2):
            copy = pltpu.make_async_remote_copy(
                src_ref=owned[w],
                dst_ref=gathered[w].at[parity, rank],
                send_sem=weight_send_sems.at[w, k],
                recv_sem=weight_recv_sems.at[w, k],
                device_id={"tm": 2 * lax.rem(rank + k, half) + parity},
                device_id_type=mesh_ids,
            )
            copy.start()
            copies.append(copy)
    for k in both_ways(expert_n):
        peer = lax.rem(me_e + k, expert_n)
        copy = pltpu.make_async_remote_copy(
            src_ref=slots_ref.at[peer],
            dst_ref=arrived_ref.at[me_e],
            send_sem=send_sems.at[k],
            recv_sem=recv_sems.at[k],
            device_id={"expert": peer},
            device_id_type=mesh_ids,
        )
        copy.start()
        copies.append(copy)
    for copy in local_copies:
        copy.wait()
    forwards = []
    for w in range(2):
        for k in range(1, half):
            source = lax.rem(rank + half - k, half)
            pltpu.make_async_remote_copy(
                src_ref=owned[w],
                dst_ref=gathered[w].at[parity, source],
                send_sem=weight_send_sems.at[w, k],
                recv_sem=weight_recv_sems.at[w, k],
                device_id={"tm": 2 * source + parity},
                device_id_type=mesh_ids,
            ).wait_recv()
        forward = pltpu.make_async_remote_copy(
            src_ref=gathered[w].at[parity],
            dst_ref=gathered[w].at[parity],
            send_sem=sibling_sems.at[0, w],
            recv_sem=sibling_sems.at[1, w],
            device_id={"tm": sibling},
            device_id_type=mesh_ids,
        )
        forward.start()
        forwards.append(forward)
    for copy in copies:
        copy.wait_send()
    for k in range(1, expert_n):
        source = lax.rem(me_e + expert_n - k, expert_n)
        pltpu.make_async_remote_copy(
            src_ref=slots_ref.at[source],
            dst_ref=arrived_ref.at[source],
            send_sem=send_sems.at[k],
            recv_sem=recv_sems.at[k],
            device_id={"expert": source},
            device_id_type=mesh_ids,
        ).wait_recv()
    for w in range(2):
        forwards[w].wait_send()
        pltpu.make_async_remote_copy(
            src_ref=gathered[w].at[1 - parity],
            dst_ref=gathered[w].at[1 - parity],
            send_sem=sibling_sems.at[0, w],
            recv_sem=sibling_sems.at[1, w],
            device_id={"tm": sibling},
            device_id_type=mesh_ids,
        ).wait_recv()


def dispatch(slots, own_up, own_down, tm_n, collective_id):
    expert_n = slots.shape[0]
    gathered_shape = jax.ShapeDtypeStruct((2, tm_n // 2) + own_up.shape, own_up.dtype)
    return pl.pallas_call(
        functools.partial(dispatch_kernel, expert_n, tm_n),
        out_shape=(jax.ShapeDtypeStruct(slots.shape, slots.dtype), gathered_shape, gathered_shape),
        in_specs=[pl.BlockSpec(memory_space=pl.ANY)] * 3,
        out_specs=tuple(pl.BlockSpec(memory_space=pl.ANY) for _ in range(3)),
        scratch_shapes=[
            pltpu.SemaphoreType.DMA((expert_n,)),
            pltpu.SemaphoreType.DMA((expert_n,)),
            pltpu.SemaphoreType.DMA((2, tm_n // 2)),
            pltpu.SemaphoreType.DMA((2, tm_n // 2)),
            pltpu.SemaphoreType.DMA((2, 2)),
            pltpu.SemaphoreType.DMA((3,)),
        ],
        compiler_params=pltpu.CompilerParams(collective_id=collective_id, has_side_effects=True),
    )(slots, own_up, own_down)

def ffn_return_kernel(
    n, group, arrived_ref, up_ref, down_ref, out_ref, rows_buf, out_buf, send_sems, recv_sems, local_sem
):
    mesh_ids = pl.DeviceIdType.MESH
    me = lax.axis_index("expert")
    cap = arrived_ref.shape[1]
    barrier = pltpu.get_barrier_semaphore()
    for k in range(1, n):
        pl.semaphore_signal(barrier, inc=1, device_id={"expert": lax.rem(me + k, n)}, device_id_type=mesh_ids)
    pl.semaphore_wait(barrier, n - 1)
    copies = []
    local = None
    for c in range(n // group):
        for j in range(group):
            peer = lax.rem(me + c * group + j, n)
            rows_buf[pl.ds(j * cap, cap), :] = arrived_ref[peer]
        hidden = lax.dot_general(
            rows_buf[...], up_ref[...], (((1,), (1,)), ((), ())), preferred_element_type=jnp.float32
        )
        hidden = jax.nn.gelu(hidden, approximate=True).astype(jnp.bfloat16)
        produced = jnp.dot(hidden, down_ref[...], preferred_element_type=jnp.float32)
        out_buf[pl.ds(c * group * cap, group * cap), :] = produced.astype(jnp.bfloat16)
        for j in range(group):
            k = c * group + j
            block = out_buf.at[pl.ds(k * cap, cap)]
            if k == 0:
                local = pltpu.make_async_copy(block, out_ref.at[me], local_sem)
                local.start()
                continue
            copy = pltpu.make_async_remote_copy(
                src_ref=block,
                dst_ref=out_ref.at[me],
                send_sem=send_sems.at[k],
                recv_sem=recv_sems.at[k],
                device_id={"expert": lax.rem(me + k, n)},
                device_id_type=mesh_ids,
            )
            copy.start()
            copies.append(copy)
    local.wait()
    for copy in copies:
        copy.wait_send()
    for k in range(1, n):
        source = lax.rem(me + n - k, n)
        pltpu.make_async_remote_copy(
            src_ref=out_buf.at[pl.ds(k * cap, cap)],
            dst_ref=out_ref.at[source],
            send_sem=send_sems.at[k],
            recv_sem=recv_sems.at[k],
            device_id={"expert": source},
            device_id_type=mesh_ids,
        ).wait_recv()


def ffn_return(arrived, up_rows, down_rows, collective_id, group=8):
    n, cap, width = arrived.shape
    vmem = pl.BlockSpec(memory_space=pltpu.VMEM)
    return pl.pallas_call(
        functools.partial(ffn_return_kernel, n, group),
        out_shape=jax.ShapeDtypeStruct(arrived.shape, arrived.dtype),
        in_specs=[vmem, vmem, vmem],
        out_specs=pl.BlockSpec(memory_space=pl.ANY),
        scratch_shapes=[
            pltpu.VMEM((group * cap, width), arrived.dtype),
            pltpu.VMEM((n * cap, width), arrived.dtype),
            pltpu.SemaphoreType.DMA((n,)),
            pltpu.SemaphoreType.DMA((n,)),
            pltpu.SemaphoreType.DMA,
        ],
        compiler_params=pltpu.CompilerParams(collective_id=collective_id, has_side_effects=True),
    )(arrived, up_rows, down_rows)


def layer_norm(mixed, shift_row, scale_row):
    center = jnp.mean(mixed, axis=-1, keepdims=True)
    deviation = mixed - center
    variance = jnp.mean(deviation * deviation, axis=-1, keepdims=True)
    return deviation * lax.rsqrt(variance + eps) * (1.0 + scale_row) + shift_row


def on_device(
    latents,
    queries,
    keys,
    values,
    inpaint_mask,
    key_bias,
    out_weight,
    modulation,
    branch_gates,
    expert_ids,
    gate_values,
    up_weight,
    down_weight,
):
    tok_rows = latents.shape[1]
    model_width = latents.shape[2]
    head_count = key_bias.shape[0]
    head_width = model_width // head_count
    score_scale = head_width ** (-0.5)
    scaled_queries = queries[0] * jnp.asarray(score_scale, jnp.bfloat16)
    offsets = jnp.where(
        inpaint_mask[0][:, None] == 1, key_bias[None, :], jnp.zeros((), jnp.bfloat16)
    )
    offset_cols = jnp.zeros((tok_rows, head_count, 16), jnp.bfloat16).at[:, :, 0].set(offsets)
    packed = jnp.concatenate(
        [
            scaled_queries.reshape(tok_rows, head_count, head_width),
            keys[0].reshape(tok_rows, head_count, head_width),
            values[0].reshape(tok_rows, head_count, head_width),
            offset_cols,
        ],
        axis=2,
    )
    packed = jnp.transpose(packed, (1, 0, 2))
    gathered = lax.all_to_all(packed, "tm", split_axis=0, concat_axis=0, tiled=True)
    clip_rows = gathered.reshape(-1, 3 * head_width + 16)
    head_out = head_attention(
        clip_rows[:, :head_width],
        clip_rows[:, head_width:2 * head_width],
        clip_rows[:, 2 * head_width:3 * head_width],
        clip_rows[:, 3 * head_width].astype(jnp.float32),
    )
    head_out = head_out.reshape(head_count, tok_rows, head_width)
    attended_heads = lax.all_to_all(head_out, "tm", split_axis=0, concat_axis=0, tiled=True)
    projected = jnp.einsum(
        "hid,hdo->io",
        attended_heads,
        out_weight.reshape(head_count, head_width, model_width),
        preferred_element_type=jnp.float32,
    )
    mixed = latents[0].astype(jnp.float32) + branch_gates[0, 0][None, :] * projected
    normed = layer_norm(mixed, modulation[0, 0][None, :], modulation[0, 1][None, :]).astype(
        jnp.bfloat16
    )
    local_experts = up_weight.shape[0]
    source_count = lax.axis_size("expert")
    expert_count = local_experts * source_count
    capacity = 4 * tok_rows // expert_count
    choice_list = expert_ids[0].reshape(2 * tok_rows)
    hits = (choice_list[:, None] == jnp.arange(expert_count, dtype=jnp.int32)[None, :]).astype(
        jnp.int32
    )
    ranks = jnp.sum((jnp.cumsum(hits, axis=0) - 1) * hits, axis=1)
    target = choice_list * capacity + ranks
    placing = (
        jnp.arange(capacity * expert_count, dtype=jnp.int32)[:, None] == target[None, :]
    ).astype(jnp.bfloat16)
    token_placing = placing.reshape(capacity * expert_count, tok_rows, 2).sum(axis=2)
    slots = jnp.dot(token_placing, normed, preferred_element_type=jnp.float32).astype(jnp.bfloat16)
    slots = slots.reshape(expert_count, capacity, model_width)
    arrived, gathered_up, gathered_down = dispatch(
        slots, jnp.transpose(up_weight[0]), down_weight[0], lax.axis_size("tm"), 2
    )
    up_rows = gathered_up.reshape(-1, model_width)
    down_rows = gathered_down.reshape(-1, model_width)
    returned = ffn_return(arrived, up_rows, down_rows, 3)
    picked = jnp.einsum(
        "sa,sd->ad",
        placing,
        returned.reshape(expert_count * capacity, model_width),
        preferred_element_type=jnp.float32,
    )
    picked = picked.reshape(tok_rows, 2, model_width)
    combined = jnp.sum(gate_values[0][:, :, None] * picked, axis=1)
    layer_out = (mixed + branch_gates[0, 1][None, :] * combined).astype(jnp.bfloat16)
    return layer_out[None]


def solution(mesh):
    placed = (
        P("expert", "tm", None),
        P("expert", "tm", None),
        P("expert", "tm", None),
        P("expert", "tm", None),
        P("expert", "tm"),
        P(),
        P(),
        P("expert", None, None),
        P("expert", None, None),
        P("expert", "tm", None),
        P("expert", "tm", None),
        P("expert", None, "tm"),
        P("expert", "tm", None),
    )
    return jax.shard_map(
        on_device, mesh=mesh, in_specs=placed, out_specs=P("expert", "tm", None), check_vma=False
    )
```

```python
import functools

import jax
import jax.numpy as jnp
from jax import lax
from jax.experimental import pallas as pl
from jax.experimental.pallas import tpu as pltpu
from jax.sharding import PartitionSpec as P

eps = 1e-06
query_block = 1024


def head_attention(query_rows, key_rows, value_rows, offset_row):
    outputs = []
    for first in range(0, query_rows.shape[0], query_block):
        block = query_rows[first:first + query_block]
        scores = jnp.dot(block, key_rows.T, preferred_element_type=jnp.float32) + offset_row[None, :]
        highest = jnp.max(scores, axis=1, keepdims=True)
        unscaled = jnp.exp(scores - highest)
        total = jnp.sum(unscaled, axis=1, keepdims=True)
        weighted = jnp.dot(
            unscaled.astype(jnp.bfloat16), value_rows, preferred_element_type=jnp.float32
        )
        outputs.append((weighted / total).astype(jnp.bfloat16))
    return jnp.concatenate(outputs, axis=0)


def both_ways(n):
    order = []
    for k in range(1, n // 2 + 1):
        order += [k] if 2 * k == n else [k, n - k]
    return order


def exchange_kernel(axis, n, x_ref, y_ref, send_sems, recv_sems, local_sem):
    me = lax.axis_index(axis)
    barrier = pltpu.get_barrier_semaphore()
    for k in range(1, n):
        pl.semaphore_signal(
            barrier, inc=1, device_id={axis: lax.rem(me + k, n)}, device_id_type=pl.DeviceIdType.MESH
        )
    pl.semaphore_wait(barrier, n - 1)
    local = pltpu.make_async_copy(x_ref.at[me], y_ref.at[me], local_sem)
    local.start()
    copies = []
    for k in both_ways(n):
        peer = lax.rem(me + k, n)
        copy = pltpu.make_async_remote_copy(
            src_ref=x_ref.at[peer],
            dst_ref=y_ref.at[me],
            send_sem=send_sems.at[k],
            recv_sem=recv_sems.at[k],
            device_id={axis: peer},
            device_id_type=pl.DeviceIdType.MESH,
        )
        copy.start()
        copies.append(copy)
    local.wait()
    for copy in copies:
        copy.wait_send()
    for k in range(1, n):
        source = lax.rem(me + n - k, n)
        pltpu.make_async_remote_copy(
            src_ref=x_ref.at[source],
            dst_ref=y_ref.at[source],
            send_sem=send_sems.at[k],
            recv_sem=recv_sems.at[k],
            device_id={axis: source},
            device_id_type=pl.DeviceIdType.MESH,
        ).wait_recv()


def exchange(x, axis, collective_id):
    n = x.shape[0]
    return pl.pallas_call(
        functools.partial(exchange_kernel, axis, n),
        out_shape=jax.ShapeDtypeStruct(x.shape, x.dtype),
        in_specs=[pl.BlockSpec(memory_space=pl.ANY)],
        out_specs=pl.BlockSpec(memory_space=pl.ANY),
        scratch_shapes=[
            pltpu.SemaphoreType.DMA((n,)),
            pltpu.SemaphoreType.DMA((n,)),
            pltpu.SemaphoreType.DMA,
        ],
        compiler_params=pltpu.CompilerParams(collective_id=collective_id, has_side_effects=True),
    )(x)


def dispatch_kernel(
    expert_n, tm_n, slots_ref, own_up_ref, own_down_ref, arrived_ref, up_ref, down_ref,
    send_sems, recv_sems, weight_send_sems, weight_recv_sems, sibling_sems, local_sems,
):
    mesh_ids = pl.DeviceIdType.MESH
    half = tm_n // 2
    me_e = lax.axis_index("expert")
    me_t = lax.axis_index("tm")
    parity = me_t % 2
    rank = me_t // 2
    sibling = me_t + 1 - 2 * parity
    owned = (own_up_ref, own_down_ref)
    gathered = (up_ref, down_ref)
    barrier = pltpu.get_barrier_semaphore()
    for k in range(1, expert_n):
        pl.semaphore_signal(barrier, inc=1, device_id={"expert": lax.rem(me_e + k, expert_n)}, device_id_type=mesh_ids)
    for k in range(1, half):
        pl.semaphore_signal(barrier, inc=1, device_id={"tm": 2 * lax.rem(rank + k, half) + parity}, device_id_type=mesh_ids)
    pl.semaphore_signal(barrier, inc=1, device_id={"tm": sibling}, device_id_type=mesh_ids)
    pl.semaphore_wait(barrier, expert_n - 1 + half)
    local_copies = [pltpu.make_async_copy(slots_ref.at[me_e], arrived_ref.at[me_e], local_sems.at[0])]
    for w in range(2):
        local_copies.append(
            pltpu.make_async_copy(owned[w], gathered[w].at[parity, rank], local_sems.at[1 + w])
        )
    for copy in local_copies:
        copy.start()
    copies = []
    for k in range(1, half):
        for w in range(2):
            copy = pltpu.make_async_remote_copy(
                src_ref=owned[w],
                dst_ref=gathered[w].at[parity, rank],
                send_sem=weight_send_sems.at[w, k],
                recv_sem=weight_recv_sems.at[w, k],
                device_id={"tm": 2 * lax.rem(rank + k, half) + parity},
                device_id_type=mesh_ids,
            )
            copy.start()
            copies.append(copy)
    for k in both_ways(expert_n):
        peer = lax.rem(me_e + k, expert_n)
        copy = pltpu.make_async_remote_copy(
            src_ref=slots_ref.at[peer],
            dst_ref=arrived_ref.at[me_e],
            send_sem=send_sems.at[k],
            recv_sem=recv_sems.at[k],
            device_id={"expert": peer},
            device_id_type=mesh_ids,
        )
        copy.start()
        copies.append(copy)
    for copy in local_copies:
        copy.wait()
    forwards = []
    for w in range(2):
        for k in range(1, half):
            source = lax.rem(rank + half - k, half)
            pltpu.make_async_remote_copy(
                src_ref=owned[w],
                dst_ref=gathered[w].at[parity, source],
                send_sem=weight_send_sems.at[w, k],
                recv_sem=weight_recv_sems.at[w, k],
                device_id={"tm": 2 * source + parity},
                device_id_type=mesh_ids,
            ).wait_recv()
        forward = pltpu.make_async_remote_copy(
            src_ref=gathered[w].at[parity],
            dst_ref=gathered[w].at[parity],
            send_sem=sibling_sems.at[0, w],
            recv_sem=sibling_sems.at[1, w],
            device_id={"tm": sibling},
            device_id_type=mesh_ids,
        )
        forward.start()
        forwards.append(forward)
    for copy in copies:
        copy.wait_send()
    for k in range(1, expert_n):
        source = lax.rem(me_e + expert_n - k, expert_n)
        pltpu.make_async_remote_copy(
            src_ref=slots_ref.at[source],
            dst_ref=arrived_ref.at[source],
            send_sem=send_sems.at[k],
            recv_sem=recv_sems.at[k],
            device_id={"expert": source},
            device_id_type=mesh_ids,
        ).wait_recv()
    for w in range(2):
        forwards[w].wait_send()
        pltpu.make_async_remote_copy(
            src_ref=gathered[w].at[1 - parity],
            dst_ref=gathered[w].at[1 - parity],
            send_sem=sibling_sems.at[0, w],
            recv_sem=sibling_sems.at[1, w],
            device_id={"tm": sibling},
            device_id_type=mesh_ids,
        ).wait_recv()


def dispatch(slots, own_up, own_down, tm_n, collective_id):
    expert_n = slots.shape[0]
    gathered_shape = jax.ShapeDtypeStruct((2, tm_n // 2) + own_up.shape, own_up.dtype)
    return pl.pallas_call(
        functools.partial(dispatch_kernel, expert_n, tm_n),
        out_shape=(jax.ShapeDtypeStruct(slots.shape, slots.dtype), gathered_shape, gathered_shape),
        in_specs=[pl.BlockSpec(memory_space=pl.ANY)] * 3,
        out_specs=tuple(pl.BlockSpec(memory_space=pl.ANY) for _ in range(3)),
        scratch_shapes=[
            pltpu.SemaphoreType.DMA((expert_n,)),
            pltpu.SemaphoreType.DMA((expert_n,)),
            pltpu.SemaphoreType.DMA((2, tm_n // 2)),
            pltpu.SemaphoreType.DMA((2, tm_n // 2)),
            pltpu.SemaphoreType.DMA((2, 2)),
            pltpu.SemaphoreType.DMA((3,)),
        ],
        compiler_params=pltpu.CompilerParams(collective_id=collective_id, has_side_effects=True),
    )(slots, own_up, own_down)

def ffn_return_kernel(
    n, group, arrived_ref, up_ref, down_ref, out_ref, rows_buf, out_buf, send_sems, recv_sems, local_sem
):
    mesh_ids = pl.DeviceIdType.MESH
    me = lax.axis_index("expert")
    cap = arrived_ref.shape[1]
    barrier = pltpu.get_barrier_semaphore()
    for k in range(1, n):
        pl.semaphore_signal(barrier, inc=1, device_id={"expert": lax.rem(me + k, n)}, device_id_type=mesh_ids)
    pl.semaphore_wait(barrier, n - 1)
    copies = []
    local = None
    for c in range(n // group):
        for j in range(group):
            peer = lax.rem(me + c * group + j, n)
            rows_buf[pl.ds(j * cap, cap), :] = arrived_ref[peer]
        hidden = lax.dot_general(
            rows_buf[...], up_ref[...], (((1,), (1,)), ((), ())), preferred_element_type=jnp.float32
        )
        hidden = jax.nn.gelu(hidden, approximate=True).astype(jnp.bfloat16)
        produced = jnp.dot(hidden, down_ref[...], preferred_element_type=jnp.float32)
        out_buf[pl.ds(c * group * cap, group * cap), :] = produced.astype(jnp.bfloat16)
        for j in range(group):
            k = c * group + j
            block = out_buf.at[pl.ds(k * cap, cap)]
            if k == 0:
                local = pltpu.make_async_copy(block, out_ref.at[me], local_sem)
                local.start()
                continue
            copy = pltpu.make_async_remote_copy(
                src_ref=block,
                dst_ref=out_ref.at[me],
                send_sem=send_sems.at[k],
                recv_sem=recv_sems.at[k],
                device_id={"expert": lax.rem(me + k, n)},
                device_id_type=mesh_ids,
            )
            copy.start()
            copies.append(copy)
    local.wait()
    for copy in copies:
        copy.wait_send()
    for k in range(1, n):
        source = lax.rem(me + n - k, n)
        pltpu.make_async_remote_copy(
            src_ref=out_buf.at[pl.ds(k * cap, cap)],
            dst_ref=out_ref.at[source],
            send_sem=send_sems.at[k],
            recv_sem=recv_sems.at[k],
            device_id={"expert": source},
            device_id_type=mesh_ids,
        ).wait_recv()


def ffn_return(arrived, up_rows, down_rows, collective_id, group=8):
    n, cap, width = arrived.shape
    vmem = pl.BlockSpec(memory_space=pltpu.VMEM)
    return pl.pallas_call(
        functools.partial(ffn_return_kernel, n, group),
        out_shape=jax.ShapeDtypeStruct(arrived.shape, arrived.dtype),
        in_specs=[vmem, vmem, vmem],
        out_specs=pl.BlockSpec(memory_space=pl.ANY),
        scratch_shapes=[
            pltpu.VMEM((group * cap, width), arrived.dtype),
            pltpu.VMEM((n * cap, width), arrived.dtype),
            pltpu.SemaphoreType.DMA((n,)),
            pltpu.SemaphoreType.DMA((n,)),
            pltpu.SemaphoreType.DMA,
        ],
        compiler_params=pltpu.CompilerParams(collective_id=collective_id, has_side_effects=True),
    )(arrived, up_rows, down_rows)


def layer_norm(mixed, shift_row, scale_row):
    center = jnp.mean(mixed, axis=-1, keepdims=True)
    deviation = mixed - center
    variance = jnp.mean(deviation * deviation, axis=-1, keepdims=True)
    return deviation * lax.rsqrt(variance + eps) * (1.0 + scale_row) + shift_row


def on_device(
    latents,
    queries,
    keys,
    values,
    inpaint_mask,
    key_bias,
    out_weight,
    modulation,
    branch_gates,
    expert_ids,
    gate_values,
    up_weight,
    down_weight,
):
    tok_rows = latents.shape[1]
    model_width = latents.shape[2]
    head_count = key_bias.shape[0]
    head_width = model_width // head_count
    score_scale = head_width ** (-0.5)
    scaled_queries = queries[0] * jnp.asarray(score_scale, jnp.bfloat16)
    offsets = jnp.where(
        inpaint_mask[0][:, None] == 1, key_bias[None, :], jnp.zeros((), jnp.bfloat16)
    )
    offset_cols = jnp.zeros((tok_rows, head_count, 16), jnp.bfloat16).at[:, :, 0].set(offsets)
    packed = jnp.concatenate(
        [
            scaled_queries.reshape(tok_rows, head_count, head_width),
            keys[0].reshape(tok_rows, head_count, head_width),
            values[0].reshape(tok_rows, head_count, head_width),
            offset_cols,
        ],
        axis=2,
    )
    packed = jnp.transpose(packed, (1, 0, 2))
    gathered = lax.all_to_all(packed, "tm", split_axis=0, concat_axis=0, tiled=True)
    clip_rows = gathered.reshape(-1, 3 * head_width + 16)
    head_out = head_attention(
        clip_rows[:, :head_width],
        clip_rows[:, head_width:2 * head_width],
        clip_rows[:, 2 * head_width:3 * head_width],
        clip_rows[:, 3 * head_width].astype(jnp.float32),
    )
    head_out = head_out.reshape(head_count, tok_rows, head_width)
    attended_heads = lax.all_to_all(head_out, "tm", split_axis=0, concat_axis=0, tiled=True)
    projected = jnp.einsum(
        "hid,hdo->io",
        attended_heads,
        out_weight.reshape(head_count, head_width, model_width),
        preferred_element_type=jnp.float32,
    )
    mixed = latents[0].astype(jnp.float32) + branch_gates[0, 0][None, :] * projected
    normed = layer_norm(mixed, modulation[0, 0][None, :], modulation[0, 1][None, :]).astype(
        jnp.bfloat16
    )
    local_experts = up_weight.shape[0]
    source_count = lax.axis_size("expert")
    expert_count = local_experts * source_count
    capacity = 4 * tok_rows // expert_count
    choice_list = expert_ids[0].reshape(2 * tok_rows)
    hits = (choice_list[:, None] == jnp.arange(expert_count, dtype=jnp.int32)[None, :]).astype(
        jnp.int32
    )
    ranks = jnp.sum((jnp.cumsum(hits, axis=0) - 1) * hits, axis=1)
    target = choice_list * capacity + ranks
    placing = (
        jnp.arange(capacity * expert_count, dtype=jnp.int32)[:, None] == target[None, :]
    ).astype(jnp.bfloat16)
    token_placing = placing.reshape(capacity * expert_count, tok_rows, 2).sum(axis=2)
    slots = jnp.dot(token_placing, normed, preferred_element_type=jnp.float32).astype(jnp.bfloat16)
    slots = slots.reshape(expert_count, capacity, model_width)
    arrived, gathered_up, gathered_down = dispatch(
        slots, jnp.transpose(up_weight[0]), down_weight[0], lax.axis_size("tm"), 2
    )
    up_rows = gathered_up.reshape(-1, model_width)
    down_rows = gathered_down.reshape(-1, model_width)
    returned = ffn_return(arrived, up_rows, down_rows, 3, group=4)
    picked = jnp.einsum(
        "sa,sd->ad",
        placing,
        returned.reshape(expert_count * capacity, model_width),
        preferred_element_type=jnp.float32,
    )
    picked = picked.reshape(tok_rows, 2, model_width)
    combined = jnp.sum(gate_values[0][:, :, None] * picked, axis=1)
    layer_out = (mixed + branch_gates[0, 1][None, :] * combined).astype(jnp.bfloat16)
    return layer_out[None]


def solution(mesh):
    placed = (
        P("expert", "tm", None),
        P("expert", "tm", None),
        P("expert", "tm", None),
        P("expert", "tm", None),
        P("expert", "tm"),
        P(),
        P(),
        P("expert", None, None),
        P("expert", None, None),
        P("expert", "tm", None),
        P("expert", "tm", None),
        P("expert", None, "tm"),
        P("expert", "tm", None),
    )
    return jax.shard_map(
        on_device, mesh=mesh, in_specs=placed, out_specs=P("expert", "tm", None), check_vma=False
    )
```

```python
import functools

import jax
import jax.numpy as jnp
from jax import lax
from jax.experimental import pallas as pl
from jax.experimental.pallas import tpu as pltpu
from jax.sharding import PartitionSpec as P

eps = 1e-06
query_block = 1024


def head_attention(query_rows, key_rows, value_rows, offset_row):
    outputs = []
    for first in range(0, query_rows.shape[0], query_block):
        block = query_rows[first:first + query_block]
        scores = jnp.dot(block, key_rows.T, preferred_element_type=jnp.float32) + offset_row[None, :]
        highest = jnp.max(scores, axis=1, keepdims=True)
        unscaled = jnp.exp(scores - highest)
        total = jnp.sum(unscaled, axis=1, keepdims=True)
        weighted = jnp.dot(
            unscaled.astype(jnp.bfloat16), value_rows, preferred_element_type=jnp.float32
        )
        outputs.append((weighted / total).astype(jnp.bfloat16))
    return jnp.concatenate(outputs, axis=0)


def both_ways(n):
    order = []
    for k in range(1, n // 2 + 1):
        order += [k] if 2 * k == n else [k, n - k]
    return order


def exchange_kernel(axis, n, x_ref, y_ref, send_sems, recv_sems, local_sem):
    me = lax.axis_index(axis)
    barrier = pltpu.get_barrier_semaphore()
    for k in range(1, n):
        pl.semaphore_signal(
            barrier, inc=1, device_id={axis: lax.rem(me + k, n)}, device_id_type=pl.DeviceIdType.MESH
        )
    pl.semaphore_wait(barrier, n - 1)
    local = pltpu.make_async_copy(x_ref.at[me], y_ref.at[me], local_sem)
    local.start()
    copies = []
    for k in both_ways(n):
        peer = lax.rem(me + k, n)
        copy = pltpu.make_async_remote_copy(
            src_ref=x_ref.at[peer],
            dst_ref=y_ref.at[me],
            send_sem=send_sems.at[k],
            recv_sem=recv_sems.at[k],
            device_id={axis: peer},
            device_id_type=pl.DeviceIdType.MESH,
        )
        copy.start()
        copies.append(copy)
    local.wait()
    for copy in copies:
        copy.wait_send()
    for k in range(1, n):
        source = lax.rem(me + n - k, n)
        pltpu.make_async_remote_copy(
            src_ref=x_ref.at[source],
            dst_ref=y_ref.at[source],
            send_sem=send_sems.at[k],
            recv_sem=recv_sems.at[k],
            device_id={axis: source},
            device_id_type=pl.DeviceIdType.MESH,
        ).wait_recv()


def exchange(x, axis, collective_id):
    n = x.shape[0]
    return pl.pallas_call(
        functools.partial(exchange_kernel, axis, n),
        out_shape=jax.ShapeDtypeStruct(x.shape, x.dtype),
        in_specs=[pl.BlockSpec(memory_space=pl.ANY)],
        out_specs=pl.BlockSpec(memory_space=pl.ANY),
        scratch_shapes=[
            pltpu.SemaphoreType.DMA((n,)),
            pltpu.SemaphoreType.DMA((n,)),
            pltpu.SemaphoreType.DMA,
        ],
        compiler_params=pltpu.CompilerParams(collective_id=collective_id, has_side_effects=True),
    )(x)


def dispatch_kernel(
    expert_n, tm_n, slots_ref, own_up_ref, own_down_ref, arrived_ref, up_ref, down_ref,
    send_sems, recv_sems, weight_send_sems, weight_recv_sems, sibling_sems, local_sems,
):
    mesh_ids = pl.DeviceIdType.MESH
    half = tm_n // 2
    me_e = lax.axis_index("expert")
    me_t = lax.axis_index("tm")
    parity = me_t % 2
    rank = me_t // 2
    sibling = me_t + 1 - 2 * parity
    owned = (own_up_ref, own_down_ref)
    gathered = (up_ref, down_ref)
    barrier = pltpu.get_barrier_semaphore()
    for k in range(1, expert_n):
        pl.semaphore_signal(barrier, inc=1, device_id={"expert": lax.rem(me_e + k, expert_n)}, device_id_type=mesh_ids)
    for k in range(1, half):
        pl.semaphore_signal(barrier, inc=1, device_id={"tm": 2 * lax.rem(rank + k, half) + parity}, device_id_type=mesh_ids)
    pl.semaphore_signal(barrier, inc=1, device_id={"tm": sibling}, device_id_type=mesh_ids)
    pl.semaphore_wait(barrier, expert_n - 1 + half)
    local_copies = [pltpu.make_async_copy(slots_ref.at[me_e], arrived_ref.at[me_e], local_sems.at[0])]
    for w in range(2):
        local_copies.append(
            pltpu.make_async_copy(owned[w], gathered[w].at[parity, rank], local_sems.at[1 + w])
        )
    for copy in local_copies:
        copy.start()
    copies = []
    for k in both_ways(expert_n):
        peer = lax.rem(me_e + k, expert_n)
        copy = pltpu.make_async_remote_copy(
            src_ref=slots_ref.at[peer],
            dst_ref=arrived_ref.at[me_e],
            send_sem=send_sems.at[k],
            recv_sem=recv_sems.at[k],
            device_id={"expert": peer},
            device_id_type=mesh_ids,
        )
        copy.start()
        copies.append(copy)
    for k in range(1, half):
        for w in range(2):
            copy = pltpu.make_async_remote_copy(
                src_ref=owned[w],
                dst_ref=gathered[w].at[parity, rank],
                send_sem=weight_send_sems.at[w, k],
                recv_sem=weight_recv_sems.at[w, k],
                device_id={"tm": 2 * lax.rem(rank + k, half) + parity},
                device_id_type=mesh_ids,
            )
            copy.start()
            copies.append(copy)
    for copy in local_copies:
        copy.wait()
    forwards = []
    for w in range(2):
        for k in range(1, half):
            source = lax.rem(rank + half - k, half)
            pltpu.make_async_remote_copy(
                src_ref=owned[w],
                dst_ref=gathered[w].at[parity, source],
                send_sem=weight_send_sems.at[w, k],
                recv_sem=weight_recv_sems.at[w, k],
                device_id={"tm": 2 * source + parity},
                device_id_type=mesh_ids,
            ).wait_recv()
        forward = pltpu.make_async_remote_copy(
            src_ref=gathered[w].at[parity],
            dst_ref=gathered[w].at[parity],
            send_sem=sibling_sems.at[0, w],
            recv_sem=sibling_sems.at[1, w],
            device_id={"tm": sibling},
            device_id_type=mesh_ids,
        )
        forward.start()
        forwards.append(forward)
    for copy in copies:
        copy.wait_send()
    for k in range(1, expert_n):
        source = lax.rem(me_e + expert_n - k, expert_n)
        pltpu.make_async_remote_copy(
            src_ref=slots_ref.at[source],
            dst_ref=arrived_ref.at[source],
            send_sem=send_sems.at[k],
            recv_sem=recv_sems.at[k],
            device_id={"expert": source},
            device_id_type=mesh_ids,
        ).wait_recv()
    for w in range(2):
        forwards[w].wait_send()
        pltpu.make_async_remote_copy(
            src_ref=gathered[w].at[1 - parity],
            dst_ref=gathered[w].at[1 - parity],
            send_sem=sibling_sems.at[0, w],
            recv_sem=sibling_sems.at[1, w],
            device_id={"tm": sibling},
            device_id_type=mesh_ids,
        ).wait_recv()


def dispatch(slots, own_up, own_down, tm_n, collective_id):
    expert_n = slots.shape[0]
    gathered_shape = jax.ShapeDtypeStruct((2, tm_n // 2) + own_up.shape, own_up.dtype)
    return pl.pallas_call(
        functools.partial(dispatch_kernel, expert_n, tm_n),
        out_shape=(jax.ShapeDtypeStruct(slots.shape, slots.dtype), gathered_shape, gathered_shape),
        in_specs=[pl.BlockSpec(memory_space=pl.ANY)] * 3,
        out_specs=tuple(pl.BlockSpec(memory_space=pl.ANY) for _ in range(3)),
        scratch_shapes=[
            pltpu.SemaphoreType.DMA((expert_n,)),
            pltpu.SemaphoreType.DMA((expert_n,)),
            pltpu.SemaphoreType.DMA((2, tm_n // 2)),
            pltpu.SemaphoreType.DMA((2, tm_n // 2)),
            pltpu.SemaphoreType.DMA((2, 2)),
            pltpu.SemaphoreType.DMA((3,)),
        ],
        compiler_params=pltpu.CompilerParams(collective_id=collective_id, has_side_effects=True),
    )(slots, own_up, own_down)

def layer_norm(mixed, shift_row, scale_row):
    center = jnp.mean(mixed, axis=-1, keepdims=True)
    deviation = mixed - center
    variance = jnp.mean(deviation * deviation, axis=-1, keepdims=True)
    return deviation * lax.rsqrt(variance + eps) * (1.0 + scale_row) + shift_row


def on_device(
    latents,
    queries,
    keys,
    values,
    inpaint_mask,
    key_bias,
    out_weight,
    modulation,
    branch_gates,
    expert_ids,
    gate_values,
    up_weight,
    down_weight,
):
    tok_rows = latents.shape[1]
    model_width = latents.shape[2]
    head_count = key_bias.shape[0]
    head_width = model_width // head_count
    score_scale = head_width ** (-0.5)
    scaled_queries = queries[0] * jnp.asarray(score_scale, jnp.bfloat16)
    offsets = jnp.where(
        inpaint_mask[0][:, None] == 1, key_bias[None, :], jnp.zeros((), jnp.bfloat16)
    )
    offset_cols = jnp.zeros((tok_rows, head_count, 16), jnp.bfloat16).at[:, :, 0].set(offsets)
    packed = jnp.concatenate(
        [
            scaled_queries.reshape(tok_rows, head_count, head_width),
            keys[0].reshape(tok_rows, head_count, head_width),
            values[0].reshape(tok_rows, head_count, head_width),
            offset_cols,
        ],
        axis=2,
    )
    packed = jnp.transpose(packed, (1, 0, 2))
    gathered = lax.all_to_all(packed, "tm", split_axis=0, concat_axis=0, tiled=True)
    clip_rows = gathered.reshape(-1, 3 * head_width + 16)
    head_out = head_attention(
        clip_rows[:, :head_width],
        clip_rows[:, head_width:2 * head_width],
        clip_rows[:, 2 * head_width:3 * head_width],
        clip_rows[:, 3 * head_width].astype(jnp.float32),
    )
    head_out = head_out.reshape(head_count, tok_rows, head_width)
    attended_heads = lax.all_to_all(head_out, "tm", split_axis=0, concat_axis=0, tiled=True)
    projected = jnp.einsum(
        "hid,hdo->io",
        attended_heads,
        out_weight.reshape(head_count, head_width, model_width),
        preferred_element_type=jnp.float32,
    )
    mixed = latents[0].astype(jnp.float32) + branch_gates[0, 0][None, :] * projected
    normed = layer_norm(mixed, modulation[0, 0][None, :], modulation[0, 1][None, :]).astype(
        jnp.bfloat16
    )
    local_experts = up_weight.shape[0]
    source_count = lax.axis_size("expert")
    expert_count = local_experts * source_count
    capacity = 4 * tok_rows // expert_count
    choice_list = expert_ids[0].reshape(2 * tok_rows)
    hits = (choice_list[:, None] == jnp.arange(expert_count, dtype=jnp.int32)[None, :]).astype(
        jnp.int32
    )
    ranks = jnp.sum((jnp.cumsum(hits, axis=0) - 1) * hits, axis=1)
    target = choice_list * capacity + ranks
    placing = (
        jnp.arange(capacity * expert_count, dtype=jnp.int32)[:, None] == target[None, :]
    ).astype(jnp.bfloat16)
    token_placing = placing.reshape(capacity * expert_count, tok_rows, 2).sum(axis=2)
    slots = jnp.dot(token_placing, normed, preferred_element_type=jnp.float32).astype(jnp.bfloat16)
    slots = slots.reshape(expert_count, capacity, model_width)
    arrived, gathered_up, gathered_down = dispatch(
        slots, jnp.transpose(up_weight[0]), down_weight[0], lax.axis_size("tm"), 2
    )
    up_rows = gathered_up.reshape(-1, model_width)
    down_rows = gathered_down.reshape(-1, model_width)
    grouped = arrived.reshape(source_count * local_experts * capacity, model_width)
    hidden = jax.nn.gelu(
        jnp.einsum("rd,fd->rf", grouped, up_rows, preferred_element_type=jnp.float32),
        approximate=True,
    ).astype(jnp.bfloat16)
    produced = jnp.dot(hidden, down_rows, preferred_element_type=jnp.float32).astype(jnp.bfloat16)
    produced = produced.reshape(source_count * local_experts, capacity, model_width)
    returned = exchange(produced, "expert", 3)
    picked = jnp.einsum(
        "sa,sd->ad",
        placing,
        returned.reshape(expert_count * capacity, model_width),
        preferred_element_type=jnp.float32,
    )
    picked = picked.reshape(tok_rows, 2, model_width)
    combined = jnp.sum(gate_values[0][:, :, None] * picked, axis=1)
    layer_out = (mixed + branch_gates[0, 1][None, :] * combined).astype(jnp.bfloat16)
    return layer_out[None]


def solution(mesh):
    placed = (
        P("expert", "tm", None),
        P("expert", "tm", None),
        P("expert", "tm", None),
        P("expert", "tm", None),
        P("expert", "tm"),
        P(),
        P(),
        P("expert", None, None),
        P("expert", None, None),
        P("expert", "tm", None),
        P("expert", "tm", None),
        P("expert", None, "tm"),
        P("expert", "tm", None),
    )
    return jax.shard_map(
        on_device, mesh=mesh, in_specs=placed, out_specs=P("expert", "tm", None), check_vma=False
    )
```

```python
import functools

import jax
import jax.numpy as jnp
from jax import lax
from jax.experimental import pallas as pl
from jax.experimental.pallas import tpu as pltpu
from jax.sharding import PartitionSpec as P

eps = 1e-06
query_block = 1024


def head_attention(query_rows, key_rows, value_rows, offset_row):
    outputs = []
    for first in range(0, query_rows.shape[0], query_block):
        block = query_rows[first:first + query_block]
        scores = jnp.dot(block, key_rows.T, preferred_element_type=jnp.float32) + offset_row[None, :]
        highest = jnp.max(scores, axis=1, keepdims=True)
        unscaled = jnp.exp(scores - highest)
        total = jnp.sum(unscaled, axis=1, keepdims=True)
        weighted = jnp.dot(
            unscaled.astype(jnp.bfloat16), value_rows, preferred_element_type=jnp.float32
        )
        outputs.append((weighted / total).astype(jnp.bfloat16))
    return jnp.concatenate(outputs, axis=0)


def both_ways(n):
    order = []
    for k in range(1, n // 2 + 1):
        order += [k] if 2 * k == n else [k, n - k]
    return order


def exchange_kernel(axis, n, x_ref, y_ref, send_sems, recv_sems, local_sem):
    me = lax.axis_index(axis)
    barrier = pltpu.get_barrier_semaphore()
    for k in range(1, n):
        pl.semaphore_signal(
            barrier, inc=1, device_id={axis: lax.rem(me + k, n)}, device_id_type=pl.DeviceIdType.MESH
        )
    pl.semaphore_wait(barrier, n - 1)
    local = pltpu.make_async_copy(x_ref.at[me], y_ref.at[me], local_sem)
    local.start()
    copies = []
    for k in both_ways(n):
        peer = lax.rem(me + k, n)
        copy = pltpu.make_async_remote_copy(
            src_ref=x_ref.at[peer],
            dst_ref=y_ref.at[me],
            send_sem=send_sems.at[k],
            recv_sem=recv_sems.at[k],
            device_id={axis: peer},
            device_id_type=pl.DeviceIdType.MESH,
        )
        copy.start()
        copies.append(copy)
    local.wait()
    for copy in copies:
        copy.wait_send()
    for k in range(1, n):
        source = lax.rem(me + n - k, n)
        pltpu.make_async_remote_copy(
            src_ref=x_ref.at[source],
            dst_ref=y_ref.at[source],
            send_sem=send_sems.at[k],
            recv_sem=recv_sems.at[k],
            device_id={axis: source},
            device_id_type=pl.DeviceIdType.MESH,
        ).wait_recv()


def exchange(x, axis, collective_id):
    n = x.shape[0]
    return pl.pallas_call(
        functools.partial(exchange_kernel, axis, n),
        out_shape=jax.ShapeDtypeStruct(x.shape, x.dtype),
        in_specs=[pl.BlockSpec(memory_space=pl.ANY)],
        out_specs=pl.BlockSpec(memory_space=pl.ANY),
        scratch_shapes=[
            pltpu.SemaphoreType.DMA((n,)),
            pltpu.SemaphoreType.DMA((n,)),
            pltpu.SemaphoreType.DMA,
        ],
        compiler_params=pltpu.CompilerParams(collective_id=collective_id, has_side_effects=True),
    )(x)


def dispatch_kernel(
    expert_n, tm_n, slots_ref, own_up_ref, own_down_ref, arrived_ref, up_ref, down_ref,
    send_sems, recv_sems, weight_send_sems, weight_recv_sems, sibling_sems, local_sems,
):
    mesh_ids = pl.DeviceIdType.MESH
    half = tm_n // 2
    me_e = lax.axis_index("expert")
    me_t = lax.axis_index("tm")
    parity = me_t % 2
    rank = me_t // 2
    sibling = me_t + 1 - 2 * parity
    owned = (own_up_ref, own_down_ref)
    gathered = (up_ref, down_ref)
    barrier = pltpu.get_barrier_semaphore()
    for k in range(1, expert_n):
        pl.semaphore_signal(barrier, inc=1, device_id={"expert": lax.rem(me_e + k, expert_n)}, device_id_type=mesh_ids)
    for k in range(1, half):
        pl.semaphore_signal(barrier, inc=1, device_id={"tm": 2 * lax.rem(rank + k, half) + parity}, device_id_type=mesh_ids)
    pl.semaphore_signal(barrier, inc=1, device_id={"tm": sibling}, device_id_type=mesh_ids)
    pl.semaphore_wait(barrier, expert_n - 1 + half)
    local_copies = [pltpu.make_async_copy(slots_ref.at[me_e], arrived_ref.at[me_e], local_sems.at[0])]
    for w in range(2):
        local_copies.append(
            pltpu.make_async_copy(owned[w], gathered[w].at[parity, rank], local_sems.at[1 + w])
        )
    for copy in local_copies:
        copy.start()
    copies = []
    for k in range(1, half):
        for w in range(2):
            copy = pltpu.make_async_remote_copy(
                src_ref=owned[w],
                dst_ref=gathered[w].at[parity, rank],
                send_sem=weight_send_sems.at[w, k],
                recv_sem=weight_recv_sems.at[w, k],
                device_id={"tm": 2 * lax.rem(rank + k, half) + parity},
                device_id_type=mesh_ids,
            )
            copy.start()
            copies.append(copy)
    for k in both_ways(expert_n):
        peer = lax.rem(me_e + k, expert_n)
        copy = pltpu.make_async_remote_copy(
            src_ref=slots_ref.at[peer],
            dst_ref=arrived_ref.at[me_e],
            send_sem=send_sems.at[k],
            recv_sem=recv_sems.at[k],
            device_id={"expert": peer},
            device_id_type=mesh_ids,
        )
        copy.start()
        copies.append(copy)
    for copy in local_copies:
        copy.wait()
    forwards = []
    for w in range(2):
        for k in range(1, half):
            source = lax.rem(rank + half - k, half)
            pltpu.make_async_remote_copy(
                src_ref=owned[w],
                dst_ref=gathered[w].at[parity, source],
                send_sem=weight_send_sems.at[w, k],
                recv_sem=weight_recv_sems.at[w, k],
                device_id={"tm": 2 * source + parity},
                device_id_type=mesh_ids,
            ).wait_recv()
        forward = pltpu.make_async_remote_copy(
            src_ref=gathered[w].at[parity],
            dst_ref=gathered[w].at[parity],
            send_sem=sibling_sems.at[0, w],
            recv_sem=sibling_sems.at[1, w],
            device_id={"tm": sibling},
            device_id_type=mesh_ids,
        )
        forward.start()
        forwards.append(forward)
    for copy in copies:
        copy.wait_send()
    for k in range(1, expert_n):
        source = lax.rem(me_e + expert_n - k, expert_n)
        pltpu.make_async_remote_copy(
            src_ref=slots_ref.at[source],
            dst_ref=arrived_ref.at[source],
            send_sem=send_sems.at[k],
            recv_sem=recv_sems.at[k],
            device_id={"expert": source},
            device_id_type=mesh_ids,
        ).wait_recv()
    for w in range(2):
        forwards[w].wait_send()
        pltpu.make_async_remote_copy(
            src_ref=gathered[w].at[1 - parity],
            dst_ref=gathered[w].at[1 - parity],
            send_sem=sibling_sems.at[0, w],
            recv_sem=sibling_sems.at[1, w],
            device_id={"tm": sibling},
            device_id_type=mesh_ids,
        ).wait_recv()


def dispatch(slots, own_up, own_down, tm_n, collective_id):
    expert_n = slots.shape[0]
    gathered_shape = jax.ShapeDtypeStruct((2, tm_n // 2) + own_up.shape, own_up.dtype)
    return pl.pallas_call(
        functools.partial(dispatch_kernel, expert_n, tm_n),
        out_shape=(jax.ShapeDtypeStruct(slots.shape, slots.dtype), gathered_shape, gathered_shape),
        in_specs=[pl.BlockSpec(memory_space=pl.ANY)] * 3,
        out_specs=tuple(pl.BlockSpec(memory_space=pl.ANY) for _ in range(3)),
        scratch_shapes=[
            pltpu.SemaphoreType.DMA((expert_n,)),
            pltpu.SemaphoreType.DMA((expert_n,)),
            pltpu.SemaphoreType.DMA((2, tm_n // 2)),
            pltpu.SemaphoreType.DMA((2, tm_n // 2)),
            pltpu.SemaphoreType.DMA((2, 2)),
            pltpu.SemaphoreType.DMA((3,)),
        ],
        compiler_params=pltpu.CompilerParams(collective_id=collective_id, has_side_effects=True),
    )(slots, own_up, own_down)

def layer_norm(mixed, shift_row, scale_row):
    center = jnp.mean(mixed, axis=-1, keepdims=True)
    deviation = mixed - center
    variance = jnp.mean(deviation * deviation, axis=-1, keepdims=True)
    return deviation * lax.rsqrt(variance + eps) * (1.0 + scale_row) + shift_row


def on_device(
    latents,
    queries,
    keys,
    values,
    inpaint_mask,
    key_bias,
    out_weight,
    modulation,
    branch_gates,
    expert_ids,
    gate_values,
    up_weight,
    down_weight,
):
    tok_rows = latents.shape[1]
    model_width = latents.shape[2]
    head_count = key_bias.shape[0]
    head_width = model_width // head_count
    score_scale = head_width ** (-0.5)
    scaled_queries = queries[0] * jnp.asarray(score_scale, jnp.bfloat16)
    offsets = jnp.where(
        inpaint_mask[0][:, None] == 1, key_bias[None, :], jnp.zeros((), jnp.bfloat16)
    )
    offset_cols = jnp.zeros((tok_rows, head_count, 16), jnp.bfloat16).at[:, :, 0].set(offsets)
    packed = jnp.concatenate(
        [
            scaled_queries.reshape(tok_rows, head_count, head_width),
            keys[0].reshape(tok_rows, head_count, head_width),
            values[0].reshape(tok_rows, head_count, head_width),
            offset_cols,
        ],
        axis=2,
    )
    packed = jnp.transpose(packed, (1, 0, 2))
    gathered = lax.all_to_all(packed, "tm", split_axis=0, concat_axis=0, tiled=True)
    clip_rows = gathered.reshape(-1, 3 * head_width + 16)
    head_out = head_attention(
        clip_rows[:, :head_width],
        clip_rows[:, head_width:2 * head_width],
        clip_rows[:, 2 * head_width:3 * head_width],
        clip_rows[:, 3 * head_width].astype(jnp.float32),
    )
    head_out = head_out.reshape(head_count, tok_rows, head_width)
    attended_heads = lax.all_to_all(head_out, "tm", split_axis=0, concat_axis=0, tiled=True)
    projected = jnp.einsum(
        "hid,hdo->io",
        attended_heads,
        out_weight.reshape(head_count, head_width, model_width),
        preferred_element_type=jnp.float32,
    )
    mixed = latents[0].astype(jnp.float32) + branch_gates[0, 0][None, :] * projected
    normed = layer_norm(mixed, modulation[0, 0][None, :], modulation[0, 1][None, :]).astype(
        jnp.bfloat16
    )
    local_experts = up_weight.shape[0]
    source_count = lax.axis_size("expert")
    expert_count = local_experts * source_count
    capacity = 4 * tok_rows // expert_count
    choice_list = expert_ids[0].reshape(2 * tok_rows)
    hits = (choice_list[:, None] == jnp.arange(expert_count, dtype=jnp.int32)[None, :]).astype(
        jnp.int32
    )
    ranks = jnp.sum((jnp.cumsum(hits, axis=0) - 1) * hits, axis=1)
    target = choice_list * capacity + ranks
    slot_token = (
        jnp.full((capacity * expert_count,), tok_rows, jnp.int32)
        .at[target]
        .set(jnp.arange(2 * tok_rows, dtype=jnp.int32) // 2)
    )
    slots = jnp.take(normed, slot_token, axis=0, mode="fill", fill_value=0)
    slots = slots.reshape(expert_count, capacity, model_width)
    arrived, gathered_up, gathered_down = dispatch(
        slots, jnp.transpose(up_weight[0]), down_weight[0], lax.axis_size("tm"), 2
    )
    up_rows = gathered_up.reshape(-1, model_width)
    down_rows = gathered_down.reshape(-1, model_width)
    grouped = arrived.reshape(source_count * local_experts * capacity, model_width)
    hidden = jax.nn.gelu(
        jnp.einsum("rd,fd->rf", grouped, up_rows, preferred_element_type=jnp.float32),
        approximate=True,
    ).astype(jnp.bfloat16)
    produced = jnp.dot(hidden, down_rows, preferred_element_type=jnp.float32).astype(jnp.bfloat16)
    produced = produced.reshape(source_count * local_experts, capacity, model_width)
    returned = exchange(produced, "expert", 3)
    picked = jnp.take(
        returned.reshape(expert_count * capacity, model_width), target, axis=0
    ).astype(jnp.float32)
    picked = picked.reshape(tok_rows, 2, model_width)
    combined = jnp.sum(gate_values[0][:, :, None] * picked, axis=1)
    layer_out = (mixed + branch_gates[0, 1][None, :] * combined).astype(jnp.bfloat16)
    return layer_out[None]


def solution(mesh):
    placed = (
        P("expert", "tm", None),
        P("expert", "tm", None),
        P("expert", "tm", None),
        P("expert", "tm", None),
        P("expert", "tm"),
        P(),
        P(),
        P("expert", None, None),
        P("expert", None, None),
        P("expert", "tm", None),
        P("expert", "tm", None),
        P("expert", None, "tm"),
        P("expert", "tm", None),
    )
    return jax.shard_map(
        on_device, mesh=mesh, in_specs=placed, out_specs=P("expert", "tm", None), check_vma=False
    )
```

```python
import functools

import jax
import jax.numpy as jnp
from jax import lax
from jax.experimental import pallas as pl
from jax.experimental.pallas import tpu as pltpu
from jax.sharding import PartitionSpec as P

eps = 1e-06
query_block = 1024


def head_attention(query_rows, key_rows, value_rows, offset_row):
    outputs = []
    for first in range(0, query_rows.shape[0], query_block):
        block = query_rows[first:first + query_block]
        scores = jnp.dot(block, key_rows.T, preferred_element_type=jnp.float32) + offset_row[None, :]
        highest = jnp.max(scores, axis=1, keepdims=True)
        unscaled = jnp.exp(scores - highest)
        total = jnp.sum(unscaled, axis=1, keepdims=True)
        weighted = jnp.dot(
            unscaled.astype(jnp.bfloat16), value_rows, preferred_element_type=jnp.float32
        )
        outputs.append((weighted / total).astype(jnp.bfloat16))
    return jnp.concatenate(outputs, axis=0)


def both_ways(n):
    order = []
    for k in range(1, n // 2 + 1):
        order += [k] if 2 * k == n else [k, n - k]
    return order


def exchange_kernel(axis, n, x_ref, y_ref, send_sems, recv_sems, local_sem):
    me = lax.axis_index(axis)
    barrier = pltpu.get_barrier_semaphore()
    for k in range(1, n):
        pl.semaphore_signal(
            barrier, inc=1, device_id={axis: lax.rem(me + k, n)}, device_id_type=pl.DeviceIdType.MESH
        )
    pl.semaphore_wait(barrier, n - 1)
    local = pltpu.make_async_copy(x_ref.at[me], y_ref.at[me], local_sem)
    local.start()
    copies = []
    for k in both_ways(n):
        peer = lax.rem(me + k, n)
        copy = pltpu.make_async_remote_copy(
            src_ref=x_ref.at[peer],
            dst_ref=y_ref.at[me],
            send_sem=send_sems.at[k],
            recv_sem=recv_sems.at[k],
            device_id={axis: peer},
            device_id_type=pl.DeviceIdType.MESH,
        )
        copy.start()
        copies.append(copy)
    local.wait()
    for copy in copies:
        copy.wait_send()
    for k in range(1, n):
        source = lax.rem(me + n - k, n)
        pltpu.make_async_remote_copy(
            src_ref=x_ref.at[source],
            dst_ref=y_ref.at[source],
            send_sem=send_sems.at[k],
            recv_sem=recv_sems.at[k],
            device_id={axis: source},
            device_id_type=pl.DeviceIdType.MESH,
        ).wait_recv()


def exchange(x, axis, collective_id):
    n = x.shape[0]
    return pl.pallas_call(
        functools.partial(exchange_kernel, axis, n),
        out_shape=jax.ShapeDtypeStruct(x.shape, x.dtype),
        in_specs=[pl.BlockSpec(memory_space=pl.ANY)],
        out_specs=pl.BlockSpec(memory_space=pl.ANY),
        scratch_shapes=[
            pltpu.SemaphoreType.DMA((n,)),
            pltpu.SemaphoreType.DMA((n,)),
            pltpu.SemaphoreType.DMA,
        ],
        compiler_params=pltpu.CompilerParams(collective_id=collective_id, has_side_effects=True),
    )(x)


def dispatch_kernel(
    expert_n, tm_n, slots_ref, own_up_ref, own_down_ref, arrived_ref, up_ref, down_ref,
    send_sems, recv_sems, weight_send_sems, weight_recv_sems, sibling_sems, local_sems,
):
    mesh_ids = pl.DeviceIdType.MESH
    half = tm_n // 2
    me_e = lax.axis_index("expert")
    me_t = lax.axis_index("tm")
    parity = me_t % 2
    rank = me_t // 2
    sibling = me_t + 1 - 2 * parity
    owned = (own_up_ref, own_down_ref)
    gathered = (up_ref, down_ref)
    barrier = pltpu.get_barrier_semaphore()
    for k in range(1, expert_n):
        pl.semaphore_signal(barrier, inc=1, device_id={"expert": lax.rem(me_e + k, expert_n)}, device_id_type=mesh_ids)
    for k in range(1, half):
        pl.semaphore_signal(barrier, inc=1, device_id={"tm": 2 * lax.rem(rank + k, half) + parity}, device_id_type=mesh_ids)
    pl.semaphore_signal(barrier, inc=1, device_id={"tm": sibling}, device_id_type=mesh_ids)
    pl.semaphore_wait(barrier, expert_n - 1 + half)
    local_copies = [pltpu.make_async_copy(slots_ref.at[me_e], arrived_ref.at[me_e], local_sems.at[0])]
    for w in range(2):
        local_copies.append(
            pltpu.make_async_copy(owned[w], gathered[w].at[parity, rank], local_sems.at[1 + w])
        )
    for copy in local_copies:
        copy.start()
    copies = []
    for k in range(1, half):
        for w in range(2):
            copy = pltpu.make_async_remote_copy(
                src_ref=owned[w],
                dst_ref=gathered[w].at[parity, rank],
                send_sem=weight_send_sems.at[w, k],
                recv_sem=weight_recv_sems.at[w, k],
                device_id={"tm": 2 * lax.rem(rank + k, half) + parity},
                device_id_type=mesh_ids,
            )
            copy.start()
            copies.append(copy)
    for k in both_ways(expert_n):
        peer = lax.rem(me_e + k, expert_n)
        copy = pltpu.make_async_remote_copy(
            src_ref=slots_ref.at[peer],
            dst_ref=arrived_ref.at[me_e],
            send_sem=send_sems.at[k],
            recv_sem=recv_sems.at[k],
            device_id={"expert": peer},
            device_id_type=mesh_ids,
        )
        copy.start()
        copies.append(copy)
    for copy in local_copies:
        copy.wait()
    forwards = []
    for w in range(2):
        for k in range(1, half):
            source = lax.rem(rank + half - k, half)
            pltpu.make_async_remote_copy(
                src_ref=owned[w],
                dst_ref=gathered[w].at[parity, source],
                send_sem=weight_send_sems.at[w, k],
                recv_sem=weight_recv_sems.at[w, k],
                device_id={"tm": 2 * source + parity},
                device_id_type=mesh_ids,
            ).wait_recv()
        forward = pltpu.make_async_remote_copy(
            src_ref=gathered[w].at[parity],
            dst_ref=gathered[w].at[parity],
            send_sem=sibling_sems.at[0, w],
            recv_sem=sibling_sems.at[1, w],
            device_id={"tm": sibling},
            device_id_type=mesh_ids,
        )
        forward.start()
        forwards.append(forward)
    for copy in copies:
        copy.wait_send()
    for k in range(1, expert_n):
        source = lax.rem(me_e + expert_n - k, expert_n)
        pltpu.make_async_remote_copy(
            src_ref=slots_ref.at[source],
            dst_ref=arrived_ref.at[source],
            send_sem=send_sems.at[k],
            recv_sem=recv_sems.at[k],
            device_id={"expert": source},
            device_id_type=mesh_ids,
        ).wait_recv()
    for w in range(2):
        forwards[w].wait_send()
        pltpu.make_async_remote_copy(
            src_ref=gathered[w].at[1 - parity],
            dst_ref=gathered[w].at[1 - parity],
            send_sem=sibling_sems.at[0, w],
            recv_sem=sibling_sems.at[1, w],
            device_id={"tm": sibling},
            device_id_type=mesh_ids,
        ).wait_recv()


def dispatch(slots, own_up, own_down, tm_n, collective_id):
    expert_n = slots.shape[0]
    gathered_shape = jax.ShapeDtypeStruct((2, tm_n // 2) + own_up.shape, own_up.dtype)
    return pl.pallas_call(
        functools.partial(dispatch_kernel, expert_n, tm_n),
        out_shape=(jax.ShapeDtypeStruct(slots.shape, slots.dtype), gathered_shape, gathered_shape),
        in_specs=[pl.BlockSpec(memory_space=pl.ANY)] * 3,
        out_specs=tuple(pl.BlockSpec(memory_space=pl.ANY) for _ in range(3)),
        scratch_shapes=[
            pltpu.SemaphoreType.DMA((expert_n,)),
            pltpu.SemaphoreType.DMA((expert_n,)),
            pltpu.SemaphoreType.DMA((2, tm_n // 2)),
            pltpu.SemaphoreType.DMA((2, tm_n // 2)),
            pltpu.SemaphoreType.DMA((2, 2)),
            pltpu.SemaphoreType.DMA((3,)),
        ],
        compiler_params=pltpu.CompilerParams(collective_id=collective_id, has_side_effects=True),
    )(slots, own_up, own_down)

def layer_norm(mixed, shift_row, scale_row):
    center = jnp.mean(mixed, axis=-1, keepdims=True)
    deviation = mixed - center
    variance = jnp.mean(deviation * deviation, axis=-1, keepdims=True)
    return deviation * lax.rsqrt(variance + eps) * (1.0 + scale_row) + shift_row


def on_device(
    latents,
    queries,
    keys,
    values,
    inpaint_mask,
    key_bias,
    out_weight,
    modulation,
    branch_gates,
    expert_ids,
    gate_values,
    up_weight,
    down_weight,
):
    tok_rows = latents.shape[1]
    model_width = latents.shape[2]
    head_count = key_bias.shape[0]
    head_width = model_width // head_count
    score_scale = head_width ** (-0.5)
    offsets = jnp.where(
        inpaint_mask[0][:, None] == 1, key_bias[None, :], jnp.zeros((), jnp.bfloat16)
    )
    offset_cols = jnp.zeros((tok_rows, head_count, 16), jnp.bfloat16).at[:, :, 0].set(offsets)
    packed = jnp.concatenate(
        [
            queries[0].reshape(tok_rows, head_count, head_width),
            keys[0].reshape(tok_rows, head_count, head_width),
            values[0].reshape(tok_rows, head_count, head_width),
            offset_cols,
        ],
        axis=2,
    )
    packed = jnp.transpose(packed, (1, 0, 2))
    gathered = lax.all_to_all(packed, "tm", split_axis=0, concat_axis=0, tiled=True)
    clip_rows = gathered.reshape(-1, 3 * head_width + 16)
    head_out = head_attention(
        clip_rows[:, :head_width] * jnp.asarray(score_scale, jnp.bfloat16),
        clip_rows[:, head_width:2 * head_width],
        clip_rows[:, 2 * head_width:3 * head_width],
        clip_rows[:, 3 * head_width].astype(jnp.float32),
    )
    head_out = head_out.reshape(head_count, tok_rows, head_width)
    attended_heads = lax.all_to_all(head_out, "tm", split_axis=0, concat_axis=0, tiled=True)
    projected = jnp.einsum(
        "hid,hdo->io",
        attended_heads,
        out_weight.reshape(head_count, head_width, model_width),
        preferred_element_type=jnp.float32,
    )
    mixed = latents[0].astype(jnp.float32) + branch_gates[0, 0][None, :] * projected
    normed = layer_norm(mixed, modulation[0, 0][None, :], modulation[0, 1][None, :]).astype(
        jnp.bfloat16
    )
    local_experts = up_weight.shape[0]
    source_count = lax.axis_size("expert")
    expert_count = local_experts * source_count
    capacity = 4 * tok_rows // expert_count
    choice_list = expert_ids[0].reshape(2 * tok_rows)
    hits = (choice_list[:, None] == jnp.arange(expert_count, dtype=jnp.int32)[None, :]).astype(
        jnp.int32
    )
    ranks = jnp.sum((jnp.cumsum(hits, axis=0) - 1) * hits, axis=1)
    target = choice_list * capacity + ranks
    placing = (
        jnp.arange(capacity * expert_count, dtype=jnp.int32)[:, None] == target[None, :]
    ).astype(jnp.bfloat16)
    token_placing = placing.reshape(capacity * expert_count, tok_rows, 2).sum(axis=2)
    slots = jnp.dot(token_placing, normed, preferred_element_type=jnp.float32).astype(jnp.bfloat16)
    slots = slots.reshape(expert_count, capacity, model_width)
    arrived, gathered_up, gathered_down = dispatch(
        slots, jnp.transpose(up_weight[0]), down_weight[0], lax.axis_size("tm"), 2
    )
    up_rows = gathered_up.reshape(-1, model_width)
    down_rows = gathered_down.reshape(-1, model_width)
    grouped = arrived.reshape(source_count * local_experts * capacity, model_width)
    hidden = jax.nn.gelu(
        jnp.einsum("rd,fd->rf", grouped, up_rows, preferred_element_type=jnp.float32),
        approximate=True,
    ).astype(jnp.bfloat16)
    produced = jnp.dot(hidden, down_rows, preferred_element_type=jnp.float32).astype(jnp.bfloat16)
    produced = produced.reshape(source_count * local_experts, capacity, model_width)
    returned = exchange(produced, "expert", 3)
    picked = jnp.einsum(
        "sa,sd->ad",
        placing,
        returned.reshape(expert_count * capacity, model_width),
        preferred_element_type=jnp.float32,
    )
    picked = picked.reshape(tok_rows, 2, model_width)
    combined = jnp.sum(gate_values[0][:, :, None] * picked, axis=1)
    layer_out = (mixed + branch_gates[0, 1][None, :] * combined).astype(jnp.bfloat16)
    return layer_out[None]


def solution(mesh):
    placed = (
        P("expert", "tm", None),
        P("expert", "tm", None),
        P("expert", "tm", None),
        P("expert", "tm", None),
        P("expert", "tm"),
        P(),
        P(),
        P("expert", None, None),
        P("expert", None, None),
        P("expert", "tm", None),
        P("expert", "tm", None),
        P("expert", None, "tm"),
        P("expert", "tm", None),
    )
    return jax.shard_map(
        on_device, mesh=mesh, in_specs=placed, out_specs=P("expert", "tm", None), check_vma=False
    )
```
